32 devices in a mesh: ctx: 8 (over z, x), tp: 4 (over y, core).
Axes of the slice: x: 2, y: 2, z: 4, core: 2. Of those that a mesh axis runs over, the one named last changes fastest.
Arguments:
- qkv: bfloat16 [3, 1024, 8192], P(None, 'ctx', 'tp'), may hold values from -6 to 6
- cotangent: bfloat16 [1024, 8192], P('ctx', 'tp'), may hold values from -6 to 6
- doc_ids: int32 [1024], P('ctx'), may hold values from 0 to 3, never falling along the last dimension, each value on 1 to 512 neighbouring positions
- short_filter: float32 [3, 8192, 7], P(None, 'tp'), may hold values from -2 to 2
- long_filter: float32 [512, 128], P('tp'), may hold values from -0.5 to 0.5
Outputs:
- layer_output: bfloat16 [1024, 8192], P('ctx', 'tp')
- qkv_grad: bfloat16 [3, 1024, 8192], P(None, 'ctx', 'tp')
- long_filter_grad: float32 [512, 128], P(('tp', 'ctx'))
- short_filter_grad: float32 [3, 8192, 7], P(None, ('tp', 'ctx'))
The draws below stay inside these ranges and needn't reach their ends.
Inputs may be any that keep to these rules, and one draw needn't show every extreme that they name: `doc_ids`: document ids never decrease along the tokens; every id in the range is used; a document holds at most 512 tokens and one holds exactly that many.
All inputs are finite; a program needn't handle non-finite values.
Results may differ from the reference program's by a relative error of at most 0.005.
Values may be sent and summed in bfloat16 or wider, within the bound.
No kernel may reach another device: no remote copies, remote signals or barrier semaphores. Data moves between devices by JAX's collectives and lax.ppermute only.
A program may use at most 128 MiB of HBM per device.

```python
import math
import jax
import jax.numpy as jnp
import numpy as np
from jax import lax

CH = 8192
SHORT = 7
LONG = 128
TOK_DEV = 128
TOKENS = 1024
GROUPS = 512
N_CTX = 8


def strengthened(array, rng, source, target, shards_of, factor):
    owner, partner = [(jnp.arange(array.shape[dim]) // (array.shape[dim] // shards_of)).reshape([-1 if axis == dim else 1 for axis in range(array.ndim)]) for dim in (source, target)]
    chosen = jax.random.permutation(rng, shards_of)[partner]
    strong = (owner == chosen) | (owner == (partner + shards_of // 2) % shards_of)
    return jnp.where(strong, factor * array, array)


def block_scale(key, dims, shards, smallest, high):
    def one(dim, parts):
        draws = jax.random.uniform(jax.random.fold_in(jax.random.fold_in(key, 6), dim), (parts,), jnp.float32, smallest / len(shards), high / len(shards))
        return jnp.repeat(jnp.exp(draws), dims[dim] // parts).reshape((-1,) + (1,) * (len(dims) - dim - 1))

    factor_of = one(*shards[0])
    for cut in shards[1:]:
        factor_of = factor_of * one(*cut)
    return factor_of


def split_up(number_of, total, reach, skew):
    loads = [(1 << 20) // math.isqrt(grade ** skew) + 1 for grade in range(2, number_of + 1)]
    rest, counts = total - reach - (number_of - 1), [1] * (number_of - 1)
    while rest > 0:
        candidates = [i for i in range(number_of - 1) if counts[i] < reach]
        whole, remaining = sum([loads[i] for i in candidates]), rest
        for i in candidates:
            extra = min(reach - counts[i], max(1, remaining * loads[i] // whole), rest)
            counts[i] = counts[i] + extra
            rest = rest - extra
    return np.array([reach] + counts)


def uneven(stream_key, number_of, total, reach, lean):
    if number_of == 2:
        one = jax.random.randint(stream_key, (), max(1, total - reach), min(reach, total - 1) + 1)
        return jnp.stack([one, total - one])
    lengths = jnp.asarray(split_up(number_of, total, reach, lean), jnp.int32)
    couples = (number_of - 1) // 2
    source_of, sink = lengths[1:1 + 2 * couples:2], lengths[2:2 + 2 * couples:2]
    slack = jnp.minimum(source_of - 1, reach - sink)
    moved = jax.random.randint(jax.random.fold_in(stream_key, 1), (couples,), 0, 1 << 20) % (slack + 1)
    lengths = lengths.at[1:1 + 2 * couples:2].set(source_of - moved).at[2:2 + 2 * couples:2].set(sink + moved)
    return lengths[jax.random.permutation(jax.random.fold_in(stream_key, 2), number_of)]


def noise(stream_key, shape, spread, bound, shards=(), kind=jnp.bfloat16):
    result = jax.random.normal(stream_key, shape, jnp.float32) * spread
    if len(shards) > 0:
        result = block_scale(stream_key, shape, shards, -0.22, 0.18) * result
    return jnp.clip(result, min=-bound, max=bound).astype(kind)


def bell_draw_with(stream_key, shape, width, bound, cuts, heavy, kind=jnp.bfloat16):
    values = width * jax.random.normal(stream_key, shape, jnp.float32)
    if cuts:
        values = values * block_scale(stream_key, shape, cuts, -0.22, 0.18)
    return jnp.clip(strengthened(values, jax.random.fold_in(stream_key, 3), *heavy), -bound, bound).astype(kind)


def setup_inputs(seed: int = 0) -> dict:
    splits = jax.random.split(jax.random.key(seed), 6)
    qkv = noise(splits[0], (3, TOKENS, CH), 1.0, 6.0, ((1, 8), (2, 4)))
    cotangent = bell_draw_with(splits[1], (TOKENS, CH), 1.0, 6.0, ((0, 8), (1, 4)), (0, 1, 8, 2.0))
    doc_ids = jnp.searchsorted(jnp.cumsum(uneven(splits[2], N_CTX // 2, TOKENS, 4 * TOK_DEV, 2)), jnp.arange(TOKENS), side="right").astype(jnp.int32)
    short_filter = noise(splits[3], (3, CH, SHORT), SHORT ** -0.5, 2.0, ((1, 4),), jnp.float32)
    long_filter = noise(splits[4], (GROUPS, LONG), LONG ** -0.5, 0.5, ((0, 4),), jnp.float32)
    return dict(qkv=qkv, cotangent=cotangent, doc_ids=doc_ids, short_filter=short_filter, long_filter=long_filter)


def delayed(values, offset, filler):
    if offset == 0:
        return values
    padding = jnp.full((offset,) + values.shape[1:], filler, values.dtype)
    return jnp.concatenate([padding, values[:-offset]], 0)

def advanced(values, offset, filler):
    if offset == 0:
        return values
    padding = jnp.full((offset,) + values.shape[1:], filler, values.dtype)
    return jnp.concatenate([values[offset:], padding], 0)

def group_pass(raw_group, cot_group, doc_group, short_taps, long_taps):
    short_count = short_taps.shape[2]
    long_count = long_taps.shape[0]
    features = jnp.zeros_like(raw_group)
    for tap_index in range(short_count):
        same_doc = (delayed(doc_group, tap_index, -1) == doc_group).astype(jnp.float32)[:, None, None]
        features = features + short_taps[:, :, tap_index] * delayed(raw_group, tap_index, 0.0) * same_doc
    kv_product = features[:, 1] * features[:, 2]
    long_conv = jnp.zeros_like(kv_product)
    for tap_index in range(long_count):
        same_doc = (delayed(doc_group, tap_index, -1) == doc_group).astype(jnp.float32)[:, None]
        long_conv = long_conv + long_taps[tap_index] * delayed(kv_product, tap_index, 0.0) * same_doc
    output = features[:, 0] * long_conv
    grad_q = cot_group * long_conv
    grad_conv = cot_group * features[:, 0]
    grad_mix = jnp.zeros_like(grad_conv)
    for tap_index in range(long_count):
        same_doc = (advanced(doc_group, tap_index, -1) == doc_group).astype(jnp.float32)[:, None]
        grad_mix = grad_mix + long_taps[tap_index] * advanced(grad_conv, tap_index, 0.0) * same_doc
    grad_feats = jnp.stack([grad_q, grad_mix * features[:, 2], grad_mix * features[:, 1]], 1)
    grad_raw = jnp.zeros_like(grad_feats)
    for tap_index in range(short_count):
        same_doc = (advanced(doc_group, tap_index, -1) == doc_group).astype(jnp.float32)[:, None, None]
        grad_raw = grad_raw + short_taps[:, :, tap_index] * advanced(grad_feats, tap_index, 0.0) * same_doc
    long_terms = []
    for tap_index in range(long_count):
        same_doc = (delayed(doc_group, tap_index, -1) == doc_group).astype(jnp.float32)[:, None]
        long_terms.append(jnp.sum(grad_conv * delayed(kv_product, tap_index, 0.0) * same_doc))
    short_terms = []
    for tap_index in range(short_count):
        same_doc = (delayed(doc_group, tap_index, -1) == doc_group).astype(jnp.float32)[:, None, None]
        short_terms.append(lax.optimization_barrier(jnp.sum(grad_feats * delayed(raw_group, tap_index, 0.0) * same_doc, axis=0)))
    return (output.astype(jnp.bfloat16), grad_raw.astype(jnp.bfloat16), jnp.stack(long_terms, 0), jnp.stack(short_terms, -1))

def reference(qkv, cotangent, doc_ids, short_filter, long_filter):
    group_count = long_filter.shape[0]
    group_size = qkv.shape[2] // group_count

    def one_group(group_index):
        first_chan = group_index * group_size
        raw_group = lax.dynamic_slice_in_dim(qkv, first_chan, group_size, 2).astype(jnp.float32).transpose(1, 0, 2)
        cot_group = lax.dynamic_slice_in_dim(cotangent, first_chan, group_size, 1).astype(jnp.float32)
        short_taps = lax.dynamic_slice_in_dim(short_filter, first_chan, group_size, 1)
        long_taps = lax.dynamic_slice_in_dim(long_filter, group_index, 1, 0)[0]
        return group_pass(raw_group, cot_group, doc_ids, short_taps, long_taps)
    outputs, grad_raw, long_grads, short_grads = lax.map(one_group, jnp.arange(group_count, dtype=jnp.int32))
    grad_scale = 1.0 / math.sqrt(TOKENS)
    layer_output = outputs.transpose(1, 0, 2).reshape(TOKENS, -1)
    qkv_grad = grad_raw.transpose(2, 1, 0, 3).reshape(3, TOKENS, -1)
    short_total = short_grads.transpose(1, 0, 2, 3).reshape(3, -1, short_filter.shape[2])
    return (layer_output, qkv_grad, long_grads * grad_scale, short_total * grad_scale)
```

```python
import functools
import math

import jax
import jax.numpy as jnp
from jax import lax
from jax.experimental import pallas as pl
from jax.experimental.pallas import tpu as pltpu
from jax.sharding import PartitionSpec as P

F32 = jnp.float32
BF16 = jnp.bfloat16
EDGE = 8
TILE = 256


def passed_along(block, distance):
    devices = range(lax.axis_size("ctx"))
    route = [(i - distance, i) for i in devices if i - distance in devices]
    return lax.ppermute(block, "ctx", route)


def iota2(shape, dim):
    return lax.broadcasted_iota(jnp.int32, shape, dim)


def dot(a, b):
    return jnp.dot(a, b, preferred_element_type=F32)


def feature_kernel(ids_ref, sf_ref, x_ref, cot_ref, edge_ref, ids_edge_ref,
                   feat_ref, kv_ref, g_ref, shift, shift_edge):
    rows = x_ref.shape[1]
    taps = sf_ref.shape[1]

    @pl.when(pl.program_id(0) == 0)
    def _():
        id_row = jnp.broadcast_to(ids_ref[...], (rows, rows)).astype(F32)
        id_col = id_row.T
        lag = iota2((rows, rows), 0) - iota2((rows, rows), 1)
        same = id_row == id_col
        before = jnp.broadcast_to(ids_edge_ref[0, 0:1, 0:rows].astype(F32), (EDGE, rows))
        before = pltpu.roll(before, EDGE, 1)
        lag_edge = iota2((EDGE, rows), 0) + EDGE - iota2((EDGE, rows), 1)
        same_edge = before == id_col[0:EDGE]
        for t in range(1, taps):
            shift[(t - 1) * rows : t * rows] = jnp.where((lag == t) & same, 1.0, 0.0).astype(BF16)
            shift_edge[(t - 1) * EDGE : t * EDGE] = jnp.where((lag_edge == t) & same_edge, 1.0, 0.0)

    feats = []
    for i in range(3):
        x = x_ref[i]
        w = sf_ref[i]
        moved = dot(shift[...], x)
        acc = w[0:1] * x.astype(F32)
        for t in range(1, taps):
            acc = acc + w[t : t + 1] * moved[(t - 1) * rows : t * rows]
        edge = jnp.concatenate([edge_ref[i].astype(F32), jnp.zeros((rows - EDGE, x.shape[1]), F32)], 0)
        moved_edge = dot(shift_edge[...].astype(BF16), edge.astype(BF16))
        fix = w[1:2] * moved_edge[0:EDGE]
        for t in range(2, taps):
            fix = fix + w[t : t + 1] * moved_edge[(t - 1) * EDGE : t * EDGE]
        acc = jnp.concatenate([acc[0:EDGE] + fix, acc[EDGE:]], 0)
        feat_ref[i] = acc
        feats.append(acc)
    kv_ref[...] = (feats[1] * feats[2]).astype(BF16)
    g = cot_ref[...].astype(F32) * feats[0]
    id_wide = jnp.concatenate([ids_ref[...].astype(F32)] * (g.shape[1] // rows), 1)
    last = iota2(g.shape, 0) == rows - 1
    g_ref[...] = jnp.where(last, jnp.broadcast_to(id_wide, g.shape), g).astype(BF16)


def mixer_kernel(ids_ref, sf_ref, lf_ref, lfr_ref, x_ref, cot_ref, edge_ref, ids_edge_ref, feat_ref,
                 kvp_ref, gn_ref, out_ref, qg_ref, tail_ref, part_ref, long_ref, short_ref,
                 shift, mask_y, mask_g, mask_a, w_kv, w_g, g_rev, y_ref, gm_ref, dh_ref):
    rows = x_ref.shape[1]
    taps = sf_ref.shape[1]
    lanes = x_ref.shape[2]
    groups = lf_ref.shape[0]
    width = lanes // groups
    lag = iota2((rows, rows), 0) - iota2((rows, rows), 1)
    flip = jnp.where(iota2((rows, rows), 0) + iota2((rows, rows), 1) == rows - 1, 1.0, 0.0)
    mirror = flip.astype(BF16)

    @pl.when(pl.program_id(0) == 0)
    def _():
        id_row = jnp.broadcast_to(ids_ref[...], (rows, rows)).astype(F32)
        id_col = id_row.T
        prev_row = jnp.broadcast_to(ids_edge_ref[0, 0:1, 0:rows].astype(F32), (rows, rows))
        prev_col = prev_row.T
        next_row = jnp.broadcast_to(gn_ref[rows - 1 : rows, 0:rows].astype(F32), (rows, rows))
        same = id_row == id_col
        own = jnp.where((lag >= 0) & same, 1.0, 0.0)
        prev = jnp.where((lag < 0) & (prev_row == id_col), 1.0, 0.0)
        mask_y[:, 0:rows] = own.astype(BF16)
        mask_y[:, rows:] = prev.astype(BF16)
        mask_a[...] = dot(mirror, mask_y[...])
        mask_g[:, 0:rows] = jnp.where((lag <= 0) & same, 1.0, 0.0).astype(BF16)
        mask_g[:, rows:] = jnp.where((lag > 0) & (next_row == id_col), 1.0, 0.0).astype(BF16)
        for t in range(1, taps):
            shift[(t - 1) * rows : t * rows] = jnp.where((lag == -t) & same, 1.0, 0.0).astype(BF16)
        base = (taps - 1) * rows
        lag_edge = iota2((EDGE, rows), 1) + EDGE - iota2((EDGE, rows), 0)
        same_edge = prev_col[rows - EDGE :] == id_row[0:EDGE]
        pieces = [jnp.where((lag_edge == t) & same_edge, 1.0, 0.0) for t in range(1, taps)]
        shift[base : base + (taps - 1) * EDGE] = jnp.concatenate(pieces, 0).astype(BF16)

    cot = cot_ref[...].astype(F32)
    g32 = cot * feat_ref[0]
    w_kv[0:rows] = (feat_ref[1] * feat_ref[2]).astype(BF16)
    w_kv[rows:] = kvp_ref[...]
    w_g[0:rows] = g32.astype(BF16)
    w_g[rows:] = gn_ref[...]
    g_rev[...] = dot(mirror, w_g[0:rows]).astype(BF16)

    half = rows
    for part in range(lanes // half):
        cols = slice(part * half, (part + 1) * half)
        per = half // width

        def one_group(j, carry, part=part, cols=cols, per=per):
            g = part * per + j
            mine = iota2((rows, half), 1) // width == j
            fwd = jnp.broadcast_to(lfr_ref[pl.ds(g, 1), :], (rows, rows))
            fwd = pltpu.roll(fwd, 0, 1, stride=1, stride_axis=0).astype(BF16)
            t_y = jnp.concatenate([fwd, fwd], 1) * mask_y[...]
            res = dot(t_y, w_kv[:, cols])
            y_ref[:, cols] = jnp.where(mine, res, y_ref[:, cols])
            bwd = jnp.broadcast_to(lf_ref[pl.ds(g, 1), :], (rows, rows))
            bwd = pltpu.roll(bwd, 0, 1, stride=1, stride_axis=0).astype(BF16)
            t_g = jnp.concatenate([bwd, bwd], 1) * mask_g[...]
            res = dot(t_g, w_g[:, cols])
            gm_ref[:, cols] = jnp.where(mine, res, gm_ref[:, cols])
            g_sel = jnp.where(mine, g_rev[:, cols], jnp.zeros((rows, half), BF16))
            cross = lax.dot_general(
                g_sel, w_kv[:, cols], (((1,), (1,)), ((), ())), preferred_element_type=F32
            ) * mask_a[...]
            folded = cross[:, 0:rows] + cross[:, rows:]
            folded = pltpu.roll(folded, 0, 1, stride=1, stride_axis=0)
            dh_ref[pl.ds(g, 1), :] = jnp.sum(folded, 0, keepdims=True)
            return carry

        lax.fori_loop(0, per, one_group, 0, unroll=2)

    long_ref[...] = jnp.dot(dh_ref[...], flip, preferred_element_type=F32, precision=lax.Precision.HIGHEST)

    y = y_ref[...]
    gm = gm_ref[...]
    out_ref[...] = (feat_ref[0] * y).astype(BF16)
    for i in range(3):
        gf = cot * y if i == 0 else gm * feat_ref[3 - i]
        w = sf_ref[i]
        x = x_ref[i].astype(F32)
        xe = edge_ref[i].astype(F32)
        moved = dot(shift[...], gf.astype(BF16))
        base = (taps - 1) * rows
        acc = w[0:1] * gf
        short_ref[i, 0:1] = jnp.sum(x * gf, 0, keepdims=True)
        sent = jnp.zeros((EDGE, lanes), F32)
        for t in range(1, taps):
            piece = moved[(t - 1) * rows : t * rows]
            piece_edge = moved[base + (t - 1) * EDGE : base + t * EDGE]
            acc = acc + w[t : t + 1] * piece
            sent = sent + w[t : t + 1] * piece_edge
            short_ref[i, t : t + 1] = (
                jnp.sum(x * piece, 0, keepdims=True) + jnp.sum(xe * piece_edge, 0, keepdims=True)
            )
        short_ref[i, taps:] = jnp.zeros((short_ref.shape[1] - taps, lanes), F32)
        qg_ref[i] = acc.astype(BF16)
        tail_ref[i] = acc[rows - EDGE :]
        part_ref[i] = sent.astype(BF16)


def shards(qkv, cotangent, doc_ids, short_filter, long_filter):
    _, rows, chans = qkv.shape
    groups, long_taps = long_filter.shape
    taps = short_filter.shape[2]
    devices = lax.axis_size("ctx")
    grad_scale = 1.0 / math.sqrt(rows * devices)
    tile_groups = TILE * groups // chans
    padded_taps = 8
    params = pltpu.CompilerParams(vmem_limit_bytes=48 << 20, dimension_semantics=("arbitrary",))

    ids = doc_ids.reshape(1, rows)
    sf = jnp.transpose(short_filter, (0, 2, 1))
    lf_rev = jnp.roll(jnp.flip(long_filter, 1), 1, 1)

    edge = qkv[:, rows - EDGE :, :]
    edge = edge.at[0, 0, :rows].set(doc_ids.astype(BF16))
    edge = passed_along(edge, 1)

    fixed = lambda shape: pl.BlockSpec(shape, lambda c: (0,) * len(shape))
    wide3 = lambda n: pl.BlockSpec((3, n, TILE), lambda c: (0, 0, c))
    wide2 = lambda n: pl.BlockSpec((n, TILE), lambda c: (0, c))
    feats, kv, grad = pl.pallas_call(
        feature_kernel,
        grid=(chans // TILE,),
        in_specs=[fixed((1, rows)), wide3(taps), wide3(rows), wide2(rows), wide3(EDGE), fixed((3, EDGE, TILE))],
        out_specs=[wide3(rows), wide2(rows), wide2(rows)],
        out_shape=[
            jax.ShapeDtypeStruct((3, rows, chans), F32),
            jax.ShapeDtypeStruct((rows, chans), BF16),
            jax.ShapeDtypeStruct((rows, chans), BF16),
        ],
        scratch_shapes=[
            pltpu.VMEM(((taps - 1) * rows, rows), BF16),
            pltpu.VMEM(((taps - 1) * EDGE, rows), F32),
        ],
        compiler_params=params,
        name="features",
    )(ids, sf, qkv, cotangent, edge, edge)

    kv_prev = passed_along(kv, 1)
    grad_next = passed_along(grad, -1)

    out, qg, tail, part, long_part, short_part = pl.pallas_call(
        mixer_kernel,
        grid=(chans // TILE,),
        in_specs=[
            fixed((1, rows)), wide3(taps),
            pl.BlockSpec((tile_groups, long_taps), lambda c: (c, 0)),
            pl.BlockSpec((tile_groups, long_taps), lambda c: (c, 0)),
            wide3(rows), wide2(rows), wide3(EDGE), fixed((3, EDGE, TILE)), wide3(rows),
            wide2(rows), wide2(rows),
        ],
        out_specs=[
            wide2(rows), wide3(rows), wide3(EDGE), wide3(EDGE),
            pl.BlockSpec((tile_groups, long_taps), lambda c: (c, 0)),
            wide3(padded_taps),
        ],
        out_shape=[
            jax.ShapeDtypeStruct((rows, chans), BF16),
            jax.ShapeDtypeStruct((3, rows, chans), BF16),
            jax.ShapeDtypeStruct((3, EDGE, chans), F32),
            jax.ShapeDtypeStruct((3, EDGE, chans), BF16),
            jax.ShapeDtypeStruct((groups, long_taps), F32),
            jax.ShapeDtypeStruct((3, padded_taps, chans), F32),
        ],
        scratch_shapes=[
            pltpu.VMEM(((taps - 1) * (rows + EDGE), rows), BF16),
            pltpu.VMEM((rows, 2 * rows), BF16),
            pltpu.VMEM((rows, 2 * rows), BF16),
            pltpu.VMEM((rows, 2 * rows), F32),
            pltpu.VMEM((2 * rows, TILE), BF16),
            pltpu.VMEM((2 * rows, TILE), BF16),
            pltpu.VMEM((rows, TILE), BF16),
            pltpu.VMEM((rows, TILE), F32),
            pltpu.VMEM((rows, TILE), F32),
            pltpu.VMEM((tile_groups, long_taps), F32),
        ],
        compiler_params=params,
        name="mixer",
    )(ids, sf, long_filter, lf_rev, qkv, cotangent, edge, edge, feats, kv_prev, grad_next)

    part = passed_along(part, -1)
    qg = lax.dynamic_update_slice(qg, (tail + part.astype(F32)).astype(BF16), (0, rows - EDGE, 0))

    per = chans // devices
    packed = jnp.concatenate(
        [
            short_part.reshape(3 * padded_taps, devices, per).transpose(1, 0, 2),
            long_part.reshape(devices, -1, per),
        ],
        1,
    )
    packed = lax.all_to_all(packed, "ctx", 0, 0)
    total = jnp.sum(packed, 0) * grad_scale
    short_grad = total[: 3 * padded_taps].reshape(3, padded_taps, per)[:, :taps].transpose(0, 2, 1)
    long_grad = total[3 * padded_taps :].reshape(groups // devices, long_taps)
    return (out, qg, long_grad, short_grad)


def solution(mesh):
    in_specs = (P(None, "ctx", "tp"), P("ctx", "tp"), P("ctx"), P(None, "tp", None), P("tp", None))
    out_specs = (
        P("ctx", "tp"),
        P(None, "ctx", "tp"),
        P(("tp", "ctx"), None),
        P(None, ("tp", "ctx"), None),
    )
    return jax.shard_map(shards, mesh=mesh, in_specs=in_specs, out_specs=out_specs, check_vma=False)
```

```python
import functools
import math

import jax
import jax.numpy as jnp
from jax import lax
from jax.experimental import pallas as pl
from jax.experimental.pallas import tpu as pltpu
from jax.sharding import PartitionSpec as P

F32 = jnp.float32
BF16 = jnp.bfloat16
EDGE = 8
TILE = 512


def passed_along(block, distance):
    devices = range(lax.axis_size("ctx"))
    route = [(i - distance, i) for i in devices if i - distance in devices]
    return lax.ppermute(block, "ctx", route)


def iota2(shape, dim):
    return lax.broadcasted_iota(jnp.int32, shape, dim)


def dot(a, b):
    return jnp.dot(a, b, preferred_element_type=F32)


def feature_kernel(ids_ref, sf_ref, x_ref, cot_ref, edge_ref, ids_edge_ref,
                   feat_ref, kv_ref, g_ref, shift, shift_edge):
    rows = x_ref.shape[1]
    taps = sf_ref.shape[1]

    @pl.when(pl.program_id(0) == 0)
    def _():
        id_row = jnp.broadcast_to(ids_ref[...], (rows, rows)).astype(F32)
        id_col = id_row.T
        lag = iota2((rows, rows), 0) - iota2((rows, rows), 1)
        same = id_row == id_col
        before = jnp.broadcast_to(ids_edge_ref[0, 0:1, 0:rows].astype(F32), (EDGE, rows))
        before = pltpu.roll(before, EDGE, 1)
        lag_edge = iota2((EDGE, rows), 0) + EDGE - iota2((EDGE, rows), 1)
        same_edge = before == id_col[0:EDGE]
        for t in range(1, taps):
            shift[(t - 1) * rows : t * rows] = jnp.where((lag == t) & same, 1.0, 0.0).astype(BF16)
            shift_edge[(t - 1) * EDGE : t * EDGE] = jnp.where((lag_edge == t) & same_edge, 1.0, 0.0)

    feats = []
    for i in range(3):
        x = x_ref[i]
        w = sf_ref[i]
        moved = dot(shift[...], x)
        acc = w[0:1] * x.astype(F32)
        for t in range(1, taps):
            acc = acc + w[t : t + 1] * moved[(t - 1) * rows : t * rows]
        edge = jnp.concatenate([edge_ref[i].astype(F32), jnp.zeros((rows - EDGE, x.shape[1]), F32)], 0)
        moved_edge = dot(shift_edge[...].astype(BF16), edge.astype(BF16))
        fix = w[1:2] * moved_edge[0:EDGE]
        for t in range(2, taps):
            fix = fix + w[t : t + 1] * moved_edge[(t - 1) * EDGE : t * EDGE]
        acc = jnp.concatenate([acc[0:EDGE] + fix, acc[EDGE:]], 0)
        feat_ref[i] = acc
        feats.append(acc)
    kv_ref[...] = (feats[1] * feats[2]).astype(BF16)
    g = cot_ref[...].astype(F32) * feats[0]
    id_wide = jnp.concatenate([ids_ref[...].astype(F32)] * (g.shape[1] // rows), 1)
    last = iota2(g.shape, 0) == rows - 1
    g_ref[...] = jnp.where(last, jnp.broadcast_to(id_wide, g.shape), g).astype(BF16)


def mixer_kernel(ids_ref, sf_ref, lf_ref, x_ref, cot_ref, edge_ref, ids_edge_ref, feat_ref,
                 kvp_ref, gn_ref, out_ref, qg_ref, tail_ref, part_ref, packed_ref,
                 shift, mask_y, mask_g, mask_a, w_kv, w_g, g_rev, y_ref, gm_ref, dh_ref, lfr_ref, short_ref):
    rows = x_ref.shape[1]
    taps = sf_ref.shape[1]
    lanes = x_ref.shape[2]
    groups = lf_ref.shape[0]
    width = lanes // groups
    lag = iota2((rows, rows), 0) - iota2((rows, rows), 1)
    flip = jnp.where(iota2((rows, rows), 0) + iota2((rows, rows), 1) == rows - 1, 1.0, 0.0)
    mirror = flip.astype(BF16)

    @pl.when(pl.program_id(0) == 0)
    def _():
        id_row = jnp.broadcast_to(ids_ref[...], (rows, rows)).astype(F32)
        id_col = id_row.T
        prev_row = jnp.broadcast_to(ids_edge_ref[0, 0:1, 0:rows].astype(F32), (rows, rows))
        prev_col = prev_row.T
        next_row = jnp.broadcast_to(gn_ref[rows - 1 : rows, 0:rows].astype(F32), (rows, rows))
        same = id_row == id_col
        own = jnp.where((lag >= 0) & same, 1.0, 0.0)
        prev = jnp.where((lag < 0) & (prev_row == id_col), 1.0, 0.0)
        mask_y[:, 0:rows] = own.astype(BF16)
        mask_y[:, rows:] = prev.astype(BF16)
        mask_a[...] = dot(mirror, mask_y[...])
        mask_g[:, 0:rows] = jnp.where((lag <= 0) & same, 1.0, 0.0).astype(BF16)
        mask_g[:, rows:] = jnp.where((lag > 0) & (next_row == id_col), 1.0, 0.0).astype(BF16)
        for t in range(1, taps):
            shift[(t - 1) * rows : t * rows] = jnp.where((lag == -t) & same, 1.0, 0.0).astype(BF16)
        base = (taps - 1) * rows
        lag_edge = iota2((EDGE, rows), 1) + EDGE - iota2((EDGE, rows), 0)
        same_edge = prev_col[rows - EDGE :] == id_row[0:EDGE]
        pieces = [jnp.where((lag_edge == t) & same_edge, 1.0, 0.0) for t in range(1, taps)]
        shift[base : base + (taps - 1) * EDGE] = jnp.concatenate(pieces, 0).astype(BF16)

    cot = cot_ref[...].astype(F32)
    g32 = cot * feat_ref[0]
    w_kv[0:rows] = (feat_ref[1] * feat_ref[2]).astype(BF16)
    w_kv[rows:] = kvp_ref[...]
    w_g[0:rows] = g32.astype(BF16)
    w_g[rows:] = gn_ref[...]
    g_rev[...] = dot(mirror, w_g[0:rows]).astype(BF16)

    half = rows
    per = half // width
    backward = jnp.where((iota2((rows, rows), 0) + iota2((rows, rows), 1)) % rows == 0, 1.0, 0.0)
    lfr_ref[...] = dot(lf_ref[...].astype(BF16), backward.astype(BF16))
    owner = iota2((rows, half), 1) // width

    def one_part(part, carry):
        cols = pl.ds(pl.multiple_of(part * half, half), half)
        w_kv_part = w_kv[:, cols]
        w_g_part = w_g[:, cols]
        g_part = g_rev[:, cols]
        y_part = jnp.zeros((rows, half), F32)
        gm_part = jnp.zeros((rows, half), F32)
        for j in range(per):
            g = part * per + j
            mine = owner == j
            fwd = jnp.broadcast_to(lfr_ref[pl.ds(g, 1), :], (rows, rows))
            fwd = pltpu.roll(fwd, 0, 1, stride=1, stride_axis=0).astype(BF16)
            t_y = jnp.concatenate([fwd, fwd], 1) * mask_y[...]
            y_part = jnp.where(mine, dot(t_y, w_kv_part), y_part)
            bwd = jnp.broadcast_to(lf_ref[pl.ds(g, 1), :], (rows, rows))
            bwd = pltpu.roll(bwd, 0, 1, stride=1, stride_axis=0).astype(BF16)
            t_g = jnp.concatenate([bwd, bwd], 1) * mask_g[...]
            gm_part = jnp.where(mine, dot(t_g, w_g_part), gm_part)
            g_sel = jnp.where(mine, g_part, jnp.zeros((rows, half), BF16))
            cross = lax.dot_general(
                g_sel, w_kv_part, (((1,), (1,)), ((), ())), preferred_element_type=F32
            ) * mask_a[...]
            folded = cross[:, 0:rows] + cross[:, rows:]
            folded = pltpu.roll(folded, 0, 1, stride=1, stride_axis=0)
            dh_ref[pl.ds(g, 1), :] = jnp.sum(folded, 0, keepdims=True)
        y_ref[:, cols] = y_part
        gm_ref[:, cols] = gm_part
        return carry

    lax.fori_loop(0, lanes // half, one_part, 0)

    dh = jnp.dot(dh_ref[...], flip, preferred_element_type=F32, precision=lax.Precision.HIGHEST)

    y = y_ref[...]
    gm = gm_ref[...]
    out_ref[...] = (feat_ref[0] * y).astype(BF16)
    for i in range(3):
        gf = cot * y if i == 0 else gm * feat_ref[3 - i]
        w = sf_ref[i]
        x = x_ref[i].astype(F32)
        xe = edge_ref[i].astype(F32)
        moved = dot(shift[...], gf.astype(BF16))
        base = (taps - 1) * rows
        acc = w[0:1] * gf
        short_ref[i, 0:1] = jnp.sum(x * gf, 0, keepdims=True)
        sent = jnp.zeros((EDGE, lanes), F32)
        for t in range(1, taps):
            piece = moved[(t - 1) * rows : t * rows]
            piece_edge = moved[base + (t - 1) * EDGE : base + t * EDGE]
            acc = acc + w[t : t + 1] * piece
            sent = sent + w[t : t + 1] * piece_edge
            short_ref[i, t : t + 1] = (
                jnp.sum(x * piece, 0, keepdims=True) + jnp.sum(xe * piece_edge, 0, keepdims=True)
            )
        short_ref[i, taps:] = jnp.zeros((short_ref.shape[1] - taps, lanes), F32)
        qg_ref[i] = acc.astype(BF16)
        tail_ref[i] = acc[rows - EDGE :]
        part_ref[i] = sent.astype(BF16)

    chunk = packed_ref.shape[2]
    pairs = chunk // rows
    size = groups * rows // lanes
    for k in range(lanes // chunk):
        heads = [short_ref[i, :, k * chunk : (k + 1) * chunk] for i in range(3)]
        first = k * pairs * size
        rest = [dh[first + p * size : first + (p + 1) * size] for p in range(pairs)]
        packed_ref[k] = jnp.concatenate(heads + [jnp.concatenate(rest, 1)], 0).astype(BF16)


def finish_kernel(scale, taps, got_ref, long_ref, short_ref):
    total = got_ref[0].astype(F32)
    for k in range(1, got_ref.shape[0]):
        total = total + got_ref[k].astype(F32)
    total = total * scale
    padded = short_ref.shape[1] + 1
    for i in range(3):
        short_ref[i] = total[i * padded : i * padded + taps]
    size = total.shape[0] - 3 * padded
    lags = long_ref.shape[1]
    for p in range(total.shape[1] // lags):
        long_ref[p * size : (p + 1) * size] = total[3 * padded :, p * lags : (p + 1) * lags]


def shards(qkv, cotangent, doc_ids, short_filter, long_filter):
    _, rows, chans = qkv.shape
    groups, long_taps = long_filter.shape
    taps = short_filter.shape[2]
    devices = lax.axis_size("ctx")
    grad_scale = 1.0 / math.sqrt(rows * devices)
    tile_groups = TILE * groups // chans
    padded_taps = 8
    params = pltpu.CompilerParams(vmem_limit_bytes=60 << 20, dimension_semantics=("arbitrary",))

    ids = doc_ids.reshape(1, rows)
    sf = jnp.transpose(short_filter, (0, 2, 1))
    chunk = 2 * rows
    packed_rows = 3 * padded_taps + groups * long_taps // chans

    edge = qkv[:, rows - EDGE :, :]
    id_lanes = jnp.pad(doc_ids.astype(BF16), (0, chans - rows))
    first = (lax.broadcasted_iota(jnp.int32, edge.shape, 0) + lax.broadcasted_iota(jnp.int32, edge.shape, 1)) == 0
    edge = jnp.where(first, id_lanes[None, None, :], edge)
    edge = passed_along(edge, 1)

    fixed = lambda shape: pl.BlockSpec(shape, lambda c: (0,) * len(shape))
    wide3 = lambda n: pl.BlockSpec((3, n, TILE), lambda c: (0, 0, c))
    wide2 = lambda n: pl.BlockSpec((n, TILE), lambda c: (0, c))
    feats, kv, grad = pl.pallas_call(
        feature_kernel,
        grid=(chans // TILE,),
        in_specs=[fixed((1, rows)), wide3(taps), wide3(rows), wide2(rows), wide3(EDGE), fixed((3, EDGE, TILE))],
        out_specs=[wide3(rows), wide2(rows), wide2(rows)],
        out_shape=[
            jax.ShapeDtypeStruct((3, rows, chans), F32),
            jax.ShapeDtypeStruct((rows, chans), BF16),
            jax.ShapeDtypeStruct((rows, chans), BF16),
        ],
        scratch_shapes=[
            pltpu.VMEM(((taps - 1) * rows, rows), BF16),
            pltpu.VMEM(((taps - 1) * EDGE, rows), F32),
        ],
        compiler_params=params,
        name="features",
    )(ids, sf, qkv, cotangent, edge, edge)

    kv_prev = passed_along(kv, 1)
    grad_next = passed_along(grad, -1)

    out, qg, tail, part, packed = pl.pallas_call(
        mixer_kernel,
        grid=(chans // TILE,),
        in_specs=[
            fixed((1, rows)), wide3(taps),
            pl.BlockSpec((tile_groups, long_taps), lambda c: (c, 0)),
            wide3(rows), wide2(rows), wide3(EDGE), fixed((3, EDGE, TILE)), wide3(rows),
            wide2(rows), wide2(rows),
        ],
        out_specs=[
            wide2(rows), wide3(rows), wide3(EDGE), wide3(EDGE),
            pl.BlockSpec((TILE // chunk, packed_rows, chunk), lambda c: (c, 0, 0)),
        ],
        out_shape=[
            jax.ShapeDtypeStruct((rows, chans), BF16),
            jax.ShapeDtypeStruct((3, rows, chans), BF16),
            jax.ShapeDtypeStruct((3, EDGE, chans), F32),
            jax.ShapeDtypeStruct((3, EDGE, chans), BF16),
            jax.ShapeDtypeStruct((chans // chunk, packed_rows, chunk), BF16),
        ],
        scratch_shapes=[
            pltpu.VMEM(((taps - 1) * (rows + EDGE), rows), BF16),
            pltpu.VMEM((rows, 2 * rows), BF16),
            pltpu.VMEM((rows, 2 * rows), BF16),
            pltpu.VMEM((rows, 2 * rows), F32),
            pltpu.VMEM((2 * rows, TILE), BF16),
            pltpu.VMEM((2 * rows, TILE), BF16),
            pltpu.VMEM((rows, TILE), BF16),
            pltpu.VMEM((rows, TILE), F32),
            pltpu.VMEM((rows, TILE), F32),
            pltpu.VMEM((tile_groups, long_taps), F32),
            pltpu.VMEM((tile_groups, long_taps), F32),
            pltpu.VMEM((3, padded_taps, TILE), F32),
        ],
        compiler_params=params,
        name="mixer",
    )(ids, sf, long_filter, qkv, cotangent, edge, edge, feats, kv_prev, grad_next)

    part = passed_along(part, -1)
    qg = lax.dynamic_update_slice(qg, (tail + part.astype(F32)).astype(BF16), (0, rows - EDGE, 0))

    per = chans // devices
    if per == chunk:
        got = lax.all_to_all(packed, "ctx", 0, 0)
        long_grad, short_grad = pl.pallas_call(
            functools.partial(finish_kernel, grad_scale, taps),
            out_shape=[
                jax.ShapeDtypeStruct((groups // devices, long_taps), F32),
                jax.ShapeDtypeStruct((3, taps, per), F32),
            ],
            name="finish",
        )(got)
        return (out, qg, long_grad, short_grad.transpose(0, 2, 1))
    head = 3 * padded_taps
    short_part = packed[:, :head].transpose(1, 0, 2).reshape(head, devices, per)
    long_part = packed[:, head:].reshape(-1, packed_rows - head, chunk // long_taps, long_taps)
    long_part = long_part.transpose(0, 2, 1, 3).reshape(devices, -1, per)
    got = jnp.concatenate([short_part.transpose(1, 0, 2), long_part], 1)
    got = lax.all_to_all(got, "ctx", 0, 0)
    total = jnp.sum(got.astype(F32), 0) * grad_scale
    short_grad = total[:head].reshape(3, padded_taps, per)[:, :taps].transpose(0, 2, 1)
    long_grad = total[head:].reshape(groups // devices, long_taps)
    return (out, qg, long_grad, short_grad)


def solution(mesh):
    in_specs = (P(None, "ctx", "tp"), P("ctx", "tp"), P("ctx"), P(None, "tp", None), P("tp", None))
    out_specs = (
        P("ctx", "tp"),
        P(None, "ctx", "tp"),
        P(("tp", "ctx"), None),
        P(None, ("tp", "ctx"), None),
    )
    return jax.shard_map(shards, mesh=mesh, in_specs=in_specs, out_specs=out_specs, check_vma=False)
```

```python
import functools
import math

import jax
import jax.numpy as jnp
from jax import lax
from jax.experimental import pallas as pl
from jax.experimental.pallas import tpu as pltpu
from jax.sharding import PartitionSpec as P

F32 = jnp.float32
BF16 = jnp.bfloat16
EDGE = 8
LANES = 512
CHUNK = 256
PADDED = 8
PARTS = 2

VMEM = pl.BlockSpec(memory_space=pltpu.VMEM)
ANY = pl.BlockSpec(memory_space=pl.ANY)
HBM = pl.BlockSpec(memory_space=pltpu.HBM)


def passed_along(block, distance):
    devices = range(lax.axis_size("ctx"))
    route = [(i - distance, i) for i in devices if i - distance in devices]
    return lax.ppermute(block, "ctx", route)


def iota2(shape, dim):
    return lax.broadcasted_iota(jnp.int32, shape, dim)


def dot(a, b):
    return jnp.dot(a, b, preferred_element_type=F32)


def lane_range(start, size):
    return pl.ds(pl.multiple_of(start, size), size)


def ones_where(cond):
    return jnp.where(cond, 1.0, 0.0)


def prepare_kernel(ids_ref, lf_ref, delay_ref, advance_ref, lfr_ref):
    rows = delay_ref.shape[1]
    taps = delay_ref.shape[0] // rows + 1
    id_row = jnp.broadcast_to(ids_ref[...], (rows, rows)).astype(F32)
    same = id_row == id_row.T
    lag = iota2((rows, rows), 0) - iota2((rows, rows), 1)
    for t in range(1, taps):
        delay_ref[(t - 1) * rows : t * rows] = ones_where((lag == t) & same).astype(BF16)
        advance_ref[(t - 1) * rows : t * rows] = ones_where((lag == -t) & same).astype(BF16)
    backward = ones_where((iota2((rows, rows), 0) + iota2((rows, rows), 1)) % rows == 0)
    lfr_ref[...] = dot(lf_ref[...].astype(BF16), backward.astype(BF16))


def feature_kernel(first, ids_ref, delay_ref, edge_ref, sf_hbm, x_hbm, cot_hbm,
                   feat_ref, kv_ref, g_ref, edge_shift, sf_ref, x_ref, cot_ref, sems):
    rows = x_ref.shape[1]
    taps = sf_ref.shape[1]
    steps = kv_ref.shape[1] // LANES

    def loads(p):
        near = lane_range(p * LANES, LANES)
        cols = lane_range(first + p * LANES, LANES)
        pairs = [
            (sf_hbm.at[:, :, cols], sf_ref.at[:, :, near]),
            (x_hbm.at[:, :, cols], x_ref.at[:, :, near]),
            (cot_hbm.at[:, cols], cot_ref.at[:, near]),
        ]
        return [pltpu.make_async_copy(src, dst, sems.at[k, p]) for k, (src, dst) in enumerate(pairs)]

    for p in range(steps):
        for copy in loads(p):
            copy.start()
    id_row = jnp.broadcast_to(ids_ref[...], (rows, rows)).astype(F32)
    head_ids = id_row.T[0:EDGE]
    before = jnp.broadcast_to(edge_ref[0, 0:1, 0:rows].astype(F32), (EDGE, rows))
    before = pltpu.roll(before, EDGE, 1)
    lag = iota2((EDGE, rows), 0) + EDGE - iota2((EDGE, rows), 1)
    for t in range(1, taps):
        edge_shift[(t - 1) * EDGE : t * EDGE] = ones_where((lag == t) & (before == head_ids))
    id_wide = jnp.concatenate([ids_ref[...].astype(F32)] * (LANES // rows), 1)

    def one_step(p, carry):
        near = lane_range(p * LANES, LANES)
        cols = lane_range(first + p * LANES, LANES)
        for copy in loads(p):
            copy.wait()
        feats = []
        for i in range(3):
            x = x_ref[i, :, near]
            w = sf_ref[i, :, near]
            moved = dot(delay_ref[...], x)
            acc = w[0:1] * x.astype(F32)
            for t in range(1, taps):
                acc = acc + w[t : t + 1] * moved[(t - 1) * rows : t * rows]
            edge = edge_ref[i, :, cols].astype(F32)
            edge = jnp.concatenate([edge, jnp.zeros((rows - EDGE, LANES), F32)], 0)
            moved = dot(edge_shift[...].astype(BF16), edge.astype(BF16))
            fix = w[1:2] * moved[0:EDGE]
            for t in range(2, taps):
                fix = fix + w[t : t + 1] * moved[(t - 1) * EDGE : t * EDGE]
            acc = jnp.concatenate([acc[0:EDGE] + fix, acc[EDGE:]], 0)
            feat_ref[i, :, near] = acc
            feats.append(acc)
        kv_ref[:, near] = (feats[1] * feats[2]).astype(BF16)
        g = cot_ref[:, near].astype(F32) * feats[0]
        last = iota2(g.shape, 0) == rows - 1
        g_ref[:, near] = jnp.where(last, jnp.broadcast_to(id_wide, g.shape), g).astype(BF16)
        return carry

    lax.fori_loop(0, steps, one_step, 0)


def mixer_kernel(first, filled, ids_ref, sf_ref, lf_ref, lfr_ref, advance_ref, x_ref, cot_ref, edge_ref,
                 feat_ref, kvp_ref, gn_ref, *refs):
    (out_hbm, qg_hbm, tail_hbm, part_hbm, packed_hbm, out_ref, qg_ref, tail_ref, part_ref, packed_ref,
     edge_shift, mask_y, mask_g, mask_a, w_kv, w_g, g_rev, dh_ref, y_ref, gm_ref, sems) = refs[filled:]
    rows = x_ref.shape[1]
    taps = sf_ref.shape[1]
    count = kvp_ref.shape[1]
    width = x_ref.shape[2] // lf_ref.shape[0]
    half = rows
    per = half // width
    lag = iota2((rows, rows), 0) - iota2((rows, rows), 1)
    flip = ones_where(iota2((rows, rows), 0) + iota2((rows, rows), 1) == rows - 1)
    mirror = flip.astype(BF16)
    id_row = jnp.broadcast_to(ids_ref[...], (rows, rows)).astype(F32)
    id_col = id_row.T
    prev_row = jnp.broadcast_to(edge_ref[0, 0:1, 0:rows].astype(F32), (rows, rows))
    next_row = jnp.broadcast_to(gn_ref[rows - 1 : rows, 0:rows].astype(F32), (rows, rows))
    same = id_row == id_col
    mask_y[:, 0:rows] = ones_where((lag >= 0) & same).astype(BF16)
    mask_y[:, rows:] = ones_where((lag < 0) & (prev_row == id_col)).astype(BF16)
    mask_g[:, 0:rows] = ones_where((lag <= 0) & same).astype(BF16)
    mask_g[:, rows:] = ones_where((lag > 0) & (next_row == id_col)).astype(BF16)
    mask_a[...] = dot(mirror, mask_y[...])
    lag_edge = iota2((EDGE, rows), 1) + EDGE - iota2((EDGE, rows), 0)
    same_edge = prev_row.T[rows - EDGE :] == id_row[0:EDGE]
    pieces = [ones_where((lag_edge == t) & same_edge) for t in range(1, taps)]
    edge_shift[...] = jnp.concatenate(pieces, 0).astype(BF16)
    owner = iota2((rows, half), 1) // width
    blocks = LANES // CHUNK

    def copies(p):
        near = lane_range(p * LANES, LANES)
        cols = lane_range(first + p * LANES, LANES)
        pairs = [
            (out_ref.at[:, near], out_hbm.at[:, cols]),
            (qg_ref.at[:, :, near], qg_hbm.at[:, :, cols]),
            (tail_ref.at[:, :, near], tail_hbm.at[:, :, cols]),
            (part_ref.at[:, :, near], part_hbm.at[:, :, cols]),
            (packed_ref.at[pl.ds(p * blocks, blocks)], packed_hbm.at[pl.ds(first // CHUNK + p * blocks, blocks)]),
        ]
        return [pltpu.make_async_copy(src, dst, sems.at[k, p]) for k, (src, dst) in enumerate(pairs)]

    def one_step(p, carry):
        near = lane_range(p * LANES, LANES)
        cols = lane_range(first + p * LANES, LANES)
        cot = cot_ref[:, cols].astype(F32)
        w_kv[0:rows] = (feat_ref[1, :, near] * feat_ref[2, :, near]).astype(BF16)
        w_kv[rows:] = kvp_ref[:, near]
        w_g[0:rows] = (cot * feat_ref[0, :, near]).astype(BF16)
        w_g[rows:] = gn_ref[:, near]
        g_rev[...] = dot(mirror, w_g[0:rows]).astype(BF16)
        for q in range(LANES // half):
            part = slice(q * half, (q + 1) * half)
            base = pl.multiple_of((first // half) * per + p * (LANES // width) + q * per, per)
            for j in range(per):
                mine = owner == j
                fwd = jnp.broadcast_to(lfr_ref[pl.ds(base + j, 1), :], (rows, rows))
                fwd = pltpu.roll(fwd, 0, 1, stride=1, stride_axis=0).astype(BF16)
                t_y = jnp.concatenate([fwd, fwd], 1) * mask_y[...]
                pltpu.store(y_ref.at[:, part], dot(t_y, w_kv[:, part]), mask=mine)
                bwd = jnp.broadcast_to(lf_ref[pl.ds(base + j, 1), :], (rows, rows))
                bwd = pltpu.roll(bwd, 0, 1, stride=1, stride_axis=0).astype(BF16)
                t_g = jnp.concatenate([bwd, bwd], 1) * mask_g[...]
                pltpu.store(gm_ref.at[:, part], dot(t_g, w_g[:, part]), mask=mine)
                g_sel = jnp.where(mine, g_rev[:, part], jnp.zeros((rows, half), BF16))
                cross = lax.dot_general(
                    g_sel, w_kv[:, part], (((1,), (1,)), ((), ())), preferred_element_type=F32
                ) * mask_a[...]
                folded = cross[:, 0:rows] + cross[:, rows:]
                folded = pltpu.roll(folded, 0, 1, stride=1, stride_axis=0)
                dh_ref[q * per + j : q * per + j + 1] = jnp.sum(folded, 0, keepdims=True)
        dh = jnp.dot(dh_ref[...], flip, preferred_element_type=F32, precision=lax.Precision.HIGHEST)
        y = y_ref[...]
        gm = gm_ref[...]
        out_ref[:, near] = (feat_ref[0, :, near] * y).astype(BF16)
        heads = []
        for i in range(3):
            gf = cot * y if i == 0 else gm * feat_ref[3 - i, :, near]
            w = sf_ref[i, :, cols]
            x = x_ref[i, :, cols].astype(F32)
            xe = edge_ref[i, :, cols].astype(F32)
            gf_sent = gf.astype(BF16)
            moved = dot(advance_ref[...], gf_sent)
            moved_edge = dot(edge_shift[...], gf_sent)
            acc = w[0:1] * gf
            sums = [jnp.sum(x * gf, 0, keepdims=True)]
            sent = jnp.zeros((EDGE, LANES), F32)
            for t in range(1, taps):
                piece = moved[(t - 1) * rows : t * rows]
                piece_edge = moved_edge[(t - 1) * EDGE : t * EDGE]
                acc = acc + w[t : t + 1] * piece
                sent = sent + w[t : t + 1] * piece_edge
                sums.append(jnp.sum(x * piece, 0, keepdims=True) + jnp.sum(xe * piece_edge, 0, keepdims=True))
            sums.append(jnp.zeros((PADDED - taps, LANES), F32))
            qg_ref[i, :, near] = acc.astype(BF16)
            tail_ref[i, :, near] = acc[rows - EDGE :]
            part_ref[i, :, near] = sent.astype(BF16)
            heads.append(jnp.concatenate(sums, 0))
        size = dh.shape[0] * rows // LANES
        for k in range(blocks):
            picked = [head[:, k * CHUNK : (k + 1) * CHUNK] for head in heads]
            lines = range(k * (CHUNK // rows), (k + 1) * (CHUNK // rows))
            picked.append(jnp.concatenate([dh[e * size : (e + 1) * size] for e in lines], 1))
            packed_ref[p * blocks + k] = jnp.concatenate(picked, 0).astype(BF16)
        for copy in copies(p):
            copy.start()
        return carry

    def drain(p, carry):
        for copy in copies(p):
            copy.wait()
        return carry

    lax.fori_loop(0, count // LANES, one_step, 0)
    lax.fori_loop(0, count // LANES, drain, 0)


def finish_kernel(scale, taps, got_ref, long_ref, short_ref):
    total = got_ref[0].astype(F32)
    for k in range(1, got_ref.shape[0]):
        total = total + got_ref[k].astype(F32)
    total = total * scale
    for i in range(3):
        short_ref[i] = total[i * PADDED : i * PADDED + taps]
    size = total.shape[0] - 3 * PADDED
    lags = long_ref.shape[1]
    for p in range(total.shape[1] // lags):
        long_ref[p * size : (p + 1) * size] = total[3 * PADDED :, p * lags : (p + 1) * lags]


def shards(qkv, cotangent, doc_ids, short_filter, long_filter):
    _, rows, chans = qkv.shape
    groups, long_taps = long_filter.shape
    taps = short_filter.shape[2]
    devices = lax.axis_size("ctx")
    grad_scale = 1.0 / math.sqrt(rows * devices)
    packed_rows = 3 * PADDED + groups * long_taps // chans
    step_groups = LANES * groups // chans
    params = pltpu.CompilerParams(vmem_limit_bytes=24 << 20)

    ids = doc_ids.reshape(1, rows)
    sf = jnp.transpose(short_filter, (0, 2, 1))

    edge = qkv[:, rows - EDGE :, :]
    id_lanes = jnp.broadcast_to(doc_ids.astype(BF16), (chans // rows, rows)).reshape(chans)
    first = (lax.broadcasted_iota(jnp.int32, edge.shape, 0) + lax.broadcasted_iota(jnp.int32, edge.shape, 1)) == 0
    edge = jnp.where(first, id_lanes[None, None, :], edge)
    edge = passed_along(edge, 1)

    shifts = ((taps - 1) * rows, rows)
    delay, advance, lf_rev = pl.pallas_call(
        prepare_kernel,
        in_specs=[VMEM] * 2,
        out_specs=[VMEM] * 3,
        out_shape=[
            jax.ShapeDtypeStruct(shifts, BF16),
            jax.ShapeDtypeStruct(shifts, BF16),
            jax.ShapeDtypeStruct((groups, long_taps), F32),
        ],
        cost_estimate=pl.CostEstimate(flops=6_000_000_000, bytes_accessed=16_000_000, transcendentals=0),
        compiler_params=pltpu.CompilerParams(vmem_limit_bytes=8 << 20),
        name="prepare",
    )(ids, long_filter)

    count = chans // PARTS
    sent = []
    for part in range(PARTS):
        feats, kv, grad = pl.pallas_call(
            functools.partial(feature_kernel, part * count),
            in_specs=[VMEM] * 3 + [HBM] * 3,
            out_specs=[VMEM] * 3,
            out_shape=[
                jax.ShapeDtypeStruct((3, rows, count), F32),
                jax.ShapeDtypeStruct((rows, count), BF16),
                jax.ShapeDtypeStruct((rows, count), BF16),
            ],
            scratch_shapes=[
                pltpu.VMEM(((taps - 1) * EDGE, rows), F32),
                pltpu.VMEM((3, taps, count), F32),
                pltpu.VMEM((3, rows, count), BF16),
                pltpu.VMEM((rows, count), BF16),
                pltpu.SemaphoreType.DMA((3, count // LANES)),
            ],
            compiler_params=params,
            cost_estimate=pl.CostEstimate(flops=2_000_000_000, bytes_accessed=4_000_000, transcendentals=0),
            name="features",
        )(ids, delay, edge, sf, qkv, cotangent)
        sent.append((feats, passed_along(kv, 1), passed_along(grad, -1)))

    results = []
    full = [
        jax.ShapeDtypeStruct((rows, chans), BF16),
        jax.ShapeDtypeStruct((3, rows, chans), BF16),
        jax.ShapeDtypeStruct((3, EDGE, chans), F32),
        jax.ShapeDtypeStruct((3, EDGE, chans), BF16),
        jax.ShapeDtypeStruct((chans // CHUNK, packed_rows, CHUNK), BF16),
    ]
    for part in range(PARTS):
        feats, kv_prev, grad_next = sent[part]
        filled = len(results)
        results = pl.pallas_call(
            functools.partial(mixer_kernel, part * count, filled),
            in_specs=[VMEM] * 11 + [ANY] * filled,
            out_specs=[ANY] * 5,
            out_shape=full,
            input_output_aliases={11 + k: k for k in range(filled)},
            scratch_shapes=[
                pltpu.VMEM((rows, count), BF16),
                pltpu.VMEM((3, rows, count), BF16),
                pltpu.VMEM((3, EDGE, count), F32),
                pltpu.VMEM((3, EDGE, count), BF16),
                pltpu.VMEM((count // CHUNK, packed_rows, CHUNK), BF16),
                pltpu.VMEM(((taps - 1) * EDGE, rows), BF16),
                pltpu.VMEM((rows, 2 * rows), BF16),
                pltpu.VMEM((rows, 2 * rows), BF16),
                pltpu.VMEM((rows, 2 * rows), F32),
                pltpu.VMEM((2 * rows, LANES), BF16),
                pltpu.VMEM((2 * rows, LANES), BF16),
                pltpu.VMEM((rows, LANES), BF16),
                pltpu.VMEM((step_groups, long_taps), F32),
                pltpu.VMEM((rows, LANES), F32),
                pltpu.VMEM((rows, LANES), F32),
                pltpu.SemaphoreType.DMA((5, count // LANES)),
            ],
            compiler_params=params,
            cost_estimate=pl.CostEstimate(flops=8_000_000_000, bytes_accessed=8_000_000, transcendentals=0),
            name="mixer",
        )(ids, sf, long_filter, lf_rev, advance, qkv, cotangent, edge, feats, kv_prev, grad_next, *results)
    out, qg, tail, part, packed = results

    part = passed_along(part, -1)
    qg = lax.dynamic_update_slice(qg, (tail + part.astype(F32)).astype(BF16), (0, rows - EDGE, 0))

    per = chans // devices
    if per == CHUNK:
        got = lax.all_to_all(packed, "ctx", 0, 0)
        long_grad, short_grad = pl.pallas_call(
            functools.partial(finish_kernel, grad_scale, taps),
            in_specs=[VMEM],
            out_specs=[VMEM] * 2,
            out_shape=[
                jax.ShapeDtypeStruct((groups // devices, long_taps), F32),
                jax.ShapeDtypeStruct((3, taps, per), F32),
            ],
            compiler_params=pltpu.CompilerParams(vmem_limit_bytes=8 << 20),
            cost_estimate=pl.CostEstimate(flops=1_000_000, bytes_accessed=200_000, transcendentals=0),
            name="finish",
        )(got)
        return (out, qg, long_grad, short_grad.transpose(0, 2, 1))
    head = 3 * PADDED
    short_part = packed[:, :head].transpose(1, 0, 2).reshape(head, devices, per)
    long_part = packed[:, head:].reshape(-1, packed_rows - head, CHUNK // long_taps, long_taps)
    long_part = long_part.transpose(0, 2, 1, 3).reshape(devices, -1, per)
    got = jnp.concatenate([short_part.transpose(1, 0, 2), long_part], 1)
    got = lax.all_to_all(got, "ctx", 0, 0)
    total = jnp.sum(got.astype(F32), 0) * grad_scale
    short_grad = total[:head].reshape(3, PADDED, per)[:, :taps].transpose(0, 2, 1)
    long_grad = total[head:].reshape(groups // devices, long_taps)
    return (out, qg, long_grad, short_grad)


def solution(mesh):
    in_specs = (P(None, "ctx", "tp"), P("ctx", "tp"), P("ctx"), P(None, "tp", None), P("tp", None))
    out_specs = (
        P("ctx", "tp"),
        P(None, "ctx", "tp"),
        P(("tp", "ctx"), None),
        P(None, ("tp", "ctx"), None),
    )
    return jax.shard_map(shards, mesh=mesh, in_specs=in_specs, out_specs=out_specs, check_vma=False)
```

```python
import functools
import math

import jax
import jax.numpy as jnp
from jax import lax
from jax.experimental import pallas as pl
from jax.experimental.pallas import tpu as pltpu
from jax.sharding import PartitionSpec as P

F32 = jnp.float32
BF16 = jnp.bfloat16
EDGE = 8
LANES = 512
CHUNK = 256
PADDED = 8
PARTS = 2

VMEM = pl.BlockSpec(memory_space=pltpu.VMEM)
ANY = pl.BlockSpec(memory_space=pl.ANY)
HBM = pl.BlockSpec(memory_space=pltpu.HBM)


def passed_along(block, distance):
    devices = range(lax.axis_size("ctx"))
    route = [(i - distance, i) for i in devices if i - distance in devices]
    return lax.ppermute(block, "ctx", route)


def iota2(shape, dim):
    return lax.broadcasted_iota(jnp.int32, shape, dim)


def dot(a, b):
    return jnp.dot(a, b, preferred_element_type=F32)


def lane_range(start, size):
    return pl.ds(pl.multiple_of(start, size), size)


def ones_where(cond):
    return jnp.where(cond, 1.0, 0.0)


def prepare_kernel(ids_ref, lf_ref, delay_ref, advance_ref, lfr_ref):
    rows = delay_ref.shape[1]
    taps = delay_ref.shape[0] // rows + 1
    id_row = jnp.broadcast_to(ids_ref[...], (rows, rows)).astype(F32)
    same = id_row == id_row.T
    lag = iota2((rows, rows), 0) - iota2((rows, rows), 1)
    for t in range(1, taps):
        delay_ref[(t - 1) * rows : t * rows] = ones_where((lag == t) & same).astype(BF16)
        advance_ref[(t - 1) * rows : t * rows] = ones_where((lag == -t) & same).astype(BF16)
    backward = ones_where((iota2((rows, rows), 0) + iota2((rows, rows), 1)) % rows == 0)
    lfr_ref[...] = dot(lf_ref[...].astype(BF16), backward.astype(BF16))


def edge_kernel(ids_ref, x_hbm, edge_ref, sem):
    rows = x_hbm.shape[1]
    copy = pltpu.make_async_copy(x_hbm.at[:, rows - EDGE :, :], edge_ref, sem)
    copy.start()
    copy.wait()
    top = edge_ref[0].astype(F32)
    id_wide = jnp.concatenate([ids_ref[...].astype(F32)] * (top.shape[1] // rows), 1)
    edge_ref[0] = jnp.where(iota2(top.shape, 0) == 0, jnp.broadcast_to(id_wide, top.shape), top).astype(BF16)


def feature_kernel(first, ids_ref, delay_ref, edge_ref, sf_hbm, x_hbm, cot_hbm,
                   feat_ref, kv_ref, g_ref, edge_shift, sf_ref, x_ref, cot_ref, sems):
    rows = x_ref.shape[1]
    taps = sf_ref.shape[1]
    steps = kv_ref.shape[1] // LANES

    def loads(p):
        near = lane_range(p * LANES, LANES)
        cols = lane_range(first + p * LANES, LANES)
        pairs = [
            (sf_hbm.at[:, :, cols], sf_ref.at[:, :, near]),
            (x_hbm.at[:, :, cols], x_ref.at[:, :, near]),
            (cot_hbm.at[:, cols], cot_ref.at[:, near]),
        ]
        return [pltpu.make_async_copy(src, dst, sems.at[k, p]) for k, (src, dst) in enumerate(pairs)]

    for p in range(steps):
        for copy in loads(p):
            copy.start()
    id_row = jnp.broadcast_to(ids_ref[...], (rows, rows)).astype(F32)
    head_ids = id_row.T[0:EDGE]
    before = jnp.broadcast_to(edge_ref[0, 0:1, 0:rows].astype(F32), (EDGE, rows))
    before = pltpu.roll(before, EDGE, 1)
    lag = iota2((EDGE, rows), 0) + EDGE - iota2((EDGE, rows), 1)
    for t in range(1, taps):
        edge_shift[(t - 1) * EDGE : t * EDGE] = ones_where((lag == t) & (before == head_ids))
    id_wide = jnp.concatenate([ids_ref[...].astype(F32)] * (LANES // rows), 1)

    def one_step(p, carry):
        near = lane_range(p * LANES, LANES)
        cols = lane_range(first + p * LANES, LANES)
        for copy in loads(p):
            copy.wait()
        feats = []
        for i in range(3):
            x = x_ref[i, :, near]
            w = sf_ref[i, :, near]
            moved = dot(delay_ref[...], x)
            acc = w[0:1] * x.astype(F32)
            for t in range(1, taps):
                acc = acc + w[t : t + 1] * moved[(t - 1) * rows : t * rows]
            edge = edge_ref[i, :, cols].astype(F32)
            edge = jnp.concatenate([edge, jnp.zeros((rows - EDGE, LANES), F32)], 0)
            moved = dot(edge_shift[...].astype(BF16), edge.astype(BF16))
            fix = w[1:2] * moved[0:EDGE]
            for t in range(2, taps):
                fix = fix + w[t : t + 1] * moved[(t - 1) * EDGE : t * EDGE]
            acc = jnp.concatenate([acc[0:EDGE] + fix, acc[EDGE:]], 0)
            feat_ref[i, :, near] = acc
            feats.append(acc)
        kv_ref[:, near] = (feats[1] * feats[2]).astype(BF16)
        g = cot_ref[:, near].astype(F32) * feats[0]
        last = iota2(g.shape, 0) == rows - 1
        g_ref[:, near] = jnp.where(last, jnp.broadcast_to(id_wide, g.shape), g).astype(BF16)
        return carry

    lax.fori_loop(0, steps, one_step, 0)


def mixer_kernel(first, filled, ids_ref, sf_ref, lf_ref, lfr_ref, advance_ref, x_ref, cot_ref, edge_ref,
                 feat_ref, kvp_ref, gn_ref, *refs):
    (out_hbm, qg_hbm, tail_hbm, part_hbm, packed_hbm, out_ref, qg_ref, tail_ref, part_ref, packed_ref,
     edge_shift, mask_y, mask_g, mask_a, w_kv, w_g, g_rev, dh_ref, kv_turned, g_turned, y_turned, gm_turned, sems) = refs[filled:]
    rows = x_ref.shape[1]
    taps = sf_ref.shape[1]
    count = kvp_ref.shape[1]
    width = x_ref.shape[2] // lf_ref.shape[0]
    half = rows
    per = half // width
    lag = iota2((rows, rows), 0) - iota2((rows, rows), 1)
    flip = ones_where(iota2((rows, rows), 0) + iota2((rows, rows), 1) == rows - 1)
    mirror = flip.astype(BF16)
    id_row = jnp.broadcast_to(ids_ref[...], (rows, rows)).astype(F32)
    id_col = id_row.T
    prev_row = jnp.broadcast_to(edge_ref[0, 0:1, 0:rows].astype(F32), (rows, rows))
    next_row = jnp.broadcast_to(gn_ref[rows - 1 : rows, 0:rows].astype(F32), (rows, rows))
    same = id_row == id_col
    prev_col = prev_row.T
    next_col = next_row.T
    own_later = ones_where((lag <= 0) & same).astype(BF16)
    own_earlier = ones_where((lag >= 0) & same).astype(BF16)
    mask_y[0:rows] = own_later
    mask_y[rows:] = ones_where((lag > 0) & (prev_col == id_row)).astype(BF16)
    mask_g[0:rows] = own_earlier
    mask_g[rows:] = ones_where((lag < 0) & (next_col == id_row)).astype(BF16)
    mask_prev = ones_where((lag < 0) & (prev_row == id_col)).astype(BF16)
    mask_a[:, 0:rows] = dot(mirror, own_earlier)
    mask_a[:, rows:] = dot(mirror, mask_prev)
    lag_edge = iota2((EDGE, rows), 1) + EDGE - iota2((EDGE, rows), 0)
    same_edge = prev_row.T[rows - EDGE :] == id_row[0:EDGE]
    pieces = [ones_where((lag_edge == t) & same_edge) for t in range(1, taps)]
    edge_shift[...] = jnp.concatenate(pieces, 0).astype(BF16)
    owner = iota2((rows, half), 1) // width
    blocks = LANES // CHUNK

    def copies(p):
        near = lane_range(p * LANES, LANES)
        cols = lane_range(first + p * LANES, LANES)
        pairs = [
            (out_ref.at[:, near], out_hbm.at[:, cols]),
            (qg_ref.at[:, :, near], qg_hbm.at[:, :, cols]),
            (tail_ref.at[:, :, near], tail_hbm.at[:, :, cols]),
            (part_ref.at[:, :, near], part_hbm.at[:, :, cols]),
            (packed_ref.at[pl.ds(p * blocks, blocks)], packed_hbm.at[pl.ds(first // CHUNK + p * blocks, blocks)]),
        ]
        return [pltpu.make_async_copy(src, dst, sems.at[k, p]) for k, (src, dst) in enumerate(pairs)]

    def one_step(p, carry):
        near = lane_range(p * LANES, LANES)
        cols = lane_range(first + p * LANES, LANES)
        cot = cot_ref[:, cols].astype(F32)
        w_kv[0:rows] = (feat_ref[1, :, near] * feat_ref[2, :, near]).astype(BF16)
        w_kv[rows:] = kvp_ref[:, near]
        w_g[0:rows] = (cot * feat_ref[0, :, near]).astype(BF16)
        w_g[rows:] = gn_ref[:, near]
        g_rev[...] = dot(mirror, w_g[0:rows]).astype(BF16)
        kv_turned[...] = w_kv[...].T
        g_turned[...] = w_g[...].T
        for q in range(LANES // half):
            part = slice(q * half, (q + 1) * half)
            base = pl.multiple_of((first // half) * per + p * (LANES // width) + q * per, per)
            for j in range(per):
                bwd = jnp.broadcast_to(lf_ref[pl.ds(base + j, 1), :], (rows, rows))
                bwd = pltpu.roll(bwd, 0, 1, stride=1, stride_axis=0).astype(BF16)
                t_y = jnp.concatenate([bwd, bwd], 0) * mask_y[...]
                mine = slice((q * per + j) * width, (q * per + j + 1) * width)
                y_turned[mine] = dot(kv_turned[mine], t_y)
                fwd = jnp.broadcast_to(lfr_ref[pl.ds(base + j, 1), :], (rows, rows))
                fwd = pltpu.roll(fwd, 0, 1, stride=1, stride_axis=0).astype(BF16)
                t_g = jnp.concatenate([fwd, fwd], 0) * mask_g[...]
                gm_turned[mine] = dot(g_turned[mine], t_g)
                g_sel = jnp.where(owner == j, g_rev[:, part], jnp.zeros((rows, half), BF16))
                cross = lax.dot_general(
                    g_sel, w_kv[:, part], (((1,), (1,)), ((), ())), preferred_element_type=F32
                ) * mask_a[...]
                folded = cross[:, 0:rows] + cross[:, rows:]
                folded = pltpu.roll(folded, 0, 1, stride=1, stride_axis=0)
                dh_ref[q * per + j : q * per + j + 1] = jnp.sum(folded, 0, keepdims=True)
        dh = dot(dh_ref[...].astype(BF16), mirror)
        y = y_turned[...].T
        gm = gm_turned[...].T
        out_ref[:, near] = (feat_ref[0, :, near] * y).astype(BF16)
        heads = []
        for i in range(3):
            gf = cot * y if i == 0 else gm * feat_ref[3 - i, :, near]
            w = sf_ref[i, :, cols]
            x = x_ref[i, :, cols].astype(F32)
            xe = edge_ref[i, :, cols].astype(F32)
            gf_sent = gf.astype(BF16)
            moved = dot(advance_ref[...], gf_sent)
            moved_edge = dot(edge_shift[...], gf_sent)
            acc = w[0:1] * gf
            sums = [jnp.sum(x * gf, 0, keepdims=True)]
            sent = jnp.zeros((EDGE, LANES), F32)
            for t in range(1, taps):
                piece = moved[(t - 1) * rows : t * rows]
                piece_edge = moved_edge[(t - 1) * EDGE : t * EDGE]
                acc = acc + w[t : t + 1] * piece
                sent = sent + w[t : t + 1] * piece_edge
                sums.append(jnp.sum(x * piece, 0, keepdims=True) + jnp.sum(xe * piece_edge, 0, keepdims=True))
            sums.append(jnp.zeros((PADDED - taps, LANES), F32))
            qg_ref[i, :, near] = acc.astype(BF16)
            tail_ref[i, :, near] = acc[rows - EDGE :]
            part_ref[i, :, near] = sent.astype(BF16)
            heads.append(jnp.concatenate(sums, 0))
        size = dh.shape[0] * rows // LANES
        for k in range(blocks):
            picked = [head[:, k * CHUNK : (k + 1) * CHUNK] for head in heads]
            lines = range(k * (CHUNK // rows), (k + 1) * (CHUNK // rows))
            picked.append(jnp.concatenate([dh[e * size : (e + 1) * size] for e in lines], 1))
            packed_ref[p * blocks + k] = jnp.concatenate(picked, 0).astype(BF16)
        for copy in copies(p):
            copy.start()
        return carry

    def drain(p, carry):
        for copy in copies(p):
            copy.wait()
        return carry

    lax.fori_loop(0, count // LANES, one_step, 0)
    lax.fori_loop(0, count // LANES, drain, 0)


def finish_kernel(scale, taps, got_ref, tail_ref, part_ref, qg_in, qg_hbm, long_ref, short_ref, last_ref, sem):
    rows = qg_hbm.shape[1]
    last_ref[...] = (tail_ref[...] + part_ref[...].astype(F32)).astype(BF16)
    copy = pltpu.make_async_copy(last_ref, qg_hbm.at[:, rows - EDGE :, :], sem)
    copy.start()
    total = got_ref[0].astype(F32)
    for k in range(1, got_ref.shape[0]):
        total = total + got_ref[k].astype(F32)
    total = total * scale
    for i in range(3):
        short_ref[i] = total[i * PADDED : i * PADDED + taps]
    size = total.shape[0] - 3 * PADDED
    lags = long_ref.shape[1]
    for p in range(total.shape[1] // lags):
        long_ref[p * size : (p + 1) * size] = total[3 * PADDED :, p * lags : (p + 1) * lags]
    copy.wait()


def shards(qkv, cotangent, doc_ids, short_filter, long_filter):
    _, rows, chans = qkv.shape
    groups, long_taps = long_filter.shape
    taps = short_filter.shape[2]
    devices = lax.axis_size("ctx")
    grad_scale = 1.0 / math.sqrt(rows * devices)
    packed_rows = 3 * PADDED + groups * long_taps // chans
    step_groups = LANES * groups // chans
    params = pltpu.CompilerParams(vmem_limit_bytes=24 << 20)

    ids = doc_ids.reshape(1, rows)
    sf = jnp.transpose(short_filter, (0, 2, 1))

    small = pltpu.CompilerParams(vmem_limit_bytes=8 << 20)
    edge = pl.pallas_call(
        edge_kernel,
        in_specs=[VMEM, HBM],
        out_specs=VMEM,
        out_shape=jax.ShapeDtypeStruct((3, EDGE, chans), BF16),
        scratch_shapes=[pltpu.SemaphoreType.DMA],
        compiler_params=pltpu.CompilerParams(vmem_limit_bytes=62 << 20),
        cost_estimate=pl.CostEstimate(flops=100_000, bytes_accessed=200_000, transcendentals=0),
        name="edge",
    )(ids, qkv)
    edge = passed_along(edge, 1)

    shifts = ((taps - 1) * rows, rows)
    delay, advance, lf_rev = pl.pallas_call(
        prepare_kernel,
        in_specs=[VMEM] * 2,
        out_specs=[VMEM] * 3,
        out_shape=[
            jax.ShapeDtypeStruct(shifts, BF16),
            jax.ShapeDtypeStruct(shifts, BF16),
            jax.ShapeDtypeStruct((groups, long_taps), F32),
        ],
        cost_estimate=pl.CostEstimate(flops=6_000_000_000, bytes_accessed=16_000_000, transcendentals=0),
        compiler_params=small,
        name="prepare",
    )(ids, long_filter)

    count = chans // PARTS
    sent = []
    for part in range(PARTS):
        feats, kv, grad = pl.pallas_call(
            functools.partial(feature_kernel, part * count),
            in_specs=[VMEM] * 3 + [HBM] * 3,
            out_specs=[VMEM] * 3,
            out_shape=[
                jax.ShapeDtypeStruct((3, rows, count), F32),
                jax.ShapeDtypeStruct((rows, count), BF16),
                jax.ShapeDtypeStruct((rows, count), BF16),
            ],
            scratch_shapes=[
                pltpu.VMEM(((taps - 1) * EDGE, rows), F32),
                pltpu.VMEM((3, taps, count), F32),
                pltpu.VMEM((3, rows, count), BF16),
                pltpu.VMEM((rows, count), BF16),
                pltpu.SemaphoreType.DMA((3, count // LANES)),
            ],
            compiler_params=params,
            cost_estimate=pl.CostEstimate(flops=2_000_000_000, bytes_accessed=4_000_000, transcendentals=0),
            name="features",
        )(ids, delay, edge, sf, qkv, cotangent)
        sent.append((feats, passed_along(kv, 1), passed_along(grad, -1)))

    results = []
    full = [
        jax.ShapeDtypeStruct((rows, chans), BF16),
        jax.ShapeDtypeStruct((3, rows, chans), BF16),
        jax.ShapeDtypeStruct((3, EDGE, chans), F32),
        jax.ShapeDtypeStruct((3, EDGE, chans), BF16),
        jax.ShapeDtypeStruct((chans // CHUNK, packed_rows, CHUNK), BF16),
    ]
    for part in range(PARTS):
        feats, kv_prev, grad_next = sent[part]
        filled = len(results)
        results = pl.pallas_call(
            functools.partial(mixer_kernel, part * count, filled),
            in_specs=[VMEM] * 11 + [ANY] * filled,
            out_specs=[ANY] * 5,
            out_shape=full,
            input_output_aliases={11 + k: k for k in range(filled)},
            scratch_shapes=[
                pltpu.VMEM((rows, count), BF16),
                pltpu.VMEM((3, rows, count), BF16),
                pltpu.VMEM((3, EDGE, count), F32),
                pltpu.VMEM((3, EDGE, count), BF16),
                pltpu.VMEM((count // CHUNK, packed_rows, CHUNK), BF16),
                pltpu.VMEM(((taps - 1) * EDGE, rows), BF16),
                pltpu.VMEM((2 * rows, rows), BF16),
                pltpu.VMEM((2 * rows, rows), BF16),
                pltpu.VMEM((rows, 2 * rows), F32),
                pltpu.VMEM((2 * rows, LANES), BF16),
                pltpu.VMEM((2 * rows, LANES), BF16),
                pltpu.VMEM((rows, LANES), BF16),
                pltpu.VMEM((step_groups, long_taps), F32),
                pltpu.VMEM((LANES, 2 * rows), BF16),
                pltpu.VMEM((LANES, 2 * rows), BF16),
                pltpu.VMEM((LANES, rows), F32),
                pltpu.VMEM((LANES, rows), F32),
                pltpu.SemaphoreType.DMA((5, count // LANES)),
            ],
            compiler_params=params,
            cost_estimate=pl.CostEstimate(flops=8_000_000_000, bytes_accessed=8_000_000, transcendentals=0),
            name="mixer",
        )(ids, sf, long_filter, lf_rev, advance, qkv, cotangent, edge, feats, kv_prev, grad_next, *results)
    out, qg, tail, part, packed = results

    part = passed_along(part, -1)
    per = chans // devices
    if per == CHUNK:
        got = lax.all_to_all(packed, "ctx", 0, 0)
        qg, long_grad, short_grad = pl.pallas_call(
            functools.partial(finish_kernel, grad_scale, taps),
            in_specs=[VMEM, VMEM, VMEM, ANY],
            out_specs=[ANY, VMEM, VMEM],
            out_shape=[
                jax.ShapeDtypeStruct(qg.shape, BF16),
                jax.ShapeDtypeStruct((groups // devices, long_taps), F32),
                jax.ShapeDtypeStruct((3, taps, per), F32),
            ],
            input_output_aliases={3: 0},
            scratch_shapes=[pltpu.VMEM((3, EDGE, chans), BF16), pltpu.SemaphoreType.DMA],
            compiler_params=small,
            cost_estimate=pl.CostEstimate(flops=1_000_000, bytes_accessed=200_000, transcendentals=0),
            name="finish",
        )(got, tail, part, qg)
        return (out, qg, long_grad, short_grad.transpose(0, 2, 1))
    qg = lax.dynamic_update_slice(qg, (tail + part.astype(F32)).astype(BF16), (0, rows - EDGE, 0))
    head = 3 * PADDED
    short_part = packed[:, :head].transpose(1, 0, 2).reshape(head, devices, per)
    long_part = packed[:, head:].reshape(-1, packed_rows - head, CHUNK // long_taps, long_taps)
    long_part = long_part.transpose(0, 2, 1, 3).reshape(devices, -1, per)
    got = jnp.concatenate([short_part.transpose(1, 0, 2), long_part], 1)
    got = lax.all_to_all(got, "ctx", 0, 0)
    total = jnp.sum(got.astype(F32), 0) * grad_scale
    short_grad = total[:head].reshape(3, PADDED, per)[:, :taps].transpose(0, 2, 1)
    long_grad = total[head:].reshape(groups // devices, long_taps)
    return (out, qg, long_grad, short_grad)


def solution(mesh):
    in_specs = (P(None, "ctx", "tp"), P("ctx", "tp"), P("ctx"), P(None, "tp", None), P("tp", None))
    out_specs = (
        P("ctx", "tp"),
        P(None, "ctx", "tp"),
        P(("tp", "ctx"), None),
        P(None, ("tp", "ctx"), None),
    )
    return jax.shard_map(shards, mesh=mesh, in_specs=in_specs, out_specs=out_specs, check_vma=False)
```

```python
import functools
import math

import jax
import jax.numpy as jnp
from jax import lax
from jax.experimental import pallas as pl
from jax.experimental.pallas import tpu as pltpu
from jax.sharding import PartitionSpec as P

F32 = jnp.float32
BF16 = jnp.bfloat16
EDGE = 8
LANES = 512
CHUNK = 256
PADDED = 8
PARTS = 2

VMEM = pl.BlockSpec(memory_space=pltpu.VMEM)
ANY = pl.BlockSpec(memory_space=pl.ANY)
HBM = pl.BlockSpec(memory_space=pltpu.HBM)


def passed_along(block, distance):
    devices = range(lax.axis_size("ctx"))
    route = [(i - distance, i) for i in devices if i - distance in devices]
    return lax.ppermute(block, "ctx", route)


def iota2(shape, dim):
    return lax.broadcasted_iota(jnp.int32, shape, dim)


def dot(a, b):
    return jnp.dot(a, b, preferred_element_type=F32)


def lane_range(start, size):
    return pl.ds(pl.multiple_of(start, size), size)


def ones_where(cond):
    return jnp.where(cond, 1.0, 0.0)


def prepare_kernel(ids_ref, lf_ref, delay_ref, advance_ref, lfr_ref):
    rows = delay_ref.shape[1]
    taps = delay_ref.shape[0] // rows + 1
    id_row = jnp.broadcast_to(ids_ref[...], (rows, rows)).astype(F32)
    same = id_row == id_row.T
    lag = iota2((rows, rows), 0) - iota2((rows, rows), 1)
    for t in range(1, taps):
        delay_ref[(t - 1) * rows : t * rows] = ones_where((lag == t) & same).astype(BF16)
        advance_ref[(t - 1) * rows : t * rows] = ones_where((lag == -t) & same).astype(BF16)
    backward = ones_where((iota2((rows, rows), 0) + iota2((rows, rows), 1)) % rows == 0)
    lfr_ref[...] = dot(lf_ref[...].astype(BF16), backward.astype(BF16))


def feature_kernel(first, ids_ref, delay_ref, edge_ref, sf_hbm, x_hbm, cot_hbm,
                   feat_ref, kv_ref, g_ref, edge_shift, sf_ref, x_ref, cot_ref, sems):
    rows = x_ref.shape[1]
    taps = sf_ref.shape[1]
    steps = kv_ref.shape[1] // LANES

    def loads(p):
        near = lane_range(p * LANES, LANES)
        cols = lane_range(first + p * LANES, LANES)
        pairs = [
            (sf_hbm.at[:, :, cols], sf_ref.at[:, :, near]),
            (x_hbm.at[:, :, cols], x_ref.at[:, :, near]),
            (cot_hbm.at[:, cols], cot_ref.at[:, near]),
        ]
        return [pltpu.make_async_copy(src, dst, sems.at[k, p]) for k, (src, dst) in enumerate(pairs)]

    for p in range(steps):
        for copy in loads(p):
            copy.start()
    id_row = jnp.broadcast_to(ids_ref[...], (rows, rows)).astype(F32)
    head_ids = id_row.T[0:EDGE]
    before = jnp.broadcast_to(edge_ref[0, 0:1, 0:rows].astype(F32), (EDGE, rows))
    before = pltpu.roll(before, EDGE, 1)
    lag = iota2((EDGE, rows), 0) + EDGE - iota2((EDGE, rows), 1)
    for t in range(1, taps):
        edge_shift[(t - 1) * EDGE : t * EDGE] = ones_where((lag == t) & (before == head_ids))
    id_wide = jnp.concatenate([ids_ref[...].astype(F32)] * (LANES // rows), 1)

    def one_step(p, carry):
        near = lane_range(p * LANES, LANES)
        cols = lane_range(first + p * LANES, LANES)
        for copy in loads(p):
            copy.wait()
        feats = []
        for i in range(3):
            x = x_ref[i, :, near]
            w = sf_ref[i, :, near]
            moved = dot(delay_ref[...], x)
            acc = w[0:1] * x.astype(F32)
            for t in range(1, taps):
                acc = acc + w[t : t + 1] * moved[(t - 1) * rows : t * rows]
            edge = edge_ref[i, :, cols].astype(F32)
            edge = jnp.concatenate([edge, jnp.zeros((rows - EDGE, LANES), F32)], 0)
            moved = dot(edge_shift[...].astype(BF16), edge.astype(BF16))
            fix = w[1:2] * moved[0:EDGE]
            for t in range(2, taps):
                fix = fix + w[t : t + 1] * moved[(t - 1) * EDGE : t * EDGE]
            acc = jnp.concatenate([acc[0:EDGE] + fix, acc[EDGE:]], 0)
            feat_ref[i, :, near] = acc
            feats.append(acc)
        kv_ref[:, near] = (feats[1] * feats[2]).astype(BF16)
        g = cot_ref[:, near].astype(F32) * feats[0]
        last = iota2(g.shape, 0) == rows - 1
        g_ref[:, near] = jnp.where(last, jnp.broadcast_to(id_wide, g.shape), g).astype(BF16)
        return carry

    lax.fori_loop(0, steps, one_step, 0)


def store_all(copies, steps):
    def drain(p, carry):
        for copy in copies(p):
            copy.wait()
        return carry

    lax.fori_loop(0, steps, drain, 0)


def edge_shifts(ids_ref, edge_ref, edge_shift):
    rows = edge_shift.shape[1]
    taps = edge_shift.shape[0] // EDGE + 1
    id_head = jnp.broadcast_to(ids_ref[...], (EDGE, rows)).astype(F32)
    prev = jnp.broadcast_to(edge_ref[0, 0:1, 0:rows].astype(F32), (rows, rows)).T
    lag = iota2((EDGE, rows), 1) + EDGE - iota2((EDGE, rows), 0)
    same = prev[rows - EDGE :] == id_head
    pieces = [ones_where((lag == t) & same) for t in range(1, taps)]
    edge_shift[...] = jnp.concatenate(pieces, 0).astype(BF16)


def short_stage(gf, w, x, xe, advance_ref, edge_shift):
    rows = gf.shape[0]
    taps = w.shape[0]
    gf_sent = gf.astype(BF16)
    moved = dot(advance_ref[...], gf_sent)
    moved_edge = dot(edge_shift[...], gf_sent)
    acc = w[0:1] * gf
    sums = [jnp.sum(x * gf, 0, keepdims=True)]
    sent = jnp.zeros((EDGE, LANES), F32)
    for t in range(1, taps):
        piece = moved[(t - 1) * rows : t * rows]
        piece_edge = moved_edge[(t - 1) * EDGE : t * EDGE]
        acc = acc + w[t : t + 1] * piece
        sent = sent + w[t : t + 1] * piece_edge
        sums.append(jnp.sum(x * piece, 0, keepdims=True) + jnp.sum(xe * piece_edge, 0, keepdims=True))
    sums.append(jnp.zeros((PADDED - taps, LANES), F32))
    return acc, sent, jnp.concatenate(sums, 0)


def query_kernel(first, filled, ids_ref, sf_ref, lf_ref, advance_ref, x_ref, cot_ref, edge_ref,
                 feat_ref, kvp_ref, *refs):
    (out_hbm, qg_hbm, tail_hbm, part_hbm, packed_hbm, out_ref, qg_ref, tail_ref, part_ref, short_ref, long_ref,
     edge_shift, mask_y, mask_a, w_kv, g_rev, dh_ref, kv_turned, y_turned, sems) = refs[filled:]
    rows = x_ref.shape[1]
    count = kvp_ref.shape[1]
    width = x_ref.shape[2] // lf_ref.shape[0]
    half = rows
    per = half // width
    lag = iota2((rows, rows), 0) - iota2((rows, rows), 1)
    mirror = ones_where(iota2((rows, rows), 0) + iota2((rows, rows), 1) == rows - 1).astype(BF16)
    id_row = jnp.broadcast_to(ids_ref[...], (rows, rows)).astype(F32)
    id_col = id_row.T
    prev_row = jnp.broadcast_to(edge_ref[0, 0:1, 0:rows].astype(F32), (rows, rows))
    same = id_row == id_col
    mask_y[0:rows] = ones_where((lag <= 0) & same).astype(BF16)
    mask_y[rows:] = ones_where((lag > 0) & (prev_row.T == id_row)).astype(BF16)
    mask_a[:, 0:rows] = dot(mirror, ones_where((lag >= 0) & same).astype(BF16))
    mask_a[:, rows:] = dot(mirror, ones_where((lag < 0) & (prev_row == id_col)).astype(BF16))
    edge_shifts(ids_ref, edge_ref, edge_shift)
    owner = iota2((rows, half), 1) // width
    blocks = LANES // CHUNK
    head = 3 * PADDED

    def copies(p):
        near = lane_range(p * LANES, LANES)
        cols = lane_range(first + p * LANES, LANES)
        here = pl.ds(p * blocks, blocks)
        there = pl.ds(first // CHUNK + p * blocks, blocks)
        pairs = [
            (out_ref.at[:, near], out_hbm.at[:, cols]),
            (qg_ref.at[:, near], qg_hbm.at[0, :, cols]),
            (tail_ref.at[:, near], tail_hbm.at[0, :, cols]),
            (part_ref.at[:, near], part_hbm.at[0, :, cols]),
            (short_ref.at[here], packed_hbm.at[there, 0:PADDED]),
            (long_ref.at[here], packed_hbm.at[there, head:]),
        ]
        return [pltpu.make_async_copy(src, dst, sems.at[k, p]) for k, (src, dst) in enumerate(pairs)]

    def one_step(p, carry):
        near = lane_range(p * LANES, LANES)
        cols = lane_range(first + p * LANES, LANES)
        cot = cot_ref[:, cols].astype(F32)
        w_kv[0:rows] = (feat_ref[1, :, near] * feat_ref[2, :, near]).astype(BF16)
        w_kv[rows:] = kvp_ref[:, near]
        kv_turned[...] = w_kv[...].T
        g_rev[...] = dot(mirror, (cot * feat_ref[0, :, near]).astype(BF16)).astype(BF16)
        for q in range(LANES // half):
            part = slice(q * half, (q + 1) * half)
            base = pl.multiple_of((first // half) * per + p * (LANES // width) + q * per, per)
            for j in range(per):
                mine = slice((q * per + j) * width, (q * per + j + 1) * width)
                taps = jnp.broadcast_to(lf_ref[pl.ds(base + j, 1), :], (rows, rows))
                taps = pltpu.roll(taps, 0, 1, stride=1, stride_axis=0).astype(BF16)
                toeplitz = jnp.concatenate([taps, taps], 0) * mask_y[...]
                y_turned[mine] = dot(kv_turned[mine], toeplitz)
                g_sel = jnp.where(owner == j, g_rev[:, part], jnp.zeros((rows, half), BF16))
                cross = lax.dot_general(
                    g_sel, w_kv[:, part], (((1,), (1,)), ((), ())), preferred_element_type=F32
                ) * mask_a[...]
                folded = cross[:, 0:rows] + cross[:, rows:]
                folded = pltpu.roll(folded, 0, 1, stride=1, stride_axis=0)
                dh_ref[q * per + j : q * per + j + 1] = jnp.sum(folded, 0, keepdims=True)
        dh = dot(dh_ref[...].astype(BF16), mirror)
        y = y_turned[...].T
        out_ref[:, near] = (feat_ref[0, :, near] * y).astype(BF16)
        acc, sent, sums = short_stage(
            cot * y, sf_ref[0, :, cols], x_ref[0, :, cols].astype(F32), edge_ref[0, :, cols].astype(F32),
            advance_ref, edge_shift,
        )
        qg_ref[:, near] = acc.astype(BF16)
        tail_ref[:, near] = acc[rows - EDGE :]
        part_ref[:, near] = sent.astype(BF16)
        size = dh.shape[0] * rows // LANES
        for k in range(blocks):
            short_ref[p * blocks + k] = sums[:, k * CHUNK : (k + 1) * CHUNK].astype(BF16)
            lines = range(k * (CHUNK // rows), (k + 1) * (CHUNK // rows))
            long_ref[p * blocks + k] = jnp.concatenate([dh[e * size : (e + 1) * size] for e in lines], 1).astype(BF16)
        for copy in copies(p):
            copy.start()
        return carry

    lax.fori_loop(0, count // LANES, one_step, 0)
    store_all(copies, count // LANES)


def pair_kernel(first, filled, ids_ref, sf_ref, lfr_ref, advance_ref, x_ref, cot_ref, edge_ref,
                feat_ref, gn_ref, *refs):
    (qg_hbm, tail_hbm, part_hbm, packed_hbm, qg_ref, tail_ref, part_ref, short_ref,
     edge_shift, mask_g, w_g, g_turned, gm_turned, sems) = refs[filled:]
    rows = x_ref.shape[1]
    count = gn_ref.shape[1]
    width = x_ref.shape[2] // lfr_ref.shape[0]
    lag = iota2((rows, rows), 0) - iota2((rows, rows), 1)
    id_row = jnp.broadcast_to(ids_ref[...], (rows, rows)).astype(F32)
    next_col = jnp.broadcast_to(gn_ref[rows - 1 : rows, 0:rows].astype(F32), (rows, rows)).T
    mask_g[0:rows] = ones_where((lag >= 0) & (id_row == id_row.T)).astype(BF16)
    mask_g[rows:] = ones_where((lag < 0) & (next_col == id_row)).astype(BF16)
    edge_shifts(ids_ref, edge_ref, edge_shift)
    blocks = LANES // CHUNK

    def copies(p):
        near = lane_range(p * LANES, LANES)
        cols = lane_range(first + p * LANES, LANES)
        pairs = [
            (qg_ref.at[:, :, near], qg_hbm.at[1:3, :, cols]),
            (tail_ref.at[:, :, near], tail_hbm.at[1:3, :, cols]),
            (part_ref.at[:, :, near], part_hbm.at[1:3, :, cols]),
            (
                short_ref.at[pl.ds(p * blocks, blocks)],
                packed_hbm.at[pl.ds(first // CHUNK + p * blocks, blocks), PADDED : 3 * PADDED],
            ),
        ]
        return [pltpu.make_async_copy(src, dst, sems.at[k, p]) for k, (src, dst) in enumerate(pairs)]

    def one_step(p, carry):
        near = lane_range(p * LANES, LANES)
        cols = lane_range(first + p * LANES, LANES)
        w_g[0:rows] = (cot_ref[:, cols].astype(F32) * feat_ref[0, :, near]).astype(BF16)
        w_g[rows:] = gn_ref[:, near]
        g_turned[...] = w_g[...].T
        for j in range(LANES // width):
            mine = slice(j * width, (j + 1) * width)
            base = pl.multiple_of(first // width + p * (LANES // width), LANES // width)
            taps = jnp.broadcast_to(lfr_ref[pl.ds(base + j, 1), :], (rows, rows))
            taps = pltpu.roll(taps, 0, 1, stride=1, stride_axis=0).astype(BF16)
            toeplitz = jnp.concatenate([taps, taps], 0) * mask_g[...]
            gm_turned[mine] = dot(g_turned[mine], toeplitz)
        gm = gm_turned[...].T
        heads = []
        for i in (1, 2):
            acc, sent, sums = short_stage(
                gm * feat_ref[3 - i, :, near], sf_ref[i, :, cols], x_ref[i, :, cols].astype(F32),
                edge_ref[i, :, cols].astype(F32), advance_ref, edge_shift,
            )
            qg_ref[i - 1, :, near] = acc.astype(BF16)
            tail_ref[i - 1, :, near] = acc[rows - EDGE :]
            part_ref[i - 1, :, near] = sent.astype(BF16)
            heads.append(sums)
        for k in range(blocks):
            picked = [head[:, k * CHUNK : (k + 1) * CHUNK] for head in heads]
            short_ref[p * blocks + k] = jnp.concatenate(picked, 0).astype(BF16)
        for copy in copies(p):
            copy.start()
        return carry

    lax.fori_loop(0, count // LANES, one_step, 0)
    store_all(copies, count // LANES)


def finish_kernel(scale, taps, got_ref, tail_ref, part_ref, qg_in, qg_hbm, long_ref, short_ref, last_ref, sem):
    rows = qg_hbm.shape[1]
    last_ref[...] = (tail_ref[...] + part_ref[...].astype(F32)).astype(BF16)
    copy = pltpu.make_async_copy(last_ref, qg_hbm.at[:, rows - EDGE :, :], sem)
    copy.start()
    total = got_ref[0].astype(F32)
    for k in range(1, got_ref.shape[0]):
        total = total + got_ref[k].astype(F32)
    total = total * scale
    for i in range(3):
        short_ref[i] = total[i * PADDED : i * PADDED + taps]
    size = total.shape[0] - 3 * PADDED
    lags = long_ref.shape[1]
    for p in range(total.shape[1] // lags):
        long_ref[p * size : (p + 1) * size] = total[3 * PADDED :, p * lags : (p + 1) * lags]
    copy.wait()


def shards(qkv, cotangent, doc_ids, short_filter, long_filter):
    _, rows, chans = qkv.shape
    groups, long_taps = long_filter.shape
    taps = short_filter.shape[2]
    devices = lax.axis_size("ctx")
    grad_scale = 1.0 / math.sqrt(rows * devices)
    packed_rows = 3 * PADDED + groups * long_taps // chans
    step_groups = LANES * groups // chans
    params = pltpu.CompilerParams(vmem_limit_bytes=24 << 20)

    ids = doc_ids.reshape(1, rows)
    sf = jnp.transpose(short_filter, (0, 2, 1))

    small = pltpu.CompilerParams(vmem_limit_bytes=8 << 20)
    edge = qkv[:, rows - EDGE :, :]
    edge = edge.at[0, 0, :rows].set(doc_ids.astype(BF16))
    edge = passed_along(edge, 1)

    shifts = ((taps - 1) * rows, rows)
    delay, advance, lf_rev = pl.pallas_call(
        prepare_kernel,
        in_specs=[VMEM] * 2,
        out_specs=[VMEM] * 3,
        out_shape=[
            jax.ShapeDtypeStruct(shifts, BF16),
            jax.ShapeDtypeStruct(shifts, BF16),
            jax.ShapeDtypeStruct((groups, long_taps), F32),
        ],
        cost_estimate=pl.CostEstimate(flops=6_000_000_000, bytes_accessed=16_000_000, transcendentals=0),
        compiler_params=small,
        name="prepare",
    )(ids, long_filter)

    count = chans // PARTS
    sent = []
    for part in range(PARTS):
        feats, kv, grad = pl.pallas_call(
            functools.partial(feature_kernel, part * count),
            in_specs=[VMEM] * 3 + [HBM] * 3,
            out_specs=[VMEM] * 3,
            out_shape=[
                jax.ShapeDtypeStruct((3, rows, count), F32),
                jax.ShapeDtypeStruct((rows, count), BF16),
                jax.ShapeDtypeStruct((rows, count), BF16),
            ],
            scratch_shapes=[
                pltpu.VMEM(((taps - 1) * EDGE, rows), F32),
                pltpu.VMEM((3, taps, count), F32),
                pltpu.VMEM((3, rows, count), BF16),
                pltpu.VMEM((rows, count), BF16),
                pltpu.SemaphoreType.DMA((3, count // LANES)),
            ],
            compiler_params=params,
            cost_estimate=pl.CostEstimate(flops=2_000_000_000, bytes_accessed=4_000_000, transcendentals=0),
            name="features",
        )(ids, delay, edge, sf, qkv, cotangent)
        sent.append((feats, passed_along(kv, 1), passed_along(grad, -1)))

    full = [
        jax.ShapeDtypeStruct((rows, chans), BF16),
        jax.ShapeDtypeStruct((3, rows, chans), BF16),
        jax.ShapeDtypeStruct((3, EDGE, chans), F32),
        jax.ShapeDtypeStruct((3, EDGE, chans), BF16),
        jax.ShapeDtypeStruct((chans // CHUNK, packed_rows, CHUNK), BF16),
    ]
    edge_scratch = pltpu.VMEM(((taps - 1) * EDGE, rows), BF16)
    results = []
    for part in range(PARTS):
        feats, kv_prev, grad_next = sent[part]
        filled = len(results)
        out, *rest = pl.pallas_call(
            functools.partial(query_kernel, part * count, filled),
            in_specs=[VMEM] * 9 + [ANY] * filled,
            out_specs=[ANY] * 5,
            out_shape=full,
            input_output_aliases={9 + k: k for k in range(filled)},
            scratch_shapes=[
                pltpu.VMEM((rows, count), BF16),
                pltpu.VMEM((rows, count), BF16),
                pltpu.VMEM((EDGE, count), F32),
                pltpu.VMEM((EDGE, count), BF16),
                pltpu.VMEM((count // CHUNK, PADDED, CHUNK), BF16),
                pltpu.VMEM((count // CHUNK, packed_rows - 3 * PADDED, CHUNK), BF16),
                edge_scratch,
                pltpu.VMEM((2 * rows, rows), BF16),
                pltpu.VMEM((rows, 2 * rows), F32),
                pltpu.VMEM((2 * rows, LANES), BF16),
                pltpu.VMEM((rows, LANES), BF16),
                pltpu.VMEM((step_groups, long_taps), F32),
                pltpu.VMEM((LANES, 2 * rows), BF16),
                pltpu.VMEM((LANES, rows), F32),
                pltpu.SemaphoreType.DMA((6, count // LANES)),
            ],
            compiler_params=params,
            cost_estimate=pl.CostEstimate(flops=4_000_000_000, bytes_accessed=4_000_000, transcendentals=0),
            name="query",
        )(ids, sf, long_filter, advance, qkv, cotangent, edge, feats, kv_prev, *results)
        rest = pl.pallas_call(
            functools.partial(pair_kernel, part * count, 4),
            in_specs=[VMEM] * 9 + [ANY] * 4,
            out_specs=[ANY] * 4,
            out_shape=full[1:],
            input_output_aliases={9 + k: k for k in range(4)},
            scratch_shapes=[
                pltpu.VMEM((2, rows, count), BF16),
                pltpu.VMEM((2, EDGE, count), F32),
                pltpu.VMEM((2, EDGE, count), BF16),
                pltpu.VMEM((count // CHUNK, 2 * PADDED, CHUNK), BF16),
                edge_scratch,
                pltpu.VMEM((2 * rows, rows), BF16),
                pltpu.VMEM((2 * rows, LANES), BF16),
                pltpu.VMEM((LANES, 2 * rows), BF16),
                pltpu.VMEM((LANES, rows), F32),
                pltpu.SemaphoreType.DMA((4, count // LANES)),
            ],
            compiler_params=params,
            cost_estimate=pl.CostEstimate(flops=4_000_000_000, bytes_accessed=4_000_000, transcendentals=0),
            name="pair",
        )(ids, sf, lf_rev, advance, qkv, cotangent, edge, feats, grad_next, *rest)
        results = [out, *rest]
    out, qg, tail, part, packed = results

    part = passed_along(part, -1)
    per = chans // devices
    if per == CHUNK:
        got = lax.all_to_all(packed, "ctx", 0, 0)
        qg, long_grad, short_grad = pl.pallas_call(
            functools.partial(finish_kernel, grad_scale, taps),
            in_specs=[VMEM, VMEM, VMEM, ANY],
            out_specs=[ANY, VMEM, VMEM],
            out_shape=[
                jax.ShapeDtypeStruct(qg.shape, BF16),
                jax.ShapeDtypeStruct((groups // devices, long_taps), F32),
                jax.ShapeDtypeStruct((3, taps, per), F32),
            ],
            input_output_aliases={3: 0},
            scratch_shapes=[pltpu.VMEM((3, EDGE, chans), BF16), pltpu.SemaphoreType.DMA],
            compiler_params=small,
            cost_estimate=pl.CostEstimate(flops=1_000_000, bytes_accessed=200_000, transcendentals=0),
            name="finish",
        )(got, tail, part, qg)
        return (out, qg, long_grad, short_grad.transpose(0, 2, 1))
    qg = lax.dynamic_update_slice(qg, (tail + part.astype(F32)).astype(BF16), (0, rows - EDGE, 0))
    head = 3 * PADDED
    short_part = packed[:, :head].transpose(1, 0, 2).reshape(head, devices, per)
    long_part = packed[:, head:].reshape(-1, packed_rows - head, CHUNK // long_taps, long_taps)
    long_part = long_part.transpose(0, 2, 1, 3).reshape(devices, -1, per)
    got = jnp.concatenate([short_part.transpose(1, 0, 2), long_part], 1)
    got = lax.all_to_all(got, "ctx", 0, 0)
    total = jnp.sum(got.astype(F32), 0) * grad_scale
    short_grad = total[:head].reshape(3, PADDED, per)[:, :taps].transpose(0, 2, 1)
    long_grad = total[head:].reshape(groups // devices, long_taps)
    return (out, qg, long_grad, short_grad)


def solution(mesh):
    in_specs = (P(None, "ctx", "tp"), P("ctx", "tp"), P("ctx"), P(None, "tp", None), P("tp", None))
    out_specs = (
        P("ctx", "tp"),
        P(None, "ctx", "tp"),
        P(("tp", "ctx"), None),
        P(None, ("tp", "ctx"), None),
    )
    return jax.shard_map(shards, mesh=mesh, in_specs=in_specs, out_specs=out_specs, check_vma=False)
```

```python
import functools
import math

import jax
import jax.numpy as jnp
from jax import lax
from jax.experimental import pallas as pl
from jax.experimental.pallas import tpu as pltpu
from jax.sharding import PartitionSpec as P

F32 = jnp.float32
BF16 = jnp.bfloat16
EDGE = 8
LANES = 512
CHUNK = 256
PADDED = 8
PARTS = 2

VMEM = pl.BlockSpec(memory_space=pltpu.VMEM)
ANY = pl.BlockSpec(memory_space=pl.ANY)
HBM = pl.BlockSpec(memory_space=pltpu.HBM)


def passed_along(block, distance):
    devices = range(lax.axis_size("ctx"))
    route = [(i - distance, i) for i in devices if i - distance in devices]
    return lax.ppermute(block, "ctx", route)


def iota2(shape, dim):
    return lax.broadcasted_iota(jnp.int32, shape, dim)


def dot(a, b):
    return jnp.dot(a, b, preferred_element_type=F32)


def lane_range(start, size):
    return pl.ds(pl.multiple_of(start, size), size)


def ones_where(cond):
    return jnp.where(cond, 1.0, 0.0)


def prepare_kernel(ids_ref, lf_ref, delay_ref, advance_ref, lfr_ref):
    rows = delay_ref.shape[1]
    taps = delay_ref.shape[0] // rows + 1
    id_row = jnp.broadcast_to(ids_ref[...], (rows, rows)).astype(F32)
    same = id_row == id_row.T
    lag = iota2((rows, rows), 0) - iota2((rows, rows), 1)
    for t in range(1, taps):
        delay_ref[(t - 1) * rows : t * rows] = ones_where((lag == t) & same).astype(BF16)
        advance_ref[(t - 1) * rows : t * rows] = ones_where((lag == -t) & same).astype(BF16)
    backward = ones_where((iota2((rows, rows), 0) + iota2((rows, rows), 1)) % rows == 0)
    lfr_ref[...] = dot(lf_ref[...].astype(BF16), backward.astype(BF16))


def feature_kernel(first, ids_ref, delay_ref, edge_ref, sf_hbm, x_hbm, cot_hbm,
                   feat_ref, kv_ref, g_ref, edge_shift, sf_ref, x_ref, cot_ref, sems):
    rows = x_ref.shape[1]
    taps = sf_ref.shape[1]
    steps = kv_ref.shape[1] // LANES

    def loads(p):
        near = lane_range(p * LANES, LANES)
        cols = lane_range(first + p * LANES, LANES)
        pairs = [
            (sf_hbm.at[:, :, cols], sf_ref.at[:, :, near]),
            (x_hbm.at[:, :, cols], x_ref.at[:, :, near]),
            (cot_hbm.at[:, cols], cot_ref.at[:, near]),
        ]
        return [pltpu.make_async_copy(src, dst, sems.at[k, p]) for k, (src, dst) in enumerate(pairs)]

    for p in range(steps):
        for copy in loads(p):
            copy.start()
    id_row = jnp.broadcast_to(ids_ref[...], (rows, rows)).astype(F32)
    head_ids = id_row.T[0:EDGE]
    before = jnp.broadcast_to(edge_ref[0, 0:1, 0:rows].astype(F32), (EDGE, rows))
    before = pltpu.roll(before, EDGE, 1)
    lag = iota2((EDGE, rows), 0) + EDGE - iota2((EDGE, rows), 1)
    for t in range(1, taps):
        edge_shift[(t - 1) * EDGE : t * EDGE] = ones_where((lag == t) & (before == head_ids))
    id_wide = jnp.concatenate([ids_ref[...].astype(F32)] * (LANES // rows), 1)

    def one_step(p, carry):
        near = lane_range(p * LANES, LANES)
        cols = lane_range(first + p * LANES, LANES)
        for copy in loads(p):
            copy.wait()
        feats = []
        for i in range(3):
            x = x_ref[i, :, near]
            w = sf_ref[i, :, near]
            moved = dot(delay_ref[...], x)
            acc = w[0:1] * x.astype(F32)
            for t in range(1, taps):
                acc = acc + w[t : t + 1] * moved[(t - 1) * rows : t * rows]
            edge = edge_ref[i, :, cols].astype(F32)
            edge = jnp.concatenate([edge, jnp.zeros((rows - EDGE, LANES), F32)], 0)
            moved = dot(edge_shift[...].astype(BF16), edge.astype(BF16))
            fix = w[1:2] * moved[0:EDGE]
            for t in range(2, taps):
                fix = fix + w[t : t + 1] * moved[(t - 1) * EDGE : t * EDGE]
            acc = jnp.concatenate([acc[0:EDGE] + fix, acc[EDGE:]], 0)
            feat_ref[i, :, near] = acc
            feats.append(acc)
        kv_ref[:, near] = (feats[1] * feats[2]).astype(BF16)
        g = cot_ref[:, near].astype(F32) * feats[0]
        last = iota2(g.shape, 0) == rows - 1
        g_ref[:, near] = jnp.where(last, jnp.broadcast_to(id_wide, g.shape), g).astype(BF16)
        return carry

    lax.fori_loop(0, steps, one_step, 0)


def run_steps(parts, steps):
    def start(p, carry):
        for one_step, copies in parts:
            one_step(p)
            for copy in copies(p):
                copy.start()
        return carry

    def drain(p, carry):
        for _, copies in parts:
            for copy in copies(p):
                copy.wait()
        return carry

    lax.fori_loop(0, steps, start, 0)
    lax.fori_loop(0, steps, drain, 0)


def edge_shifts(ids_ref, edge_ref, edge_shift):
    rows = edge_shift.shape[1]
    taps = edge_shift.shape[0] // EDGE + 1
    id_head = jnp.broadcast_to(ids_ref[...], (EDGE, rows)).astype(F32)
    prev = jnp.broadcast_to(edge_ref[0, 0:1, 0:rows].astype(F32), (rows, rows)).T
    lag = iota2((EDGE, rows), 1) + EDGE - iota2((EDGE, rows), 0)
    same = prev[rows - EDGE :] == id_head
    pieces = [ones_where((lag == t) & same) for t in range(1, taps)]
    edge_shift[...] = jnp.concatenate(pieces, 0).astype(BF16)


def short_stage(gf, w, x, xe, advance_ref, edge_shift):
    rows = gf.shape[0]
    taps = w.shape[0]
    gf_sent = gf.astype(BF16)
    moved = dot(advance_ref[...], gf_sent)
    moved_edge = dot(edge_shift[...], gf_sent)
    acc = w[0:1] * gf
    sums = [jnp.sum(x * gf, 0, keepdims=True)]
    sent = jnp.zeros((EDGE, LANES), F32)
    for t in range(1, taps):
        piece = moved[(t - 1) * rows : t * rows]
        piece_edge = moved_edge[(t - 1) * EDGE : t * EDGE]
        acc = acc + w[t : t + 1] * piece
        sent = sent + w[t : t + 1] * piece_edge
        sums.append(jnp.sum(x * piece, 0, keepdims=True) + jnp.sum(xe * piece_edge, 0, keepdims=True))
    sums.append(jnp.zeros((PADDED - taps, LANES), F32))
    return acc, sent, jnp.concatenate(sums, 0)


def query_part(first, shared, lf_ref, feat_ref, kvp_ref, outs, scratch):
    ids_ref, sf_ref, advance_ref, x_ref, cot_ref, edge_ref = shared
    out_hbm, qg_hbm, tail_hbm, part_hbm, packed_hbm = outs
    (out_ref, qg_ref, tail_ref, part_ref, short_ref, long_ref,
     edge_shift, mask_y, mask_a, w_kv, g_rev, dh_ref, kv_turned, y_turned, sems) = scratch
    rows = x_ref.shape[1]
    width = x_ref.shape[2] // lf_ref.shape[0]
    half = rows
    per = half // width
    lag = iota2((rows, rows), 0) - iota2((rows, rows), 1)
    mirror = ones_where(iota2((rows, rows), 0) + iota2((rows, rows), 1) == rows - 1).astype(BF16)
    id_row = jnp.broadcast_to(ids_ref[...], (rows, rows)).astype(F32)
    id_col = id_row.T
    prev_row = jnp.broadcast_to(edge_ref[0, 0:1, 0:rows].astype(F32), (rows, rows))
    same = id_row == id_col
    mask_y[0:rows] = ones_where((lag <= 0) & same).astype(BF16)
    mask_y[rows:] = ones_where((lag > 0) & (prev_row.T == id_row)).astype(BF16)
    mask_a[:, 0:rows] = dot(mirror, ones_where((lag >= 0) & same).astype(BF16))
    mask_a[:, rows:] = dot(mirror, ones_where((lag < 0) & (prev_row == id_col)).astype(BF16))
    edge_shifts(ids_ref, edge_ref, edge_shift)
    owner = iota2((rows, half), 1) // width
    blocks = LANES // CHUNK
    head = 3 * PADDED

    def copies(p):
        near = lane_range(p * LANES, LANES)
        cols = lane_range(first + p * LANES, LANES)
        here = pl.ds(p * blocks, blocks)
        there = pl.ds(first // CHUNK + p * blocks, blocks)
        pairs = [
            (out_ref.at[:, near], out_hbm.at[:, cols]),
            (qg_ref.at[:, near], qg_hbm.at[0, :, cols]),
            (tail_ref.at[:, near], tail_hbm.at[0, :, cols]),
            (part_ref.at[:, near], part_hbm.at[0, :, cols]),
            (short_ref.at[here], packed_hbm.at[there, 0:PADDED]),
            (long_ref.at[here], packed_hbm.at[there, head:]),
        ]
        return [pltpu.make_async_copy(src, dst, sems.at[k, p]) for k, (src, dst) in enumerate(pairs)]

    def one_step(p):
        near = lane_range(p * LANES, LANES)
        cols = lane_range(first + p * LANES, LANES)
        cot = cot_ref[:, cols].astype(F32)
        w_kv[0:rows] = (feat_ref[1, :, near] * feat_ref[2, :, near]).astype(BF16)
        w_kv[rows:] = kvp_ref[:, near]
        kv_turned[...] = w_kv[...].T
        g_rev[...] = dot(mirror, (cot * feat_ref[0, :, near]).astype(BF16)).astype(BF16)
        for q in range(LANES // half):
            part = slice(q * half, (q + 1) * half)
            base = pl.multiple_of((first // half) * per + p * (LANES // width) + q * per, per)
            for j in range(per):
                mine = slice((q * per + j) * width, (q * per + j + 1) * width)
                taps = jnp.broadcast_to(lf_ref[pl.ds(base + j, 1), :], (rows, rows))
                taps = pltpu.roll(taps, 0, 1, stride=1, stride_axis=0).astype(BF16)
                toeplitz = jnp.concatenate([taps, taps], 0) * mask_y[...]
                y_turned[mine] = dot(kv_turned[mine], toeplitz)
                g_sel = jnp.where(owner == j, g_rev[:, part], jnp.zeros((rows, half), BF16))
                cross = dot(g_sel, kv_turned[part, :]) * mask_a[...]
                folded = cross[:, 0:rows] + cross[:, rows:]
                folded = pltpu.roll(folded, 0, 1, stride=1, stride_axis=0)
                dh_ref[q * per + j : q * per + j + 1] = jnp.sum(folded, 0, keepdims=True)
        dh = dot(dh_ref[...].astype(BF16), mirror)
        y = y_turned[...].T
        out_ref[:, near] = (feat_ref[0, :, near] * y).astype(BF16)
        acc, sent, sums = short_stage(
            cot * y, sf_ref[0, :, cols], x_ref[0, :, cols].astype(F32), edge_ref[0, :, cols].astype(F32),
            advance_ref, edge_shift,
        )
        qg_ref[:, near] = acc.astype(BF16)
        tail_ref[:, near] = acc[rows - EDGE :]
        part_ref[:, near] = sent.astype(BF16)
        size = dh.shape[0] * rows // LANES
        for k in range(blocks):
            short_ref[p * blocks + k] = sums[:, k * CHUNK : (k + 1) * CHUNK].astype(BF16)
            lines = range(k * (CHUNK // rows), (k + 1) * (CHUNK // rows))
            long_ref[p * blocks + k] = jnp.concatenate([dh[e * size : (e + 1) * size] for e in lines], 1).astype(BF16)

    return one_step, copies


def pair_part(first, shared, lfr_ref, feat_ref, gn_ref, outs, scratch):
    ids_ref, sf_ref, advance_ref, x_ref, cot_ref, edge_ref = shared
    _, qg_hbm, tail_hbm, part_hbm, packed_hbm = outs
    (qg_ref, tail_ref, part_ref, short_ref,
     edge_shift, mask_g, w_g, g_turned, gm_turned, sems) = scratch
    rows = x_ref.shape[1]
    width = x_ref.shape[2] // lfr_ref.shape[0]
    lag = iota2((rows, rows), 0) - iota2((rows, rows), 1)
    id_row = jnp.broadcast_to(ids_ref[...], (rows, rows)).astype(F32)
    next_col = jnp.broadcast_to(gn_ref[rows - 1 : rows, 0:rows].astype(F32), (rows, rows)).T
    mask_g[0:rows] = ones_where((lag >= 0) & (id_row == id_row.T)).astype(BF16)
    mask_g[rows:] = ones_where((lag < 0) & (next_col == id_row)).astype(BF16)
    edge_shifts(ids_ref, edge_ref, edge_shift)
    blocks = LANES // CHUNK

    def copies(p):
        near = lane_range(p * LANES, LANES)
        cols = lane_range(first + p * LANES, LANES)
        pairs = [
            (qg_ref.at[:, :, near], qg_hbm.at[1:3, :, cols]),
            (tail_ref.at[:, :, near], tail_hbm.at[1:3, :, cols]),
            (part_ref.at[:, :, near], part_hbm.at[1:3, :, cols]),
            (
                short_ref.at[pl.ds(p * blocks, blocks)],
                packed_hbm.at[pl.ds(first // CHUNK + p * blocks, blocks), PADDED : 3 * PADDED],
            ),
        ]
        return [pltpu.make_async_copy(src, dst, sems.at[k, p]) for k, (src, dst) in enumerate(pairs)]

    def one_step(p):
        near = lane_range(p * LANES, LANES)
        cols = lane_range(first + p * LANES, LANES)
        w_g[0:rows] = (cot_ref[:, cols].astype(F32) * feat_ref[0, :, near]).astype(BF16)
        w_g[rows:] = gn_ref[:, near]
        g_turned[...] = w_g[...].T
        for j in range(LANES // width):
            mine = slice(j * width, (j + 1) * width)
            base = pl.multiple_of(first // width + p * (LANES // width), LANES // width)
            taps = jnp.broadcast_to(lfr_ref[pl.ds(base + j, 1), :], (rows, rows))
            taps = pltpu.roll(taps, 0, 1, stride=1, stride_axis=0).astype(BF16)
            toeplitz = jnp.concatenate([taps, taps], 0) * mask_g[...]
            gm_turned[mine] = dot(g_turned[mine], toeplitz)
        gm = gm_turned[...].T
        heads = []
        for i in (1, 2):
            acc, sent, sums = short_stage(
                gm * feat_ref[3 - i, :, near], sf_ref[i, :, cols], x_ref[i, :, cols].astype(F32),
                edge_ref[i, :, cols].astype(F32), advance_ref, edge_shift,
            )
            qg_ref[i - 1, :, near] = acc.astype(BF16)
            tail_ref[i - 1, :, near] = acc[rows - EDGE :]
            part_ref[i - 1, :, near] = sent.astype(BF16)
            heads.append(sums)
        for k in range(blocks):
            picked = [head[:, k * CHUNK : (k + 1) * CHUNK] for head in heads]
            short_ref[p * blocks + k] = jnp.concatenate(picked, 0).astype(BF16)

    return one_step, copies


def mixer_kernel(query_first, pair_first, filled, *refs):
    shared = refs[:6]
    halves = [query_first, pair_first]
    inputs = refs[6:]
    used = 3 * sum(first is not None for first in halves)
    outs = inputs[used + filled : used + filled + 5]
    scratch = inputs[used + filled + 5 :]
    parts = []
    for first, make, size in zip(halves, (query_part, pair_part), (15, 10)):
        if first is not None:
            steps = inputs[2].shape[1] // LANES
            parts.append(make(first, shared, *inputs[:3], outs, scratch[:size]))
            inputs = inputs[3:]
            scratch = scratch[size:]
    run_steps(parts, steps)


def finish_kernel(scale, taps, got_ref, tail_ref, part_ref, qg_in, qg_hbm, long_ref, short_ref, last_ref, sem):
    rows = qg_hbm.shape[1]
    last_ref[...] = (tail_ref[...] + part_ref[...].astype(F32)).astype(BF16)
    copy = pltpu.make_async_copy(last_ref, qg_hbm.at[:, rows - EDGE :, :], sem)
    copy.start()
    total = got_ref[0].astype(F32)
    for k in range(1, got_ref.shape[0]):
        total = total + got_ref[k].astype(F32)
    total = total * scale
    for i in range(3):
        short_ref[i] = total[i * PADDED : i * PADDED + taps]
    size = total.shape[0] - 3 * PADDED
    lags = long_ref.shape[1]
    for p in range(total.shape[1] // lags):
        long_ref[p * size : (p + 1) * size] = total[3 * PADDED :, p * lags : (p + 1) * lags]
    copy.wait()


def shards(qkv, cotangent, doc_ids, short_filter, long_filter):
    _, rows, chans = qkv.shape
    groups, long_taps = long_filter.shape
    taps = short_filter.shape[2]
    devices = lax.axis_size("ctx")
    grad_scale = 1.0 / math.sqrt(rows * devices)
    packed_rows = 3 * PADDED + groups * long_taps // chans
    step_groups = LANES * groups // chans
    params = pltpu.CompilerParams(vmem_limit_bytes=24 << 20)

    ids = doc_ids.reshape(1, rows)
    sf = jnp.transpose(short_filter, (0, 2, 1))

    small = pltpu.CompilerParams(vmem_limit_bytes=8 << 20)
    edge = qkv[:, rows - EDGE :, :]
    edge = edge.at[0, 0, :rows].set(doc_ids.astype(BF16))
    edge = passed_along(edge, 1)

    shifts = ((taps - 1) * rows, rows)
    delay, advance, lf_rev = pl.pallas_call(
        prepare_kernel,
        in_specs=[VMEM] * 2,
        out_specs=[VMEM] * 3,
        out_shape=[
            jax.ShapeDtypeStruct(shifts, BF16),
            jax.ShapeDtypeStruct(shifts, BF16),
            jax.ShapeDtypeStruct((groups, long_taps), F32),
        ],
        cost_estimate=pl.CostEstimate(flops=6_000_000_000, bytes_accessed=16_000_000, transcendentals=0),
        compiler_params=small,
        name="prepare",
    )(ids, long_filter)

    count = chans // PARTS
    sent = []
    for part in range(PARTS):
        feats, kv, grad = pl.pallas_call(
            functools.partial(feature_kernel, part * count),
            in_specs=[VMEM] * 3 + [HBM] * 3,
            out_specs=[VMEM] * 3,
            out_shape=[
                jax.ShapeDtypeStruct((3, rows, count), F32),
                jax.ShapeDtypeStruct((rows, count), BF16),
                jax.ShapeDtypeStruct((rows, count), BF16),
            ],
            scratch_shapes=[
                pltpu.VMEM(((taps - 1) * EDGE, rows), F32),
                pltpu.VMEM((3, taps, count), F32),
                pltpu.VMEM((3, rows, count), BF16),
                pltpu.VMEM((rows, count), BF16),
                pltpu.SemaphoreType.DMA((3, count // LANES)),
            ],
            compiler_params=params,
            cost_estimate=pl.CostEstimate(flops=2_000_000_000, bytes_accessed=4_000_000, transcendentals=0),
            name="features",
        )(ids, delay, edge, sf, qkv, cotangent)
        sent.append((feats, passed_along(kv, 1), passed_along(grad, -1)))

    full = [
        jax.ShapeDtypeStruct((rows, chans), BF16),
        jax.ShapeDtypeStruct((3, rows, chans), BF16),
        jax.ShapeDtypeStruct((3, EDGE, chans), F32),
        jax.ShapeDtypeStruct((3, EDGE, chans), BF16),
        jax.ShapeDtypeStruct((chans // CHUNK, packed_rows, CHUNK), BF16),
    ]
    edge_scratch = pltpu.VMEM(((taps - 1) * EDGE, rows), BF16)
    query_scratch = [
        pltpu.VMEM((rows, count), BF16),
        pltpu.VMEM((rows, count), BF16),
        pltpu.VMEM((EDGE, count), F32),
        pltpu.VMEM((EDGE, count), BF16),
        pltpu.VMEM((count // CHUNK, PADDED, CHUNK), BF16),
        pltpu.VMEM((count // CHUNK, packed_rows - 3 * PADDED, CHUNK), BF16),
        edge_scratch,
        pltpu.VMEM((2 * rows, rows), BF16),
        pltpu.VMEM((rows, 2 * rows), F32),
        pltpu.VMEM((2 * rows, LANES), BF16),
        pltpu.VMEM((rows, LANES), BF16),
        pltpu.VMEM((step_groups, long_taps), F32),
        pltpu.VMEM((LANES, 2 * rows), BF16),
        pltpu.VMEM((LANES, rows), F32),
        pltpu.SemaphoreType.DMA((6, count // LANES)),
    ]
    pair_scratch = [
        pltpu.VMEM((2, rows, count), BF16),
        pltpu.VMEM((2, EDGE, count), F32),
        pltpu.VMEM((2, EDGE, count), BF16),
        pltpu.VMEM((count // CHUNK, 2 * PADDED, CHUNK), BF16),
        edge_scratch,
        pltpu.VMEM((2 * rows, rows), BF16),
        pltpu.VMEM((2 * rows, LANES), BF16),
        pltpu.VMEM((LANES, 2 * rows), BF16),
        pltpu.VMEM((LANES, rows), F32),
        pltpu.SemaphoreType.DMA((4, count // LANES)),
    ]
    results = []
    for stage in range(PARTS + 1):
        operands = [ids, sf, advance, qkv, cotangent, edge]
        scratch = []
        query_first = pair_first = None
        if stage < PARTS:
            query_first = stage * count
            operands += [long_filter, sent[stage][0], sent[stage][1]]
            scratch += query_scratch
        if stage > 0:
            pair_first = (stage - 1) * count
            operands += [lf_rev, sent[stage - 1][0], sent[stage - 1][2]]
            scratch += pair_scratch
        filled = len(results)
        results = pl.pallas_call(
            functools.partial(mixer_kernel, query_first, pair_first, filled),
            in_specs=[VMEM] * len(operands) + [ANY] * filled,
            out_specs=[ANY] * 5,
            out_shape=full,
            input_output_aliases={len(operands) + k: k for k in range(filled)},
            scratch_shapes=scratch,
            compiler_params=params,
            cost_estimate=pl.CostEstimate(flops=4_000_000_000, bytes_accessed=4_000_000, transcendentals=0),
            name=f"mixer{stage}",
        )(*operands, *results)
    out, qg, tail, part, packed = results

    part = passed_along(part, -1)
    per = chans // devices
    if per == CHUNK:
        got = lax.all_to_all(packed, "ctx", 0, 0)
        qg, long_grad, short_grad = pl.pallas_call(
            functools.partial(finish_kernel, grad_scale, taps),
            in_specs=[VMEM, VMEM, VMEM, ANY],
            out_specs=[ANY, VMEM, VMEM],
            out_shape=[
                jax.ShapeDtypeStruct(qg.shape, BF16),
                jax.ShapeDtypeStruct((groups // devices, long_taps), F32),
                jax.ShapeDtypeStruct((3, taps, per), F32),
            ],
            input_output_aliases={3: 0},
            scratch_shapes=[pltpu.VMEM((3, EDGE, chans), BF16), pltpu.SemaphoreType.DMA],
            compiler_params=small,
            cost_estimate=pl.CostEstimate(flops=1_000_000, bytes_accessed=200_000, transcendentals=0),
            name="finish",
        )(got, tail, part, qg)
        return (out, qg, long_grad, short_grad.transpose(0, 2, 1))
    qg = lax.dynamic_update_slice(qg, (tail + part.astype(F32)).astype(BF16), (0, rows - EDGE, 0))
    head = 3 * PADDED
    short_part = packed[:, :head].transpose(1, 0, 2).reshape(head, devices, per)
    long_part = packed[:, head:].reshape(-1, packed_rows - head, CHUNK // long_taps, long_taps)
    long_part = long_part.transpose(0, 2, 1, 3).reshape(devices, -1, per)
    got = jnp.concatenate([short_part.transpose(1, 0, 2), long_part], 1)
    got = lax.all_to_all(got, "ctx", 0, 0)
    total = jnp.sum(got.astype(F32), 0) * grad_scale
    short_grad = total[:head].reshape(3, PADDED, per)[:, :taps].transpose(0, 2, 1)
    long_grad = total[head:].reshape(groups // devices, long_taps)
    return (out, qg, long_grad, short_grad)


def solution(mesh):
    in_specs = (P(None, "ctx", "tp"), P("ctx", "tp"), P("ctx"), P(None, "tp", None), P("tp", None))
    out_specs = (
        P("ctx", "tp"),
        P(None, "ctx", "tp"),
        P(("tp", "ctx"), None),
        P(None, ("tp", "ctx"), None),
    )
    return jax.shard_map(shards, mesh=mesh, in_specs=in_specs, out_specs=out_specs, check_vma=False)
```

```python
import functools
import math

import jax
import jax.numpy as jnp
from jax import lax
from jax.experimental import pallas as pl
from jax.experimental.pallas import tpu as pltpu
from jax.sharding import PartitionSpec as P

F32 = jnp.float32
BF16 = jnp.bfloat16
EDGE = 8
LANES = 512
CHUNK = 256
PADDED = 8
PARTS = 2

VMEM = pl.BlockSpec(memory_space=pltpu.VMEM)
ANY = pl.BlockSpec(memory_space=pl.ANY)
HBM = pl.BlockSpec(memory_space=pltpu.HBM)


def passed_along(block, distance):
    devices = range(lax.axis_size("ctx"))
    route = [(i - distance, i) for i in devices if i - distance in devices]
    return lax.ppermute(block, "ctx", route)


def iota2(shape, dim):
    return lax.broadcasted_iota(jnp.int32, shape, dim)


def dot(a, b):
    return jnp.dot(a, b, preferred_element_type=F32)


def lane_range(start, size):
    return pl.ds(pl.multiple_of(start, size), size)


def ones_where(cond):
    return jnp.where(cond, 1.0, 0.0)


def prepare_kernel(ids_ref, lf_ref, delay_ref, advance_ref, lfr_ref):
    rows = delay_ref.shape[1]
    taps = delay_ref.shape[0] // rows + 1
    id_row = jnp.broadcast_to(ids_ref[...], (rows, rows)).astype(F32)
    same = id_row == id_row.T
    lag = iota2((rows, rows), 0) - iota2((rows, rows), 1)
    for t in range(1, taps):
        delay_ref[(t - 1) * rows : t * rows] = ones_where((lag == t) & same).astype(BF16)
        advance_ref[(t - 1) * rows : t * rows] = ones_where((lag == -t) & same).astype(BF16)
    backward = ones_where((iota2((rows, rows), 0) + iota2((rows, rows), 1)) % rows == 0)
    lfr_ref[...] = dot(lf_ref[...].astype(BF16), backward.astype(BF16))


def feature_kernel(first, streams, ids_ref, delay_ref, edge_ref, sf_hbm, x_hbm, cot_hbm, _,
                   feat_ref, sent_ref, edge_shift, sf_ref, x_ref, cot_ref, sems):
    rows = x_ref.shape[1]
    taps = sf_ref.shape[1]
    steps = sent_ref.shape[1] // LANES
    pick = pl.ds(streams[0], len(streams))
    gradient = len(streams) == 1

    def loads(p):
        near = lane_range(p * LANES, LANES)
        cols = lane_range(first + p * LANES, LANES)
        pairs = [
            (sf_hbm.at[pick, :, cols], sf_ref.at[:, :, near]),
            (x_hbm.at[pick, :, cols], x_ref.at[:, :, near]),
        ]
        if gradient:
            pairs.append((cot_hbm.at[:, cols], cot_ref.at[:, near]))
        return [pltpu.make_async_copy(src, dst, sems.at[k, p]) for k, (src, dst) in enumerate(pairs)]

    for p in range(steps):
        for copy in loads(p):
            copy.start()
    id_row = jnp.broadcast_to(ids_ref[...], (rows, rows)).astype(F32)
    head_ids = id_row.T[0:EDGE]
    before = jnp.broadcast_to(edge_ref[0, 0:1, 0:rows].astype(F32), (EDGE, rows))
    before = pltpu.roll(before, EDGE, 1)
    lag = iota2((EDGE, rows), 0) + EDGE - iota2((EDGE, rows), 1)
    for t in range(1, taps):
        edge_shift[(t - 1) * EDGE : t * EDGE] = ones_where((lag == t) & (before == head_ids))
    id_wide = jnp.concatenate([ids_ref[...].astype(F32)] * (LANES // rows), 1)

    def one_step(p, carry):
        near = lane_range(p * LANES, LANES)
        cols = lane_range(first + p * LANES, LANES)
        for copy in loads(p):
            copy.wait()
        feats = []
        for i, stream in enumerate(streams):
            x = x_ref[i, :, near]
            w = sf_ref[i, :, near]
            moved = dot(delay_ref[...], x)
            acc = w[0:1] * x.astype(F32)
            for t in range(1, taps):
                acc = acc + w[t : t + 1] * moved[(t - 1) * rows : t * rows]
            edge = edge_ref[stream, :, cols].astype(F32)
            edge = jnp.concatenate([edge, jnp.zeros((rows - EDGE, LANES), F32)], 0)
            moved = dot(edge_shift[...].astype(BF16), edge.astype(BF16))
            fix = w[1:2] * moved[0:EDGE]
            for t in range(2, taps):
                fix = fix + w[t : t + 1] * moved[(t - 1) * EDGE : t * EDGE]
            acc = jnp.concatenate([acc[0:EDGE] + fix, acc[EDGE:]], 0)
            feat_ref[i, :, near] = acc
            feats.append(acc)
        if gradient:
            g = cot_ref[:, near].astype(F32) * feats[0]
            last = iota2(g.shape, 0) == rows - 1
            sent_ref[:, near] = jnp.where(last, jnp.broadcast_to(id_wide, g.shape), g).astype(BF16)
        else:
            sent_ref[:, near] = (feats[0] * feats[1]).astype(BF16)
        return carry

    lax.fori_loop(0, steps, one_step, 0)


def run_steps(parts, steps):
    def start(p, carry):
        for one_step, copies in parts:
            one_step(p)
            for copy in copies(p):
                copy.start()
        return carry

    def drain(p, carry):
        for _, copies in parts:
            for copy in copies(p):
                copy.wait()
        return carry

    lax.fori_loop(0, steps, start, 0)
    lax.fori_loop(0, steps, drain, 0)


def edge_shifts(ids_ref, edge_ref, edge_shift):
    rows = edge_shift.shape[1]
    taps = edge_shift.shape[0] // EDGE + 1
    id_head = jnp.broadcast_to(ids_ref[...], (EDGE, rows)).astype(F32)
    prev = jnp.broadcast_to(edge_ref[0, 0:1, 0:rows].astype(F32), (rows, rows)).T
    lag = iota2((EDGE, rows), 1) + EDGE - iota2((EDGE, rows), 0)
    same = prev[rows - EDGE :] == id_head
    pieces = [ones_where((lag == t) & same) for t in range(1, taps)]
    edge_shift[...] = jnp.concatenate(pieces, 0).astype(BF16)


def short_stage(gf, w, x, xe, advance_ref, edge_shift):
    rows = gf.shape[0]
    taps = w.shape[0]
    gf_sent = gf.astype(BF16)
    moved = dot(advance_ref[...], gf_sent)
    moved_edge = dot(edge_shift[...], gf_sent)
    acc = w[0:1] * gf
    sums = [jnp.sum(x * gf, 0, keepdims=True)]
    sent = jnp.zeros((EDGE, LANES), F32)
    for t in range(1, taps):
        piece = moved[(t - 1) * rows : t * rows]
        piece_edge = moved_edge[(t - 1) * EDGE : t * EDGE]
        acc = acc + w[t : t + 1] * piece
        sent = sent + w[t : t + 1] * piece_edge
        sums.append(jnp.sum(x * piece, 0, keepdims=True) + jnp.sum(xe * piece_edge, 0, keepdims=True))
    sums.append(jnp.zeros((PADDED - taps, LANES), F32))
    return acc, sent, jnp.concatenate(sums, 0)


def query_part(first, shared, lf_ref, q_ref, feat_ref, kvp_ref, outs, scratch):
    ids_ref, sf_ref, advance_ref, x_ref, cot_ref, edge_ref = shared
    out_hbm, qg_hbm, tail_hbm, part_hbm, packed_hbm = outs
    (out_ref, qg_ref, tail_ref, part_ref, short_ref, long_ref,
     edge_shift, mask_y, mask_a, w_kv, g_rev, dh_ref, kv_turned, y_turned, sems) = scratch
    rows = x_ref.shape[1]
    width = x_ref.shape[2] // lf_ref.shape[0]
    half = rows
    per = half // width
    lag = iota2((rows, rows), 0) - iota2((rows, rows), 1)
    mirror = ones_where(iota2((rows, rows), 0) + iota2((rows, rows), 1) == rows - 1).astype(BF16)
    id_row = jnp.broadcast_to(ids_ref[...], (rows, rows)).astype(F32)
    id_col = id_row.T
    prev_row = jnp.broadcast_to(edge_ref[0, 0:1, 0:rows].astype(F32), (rows, rows))
    same = id_row == id_col
    mask_y[0:rows] = ones_where((lag <= 0) & same).astype(BF16)
    mask_y[rows:] = ones_where((lag > 0) & (prev_row.T == id_row)).astype(BF16)
    mask_a[:, 0:rows] = dot(mirror, ones_where((lag >= 0) & same).astype(BF16))
    mask_a[:, rows:] = dot(mirror, ones_where((lag < 0) & (prev_row == id_col)).astype(BF16))
    edge_shifts(ids_ref, edge_ref, edge_shift)
    owner = iota2((rows, half), 1) // width
    blocks = LANES // CHUNK
    head = 3 * PADDED

    def copies(p):
        near = lane_range(p * LANES, LANES)
        cols = lane_range(first + p * LANES, LANES)
        here = pl.ds(p * blocks, blocks)
        there = pl.ds(first // CHUNK + p * blocks, blocks)
        pairs = [
            (out_ref.at[:, near], out_hbm.at[:, cols]),
            (qg_ref.at[:, near], qg_hbm.at[0, :, cols]),
            (tail_ref.at[:, near], tail_hbm.at[0, :, cols]),
            (part_ref.at[:, near], part_hbm.at[0, :, cols]),
            (short_ref.at[here], packed_hbm.at[there, 0:PADDED]),
            (long_ref.at[here], packed_hbm.at[there, head:]),
        ]
        return [pltpu.make_async_copy(src, dst, sems.at[k, p]) for k, (src, dst) in enumerate(pairs)]

    def one_step(p):
        near = lane_range(p * LANES, LANES)
        cols = lane_range(first + p * LANES, LANES)
        cot = cot_ref[:, cols].astype(F32)
        w_kv[0:rows] = (feat_ref[0, :, near] * feat_ref[1, :, near]).astype(BF16)
        w_kv[rows:] = kvp_ref[:, near]
        kv_turned[...] = w_kv[...].T
        g_rev[...] = dot(mirror, (cot * q_ref[0, :, near]).astype(BF16)).astype(BF16)
        for q in range(LANES // half):
            part = slice(q * half, (q + 1) * half)
            base = pl.multiple_of((first // half) * per + p * (LANES // width) + q * per, per)
            for j in range(per):
                mine = slice((q * per + j) * width, (q * per + j + 1) * width)
                taps = jnp.broadcast_to(lf_ref[pl.ds(base + j, 1), :], (rows, rows))
                taps = pltpu.roll(taps, 0, 1, stride=1, stride_axis=0).astype(BF16)
                toeplitz = jnp.concatenate([taps, taps], 0) * mask_y[...]
                y_turned[mine] = dot(kv_turned[mine], toeplitz)
                g_sel = jnp.where(owner == j, g_rev[:, part], jnp.zeros((rows, half), BF16))
                cross = dot(g_sel, kv_turned[part, :]) * mask_a[...]
                folded = cross[:, 0:rows] + cross[:, rows:]
                folded = pltpu.roll(folded, 0, 1, stride=1, stride_axis=0)
                dh_ref[q * per + j : q * per + j + 1] = jnp.sum(folded, 0, keepdims=True)
        dh = dot(dh_ref[...].astype(BF16), mirror)
        y = y_turned[...].T
        out_ref[:, near] = (q_ref[0, :, near] * y).astype(BF16)
        acc, sent, sums = short_stage(
            cot * y, sf_ref[0, :, cols], x_ref[0, :, cols].astype(F32), edge_ref[0, :, cols].astype(F32),
            advance_ref, edge_shift,
        )
        qg_ref[:, near] = acc.astype(BF16)
        tail_ref[:, near] = acc[rows - EDGE :]
        part_ref[:, near] = sent.astype(BF16)
        size = dh.shape[0] * rows // LANES
        for k in range(blocks):
            short_ref[p * blocks + k] = sums[:, k * CHUNK : (k + 1) * CHUNK].astype(BF16)
            lines = range(k * (CHUNK // rows), (k + 1) * (CHUNK // rows))
            long_ref[p * blocks + k] = jnp.concatenate([dh[e * size : (e + 1) * size] for e in lines], 1).astype(BF16)

    return one_step, copies


def pair_part(first, shared, lfr_ref, q_ref, feat_ref, gn_ref, outs, scratch):
    ids_ref, sf_ref, advance_ref, x_ref, cot_ref, edge_ref = shared
    _, qg_hbm, tail_hbm, part_hbm, packed_hbm = outs
    (qg_ref, tail_ref, part_ref, short_ref,
     edge_shift, mask_g, w_g, g_turned, gm_turned, sems) = scratch
    rows = x_ref.shape[1]
    width = x_ref.shape[2] // lfr_ref.shape[0]
    lag = iota2((rows, rows), 0) - iota2((rows, rows), 1)
    id_row = jnp.broadcast_to(ids_ref[...], (rows, rows)).astype(F32)
    next_col = jnp.broadcast_to(gn_ref[rows - 1 : rows, 0:rows].astype(F32), (rows, rows)).T
    mask_g[0:rows] = ones_where((lag >= 0) & (id_row == id_row.T)).astype(BF16)
    mask_g[rows:] = ones_where((lag < 0) & (next_col == id_row)).astype(BF16)
    edge_shifts(ids_ref, edge_ref, edge_shift)
    blocks = LANES // CHUNK

    def copies(p):
        near = lane_range(p * LANES, LANES)
        cols = lane_range(first + p * LANES, LANES)
        pairs = [
            (qg_ref.at[:, :, near], qg_hbm.at[1:3, :, cols]),
            (tail_ref.at[:, :, near], tail_hbm.at[1:3, :, cols]),
            (part_ref.at[:, :, near], part_hbm.at[1:3, :, cols]),
            (
                short_ref.at[pl.ds(p * blocks, blocks)],
                packed_hbm.at[pl.ds(first // CHUNK + p * blocks, blocks), PADDED : 3 * PADDED],
            ),
        ]
        return [pltpu.make_async_copy(src, dst, sems.at[k, p]) for k, (src, dst) in enumerate(pairs)]

    def one_step(p):
        near = lane_range(p * LANES, LANES)
        cols = lane_range(first + p * LANES, LANES)
        w_g[0:rows] = (cot_ref[:, cols].astype(F32) * q_ref[0, :, near]).astype(BF16)
        w_g[rows:] = gn_ref[:, near]
        g_turned[...] = w_g[...].T
        for j in range(LANES // width):
            mine = slice(j * width, (j + 1) * width)
            base = pl.multiple_of(first // width + p * (LANES // width), LANES // width)
            taps = jnp.broadcast_to(lfr_ref[pl.ds(base + j, 1), :], (rows, rows))
            taps = pltpu.roll(taps, 0, 1, stride=1, stride_axis=0).astype(BF16)
            toeplitz = jnp.concatenate([taps, taps], 0) * mask_g[...]
            gm_turned[mine] = dot(g_turned[mine], toeplitz)
        gm = gm_turned[...].T
        heads = []
        for i in (1, 2):
            acc, sent, sums = short_stage(
                gm * feat_ref[2 - i, :, near], sf_ref[i, :, cols], x_ref[i, :, cols].astype(F32),
                edge_ref[i, :, cols].astype(F32), advance_ref, edge_shift,
            )
            qg_ref[i - 1, :, near] = acc.astype(BF16)
            tail_ref[i - 1, :, near] = acc[rows - EDGE :]
            part_ref[i - 1, :, near] = sent.astype(BF16)
            heads.append(sums)
        for k in range(blocks):
            picked = [head[:, k * CHUNK : (k + 1) * CHUNK] for head in heads]
            short_ref[p * blocks + k] = jnp.concatenate(picked, 0).astype(BF16)

    return one_step, copies


def mixer_kernel(query_first, pair_first, filled, *refs):
    shared = refs[:6]
    halves = [query_first, pair_first]
    inputs = refs[6:]
    used = 4 * sum(first is not None for first in halves)
    outs = inputs[used + filled : used + filled + 5]
    scratch = inputs[used + filled + 5 :]
    parts = []
    for first, make, size in zip(halves, (query_part, pair_part), (15, 10)):
        if first is not None:
            steps = inputs[3].shape[1] // LANES
            parts.append(make(first, shared, *inputs[:4], outs, scratch[:size]))
            inputs = inputs[4:]
            scratch = scratch[size:]
    run_steps(parts, steps)


def finish_kernel(scale, taps, got_ref, tail_ref, part_ref, qg_in, qg_hbm, long_ref, short_ref, last_ref, sem):
    rows = qg_hbm.shape[1]
    last_ref[...] = (tail_ref[...] + part_ref[...].astype(F32)).astype(BF16)
    copy = pltpu.make_async_copy(last_ref, qg_hbm.at[:, rows - EDGE :, :], sem)
    copy.start()
    total = got_ref[0].astype(F32)
    for k in range(1, got_ref.shape[0]):
        total = total + got_ref[k].astype(F32)
    total = total * scale
    for i in range(3):
        short_ref[i] = total[i * PADDED : i * PADDED + taps]
    size = total.shape[0] - 3 * PADDED
    lags = long_ref.shape[1]
    for p in range(total.shape[1] // lags):
        long_ref[p * size : (p + 1) * size] = total[3 * PADDED :, p * lags : (p + 1) * lags]
    copy.wait()


def shards(qkv, cotangent, doc_ids, short_filter, long_filter):
    _, rows, chans = qkv.shape
    groups, long_taps = long_filter.shape
    taps = short_filter.shape[2]
    devices = lax.axis_size("ctx")
    grad_scale = 1.0 / math.sqrt(rows * devices)
    packed_rows = 3 * PADDED + groups * long_taps // chans
    step_groups = LANES * groups // chans
    params = pltpu.CompilerParams(vmem_limit_bytes=24 << 20)

    ids = doc_ids.reshape(1, rows)
    sf = jnp.transpose(short_filter, (0, 2, 1))

    small = pltpu.CompilerParams(vmem_limit_bytes=8 << 20)
    edge = qkv[:, rows - EDGE :, :]
    edge = edge.at[0, 0, :rows].set(doc_ids.astype(BF16))
    edge = passed_along(edge, 1)

    shifts = ((taps - 1) * rows, rows)
    delay, advance, lf_rev = pl.pallas_call(
        prepare_kernel,
        in_specs=[VMEM] * 2,
        out_specs=[VMEM] * 3,
        out_shape=[
            jax.ShapeDtypeStruct(shifts, BF16),
            jax.ShapeDtypeStruct(shifts, BF16),
            jax.ShapeDtypeStruct((groups, long_taps), F32),
        ],
        cost_estimate=pl.CostEstimate(flops=6_000_000_000, bytes_accessed=16_000_000, transcendentals=0),
        compiler_params=small,
        name="prepare",
    )(ids, long_filter)

    count = chans // PARTS
    after = ids
    features = []
    for streams, distance in (((1, 2), 1), ((0,), -1)):
        for part in range(PARTS):
            feats, message = pl.pallas_call(
                functools.partial(feature_kernel, part * count, streams),
                in_specs=[VMEM] * 3 + [HBM] * 3 + [ANY],
                out_specs=[VMEM] * 2,
                out_shape=[
                    jax.ShapeDtypeStruct((len(streams), rows, count), F32),
                    jax.ShapeDtypeStruct((rows, count), BF16),
                ],
                scratch_shapes=[
                    pltpu.VMEM(((taps - 1) * EDGE, rows), F32),
                    pltpu.VMEM((len(streams), taps, count), F32),
                    pltpu.VMEM((len(streams), rows, count), BF16),
                    pltpu.VMEM((rows, count), BF16),
                    pltpu.SemaphoreType.DMA((3, count // LANES)),
                ],
                compiler_params=params,
                cost_estimate=pl.CostEstimate(flops=2_000_000_000, bytes_accessed=4_000_000, transcendentals=0),
                name="features",
            )(ids, delay, edge, sf, qkv, cotangent, after)
            after = message
            features.append((feats, passed_along(message, distance)))

    full = [
        jax.ShapeDtypeStruct((rows, chans), BF16),
        jax.ShapeDtypeStruct((3, rows, chans), BF16),
        jax.ShapeDtypeStruct((3, EDGE, chans), F32),
        jax.ShapeDtypeStruct((3, EDGE, chans), BF16),
        jax.ShapeDtypeStruct((chans // CHUNK, packed_rows, CHUNK), BF16),
    ]
    edge_scratch = pltpu.VMEM(((taps - 1) * EDGE, rows), BF16)
    query_scratch = [
        pltpu.VMEM((rows, count), BF16),
        pltpu.VMEM((rows, count), BF16),
        pltpu.VMEM((EDGE, count), F32),
        pltpu.VMEM((EDGE, count), BF16),
        pltpu.VMEM((count // CHUNK, PADDED, CHUNK), BF16),
        pltpu.VMEM((count // CHUNK, packed_rows - 3 * PADDED, CHUNK), BF16),
        edge_scratch,
        pltpu.VMEM((2 * rows, rows), BF16),
        pltpu.VMEM((rows, 2 * rows), F32),
        pltpu.VMEM((2 * rows, LANES), BF16),
        pltpu.VMEM((rows, LANES), BF16),
        pltpu.VMEM((step_groups, long_taps), F32),
        pltpu.VMEM((LANES, 2 * rows), BF16),
        pltpu.VMEM((LANES, rows), F32),
        pltpu.SemaphoreType.DMA((6, count // LANES)),
    ]
    pair_scratch = [
        pltpu.VMEM((2, rows, count), BF16),
        pltpu.VMEM((2, EDGE, count), F32),
        pltpu.VMEM((2, EDGE, count), BF16),
        pltpu.VMEM((count // CHUNK, 2 * PADDED, CHUNK), BF16),
        edge_scratch,
        pltpu.VMEM((2 * rows, rows), BF16),
        pltpu.VMEM((2 * rows, LANES), BF16),
        pltpu.VMEM((LANES, 2 * rows), BF16),
        pltpu.VMEM((LANES, rows), F32),
        pltpu.SemaphoreType.DMA((4, count // LANES)),
    ]
    results = []
    stages = [(stage, None) for stage in range(PARTS)] + [(None, stage) for stage in range(PARTS)]
    for query, pair in stages:
        operands = [ids, sf, advance, qkv, cotangent, edge]
        scratch = []
        query_first = pair_first = None
        if query is not None:
            query_first = query * count
            operands += [long_filter, features[PARTS + query][0], *features[query]]
            scratch += query_scratch
        if pair is not None:
            pair_first = pair * count
            operands += [lf_rev, features[PARTS + pair][0], features[pair][0], features[PARTS + pair][1]]
            scratch += pair_scratch
        filled = len(results)
        results = pl.pallas_call(
            functools.partial(mixer_kernel, query_first, pair_first, filled),
            in_specs=[VMEM] * len(operands) + [ANY] * filled,
            out_specs=[ANY] * 5,
            out_shape=full,
            input_output_aliases={len(operands) + k: k for k in range(filled)},
            scratch_shapes=scratch,
            compiler_params=params,
            cost_estimate=pl.CostEstimate(flops=4_000_000_000, bytes_accessed=4_000_000, transcendentals=0),
            name="query" if pair is None else "pair",
        )(*operands, *results)
    out, qg, tail, part, packed = results

    part = passed_along(part, -1)
    per = chans // devices
    if per == CHUNK:
        got = lax.all_to_all(packed, "ctx", 0, 0)
        qg, long_grad, short_grad = pl.pallas_call(
            functools.partial(finish_kernel, grad_scale, taps),
            in_specs=[VMEM, VMEM, VMEM, ANY],
            out_specs=[ANY, VMEM, VMEM],
            out_shape=[
                jax.ShapeDtypeStruct(qg.shape, BF16),
                jax.ShapeDtypeStruct((groups // devices, long_taps), F32),
                jax.ShapeDtypeStruct((3, taps, per), F32),
            ],
            input_output_aliases={3: 0},
            scratch_shapes=[pltpu.VMEM((3, EDGE, chans), BF16), pltpu.SemaphoreType.DMA],
            compiler_params=small,
            cost_estimate=pl.CostEstimate(flops=1_000_000, bytes_accessed=200_000, transcendentals=0),
            name="finish",
        )(got, tail, part, qg)
        return (out, qg, long_grad, short_grad.transpose(0, 2, 1))
    qg = lax.dynamic_update_slice(qg, (tail + part.astype(F32)).astype(BF16), (0, rows - EDGE, 0))
    head = 3 * PADDED
    short_part = packed[:, :head].transpose(1, 0, 2).reshape(head, devices, per)
    long_part = packed[:, head:].reshape(-1, packed_rows - head, CHUNK // long_taps, long_taps)
    long_part = long_part.transpose(0, 2, 1, 3).reshape(devices, -1, per)
    got = jnp.concatenate([short_part.transpose(1, 0, 2), long_part], 1)
    got = lax.all_to_all(got, "ctx", 0, 0)
    total = jnp.sum(got.astype(F32), 0) * grad_scale
    short_grad = total[:head].reshape(3, PADDED, per)[:, :taps].transpose(0, 2, 1)
    long_grad = total[head:].reshape(groups // devices, long_taps)
    return (out, qg, long_grad, short_grad)


def solution(mesh):
    in_specs = (P(None, "ctx", "tp"), P("ctx", "tp"), P("ctx"), P(None, "tp", None), P("tp", None))
    out_specs = (
        P("ctx", "tp"),
        P(None, "ctx", "tp"),
        P(("tp", "ctx"), None),
        P(None, ("tp", "ctx"), None),
    )
    return jax.shard_map(shards, mesh=mesh, in_specs=in_specs, out_specs=out_specs, check_vma=False)
```

```python
import functools
import math

import jax
import jax.numpy as jnp
from jax import lax
from jax.experimental import pallas as pl
from jax.experimental.pallas import tpu as pltpu
from jax.sharding import PartitionSpec as P

F32 = jnp.float32
BF16 = jnp.bfloat16
EDGE = 8
LANES = 512
CHUNK = 256
PADDED = 8
PARTS = 2

VMEM = pl.BlockSpec(memory_space=pltpu.VMEM)
ANY = pl.BlockSpec(memory_space=pl.ANY)
HBM = pl.BlockSpec(memory_space=pltpu.HBM)


def passed_along(block, distance):
    devices = range(lax.axis_size("ctx"))
    route = [(i - distance, i) for i in devices if i - distance in devices]
    return lax.ppermute(block, "ctx", route)


def iota2(shape, dim):
    return lax.broadcasted_iota(jnp.int32, shape, dim)


def dot(a, b):
    return jnp.dot(a, b, preferred_element_type=F32)


def lane_range(start, size):
    return pl.ds(pl.multiple_of(start, size), size)


def ones_where(cond):
    return jnp.where(cond, 1.0, 0.0)


def prepare_kernel(ids_ref, lf_ref, delay_ref, advance_ref, lfr_ref):
    rows = delay_ref.shape[1]
    taps = delay_ref.shape[0] // rows + 1
    id_row = jnp.broadcast_to(ids_ref[...], (rows, rows)).astype(F32)
    same = id_row == id_row.T
    lag = iota2((rows, rows), 0) - iota2((rows, rows), 1)
    for t in range(1, taps):
        delay_ref[(t - 1) * rows : t * rows] = ones_where((lag == t) & same).astype(BF16)
        advance_ref[(t - 1) * rows : t * rows] = ones_where((lag == -t) & same).astype(BF16)
    backward = ones_where((iota2((rows, rows), 0) + iota2((rows, rows), 1)) % rows == 0)
    lfr_ref[...] = dot(lf_ref[...].astype(BF16), backward.astype(BF16))


def local_kernel(first, ids_ref, delay_ref, sf_hbm, x_hbm, _, feat_ref, sf_ref, x_ref, sems):
    rows = x_ref.shape[1]
    taps = sf_ref.shape[1]
    steps = feat_ref.shape[2] // LANES

    def loads(p):
        near = lane_range(p * LANES, LANES)
        cols = lane_range(first + p * LANES, LANES)
        pairs = [
            (sf_hbm.at[:, :, cols], sf_ref.at[:, :, near]),
            (x_hbm.at[:, :, cols], x_ref.at[:, :, near]),
        ]
        return [pltpu.make_async_copy(src, dst, sems.at[k, p]) for k, (src, dst) in enumerate(pairs)]

    for p in range(steps):
        for copy in loads(p):
            copy.start()

    def one_step(p, carry):
        near = lane_range(p * LANES, LANES)
        for copy in loads(p):
            copy.wait()
        for i in range(3):
            x = x_ref[i, :, near]
            w = sf_ref[i, :, near]
            moved = dot(delay_ref[...], x)
            acc = w[0:1] * x.astype(F32)
            for t in range(1, taps):
                acc = acc + w[t : t + 1] * moved[(t - 1) * rows : t * rows]
            feat_ref[i, :, near] = acc
        return carry

    lax.fori_loop(0, steps, one_step, 0)


def message_kernel(first, streams, ids_ref, prev_ref, edge_ref, sf_ref, cot_ref, local_ref, _,
                   head_ref, sent_ref, edge_shift):
    rows = local_ref.shape[1]
    taps = sf_ref.shape[1]
    head_ids = jnp.broadcast_to(ids_ref[...], (rows, rows)).astype(F32).T[0:EDGE]
    before = pltpu.roll(jnp.broadcast_to(prev_ref[...].astype(F32), (EDGE, rows)), EDGE, 1)
    lag = iota2((EDGE, rows), 0) + EDGE - iota2((EDGE, rows), 1)
    for t in range(1, taps):
        edge_shift[(t - 1) * EDGE : t * EDGE] = ones_where((lag == t) & (before == head_ids))
    id_wide = jnp.concatenate([ids_ref[...].astype(F32)] * (LANES // rows), 1)

    def one_step(p, carry):
        near = lane_range(p * LANES, LANES)
        cols = lane_range(first + p * LANES, LANES)
        feats = []
        for i, stream in enumerate(streams):
            w = sf_ref[stream, :, cols]
            edge = edge_ref[stream, :, cols].astype(F32)
            edge = jnp.concatenate([edge, jnp.zeros((rows - EDGE, LANES), F32)], 0)
            moved = dot(edge_shift[...].astype(BF16), edge.astype(BF16))
            head = local_ref[stream, 0:EDGE, near] + w[1:2] * moved[0:EDGE]
            for t in range(2, taps):
                head = head + w[t : t + 1] * moved[(t - 1) * EDGE : t * EDGE]
            head_ref[i, :, near] = head
            feats.append(jnp.concatenate([head, local_ref[stream, EDGE:, near]], 0))
        if len(streams) == 1:
            g = cot_ref[:, cols].astype(F32) * feats[0]
            last = iota2(g.shape, 0) == rows - 1
            sent_ref[:, near] = jnp.where(last, jnp.broadcast_to(id_wide, g.shape), g).astype(BF16)
        else:
            sent_ref[:, near] = (feats[0] * feats[1]).astype(BF16)
        return carry

    lax.fori_loop(0, sent_ref.shape[1] // LANES, one_step, 0)


def run_steps(parts, steps):
    def start(p, carry):
        for one_step, copies in parts:
            one_step(p)
            for copy in copies(p):
                copy.start()
        return carry

    def drain(p, carry):
        for _, copies in parts:
            for copy in copies(p):
                copy.wait()
        return carry

    lax.fori_loop(0, steps, start, 0)
    lax.fori_loop(0, steps, drain, 0)


def joined(head, local):
    return jnp.concatenate([head, local[EDGE:]], 0)


def edge_shifts(ids_ref, prev_ref, edge_shift):
    rows = edge_shift.shape[1]
    taps = edge_shift.shape[0] // EDGE + 1
    id_head = jnp.broadcast_to(ids_ref[...], (EDGE, rows)).astype(F32)
    prev = jnp.broadcast_to(prev_ref[...], (rows, rows)).astype(F32).T
    lag = iota2((EDGE, rows), 1) + EDGE - iota2((EDGE, rows), 0)
    same = prev[rows - EDGE :] == id_head
    pieces = [ones_where((lag == t) & same) for t in range(1, taps)]
    edge_shift[...] = jnp.concatenate(pieces, 0).astype(BF16)


def short_stage(gf, w, x, xe, advance_ref, edge_shift):
    rows = gf.shape[0]
    taps = w.shape[0]
    gf_sent = gf.astype(BF16)
    moved = dot(advance_ref[...], gf_sent)
    moved_edge = dot(edge_shift[...], gf_sent)
    acc = w[0:1] * gf
    sums = [jnp.sum(x * gf, 0, keepdims=True)]
    sent = jnp.zeros((EDGE, LANES), F32)
    for t in range(1, taps):
        piece = moved[(t - 1) * rows : t * rows]
        piece_edge = moved_edge[(t - 1) * EDGE : t * EDGE]
        acc = acc + w[t : t + 1] * piece
        sent = sent + w[t : t + 1] * piece_edge
        sums.append(jnp.sum(x * piece, 0, keepdims=True) + jnp.sum(xe * piece_edge, 0, keepdims=True))
    sums.append(jnp.zeros((PADDED - taps, LANES), F32))
    return acc, sent, jnp.concatenate(sums, 0)


def query_part(first, shared, lf_ref, local_ref, q_head_ref, kv_head_ref, kvp_ref, outs, scratch):
    ids_ref, prev_ref, sf_ref, advance_ref, x_ref, cot_ref, edge_ref = shared
    out_hbm, qg_hbm, tail_hbm, part_hbm, packed_hbm = outs
    (out_ref, qg_ref, tail_ref, part_ref, short_ref, long_ref,
     edge_shift, mask_y, mask_a, w_kv, g_rev, dh_ref, kv_turned, y_turned, sems) = scratch
    rows = x_ref.shape[1]
    width = x_ref.shape[2] // lf_ref.shape[0]
    half = rows
    per = half // width
    lag = iota2((rows, rows), 0) - iota2((rows, rows), 1)
    mirror = ones_where(iota2((rows, rows), 0) + iota2((rows, rows), 1) == rows - 1).astype(BF16)
    id_row = jnp.broadcast_to(ids_ref[...], (rows, rows)).astype(F32)
    id_col = id_row.T
    prev_row = jnp.broadcast_to(prev_ref[...], (rows, rows)).astype(F32)
    same = id_row == id_col
    mask_y[0:rows] = ones_where((lag <= 0) & same).astype(BF16)
    mask_y[rows:] = ones_where((lag > 0) & (prev_row.T == id_row)).astype(BF16)
    mask_a[:, 0:rows] = dot(mirror, ones_where((lag >= 0) & same).astype(BF16))
    mask_a[:, rows:] = dot(mirror, ones_where((lag < 0) & (prev_row == id_col)).astype(BF16))
    edge_shifts(ids_ref, prev_ref, edge_shift)
    owner = iota2((rows, half), 1) // width
    blocks = LANES // CHUNK
    head = 3 * PADDED

    def copies(p):
        near = lane_range(p * LANES, LANES)
        cols = lane_range(first + p * LANES, LANES)
        here = pl.ds(p * blocks, blocks)
        there = pl.ds(first // CHUNK + p * blocks, blocks)
        pairs = [
            (out_ref.at[:, near], out_hbm.at[:, cols]),
            (qg_ref.at[:, near], qg_hbm.at[0, :, cols]),
            (tail_ref.at[:, near], tail_hbm.at[0, :, cols]),
            (part_ref.at[:, near], part_hbm.at[0, :, cols]),
            (short_ref.at[here], packed_hbm.at[there, 0:PADDED]),
            (long_ref.at[here], packed_hbm.at[there, head:]),
        ]
        return [pltpu.make_async_copy(src, dst, sems.at[k, p]) for k, (src, dst) in enumerate(pairs)]

    def one_step(p):
        near = lane_range(p * LANES, LANES)
        cols = lane_range(first + p * LANES, LANES)
        cot = cot_ref[:, cols].astype(F32)
        q = joined(q_head_ref[0, :, near], local_ref[0, :, near])
        k = joined(kv_head_ref[0, :, near], local_ref[1, :, near])
        v = joined(kv_head_ref[1, :, near], local_ref[2, :, near])
        w_kv[0:rows] = (k * v).astype(BF16)
        w_kv[rows:] = kvp_ref[:, near]
        kv_turned[...] = w_kv[...].T
        g_rev[...] = dot(mirror, (cot * q).astype(BF16)).astype(BF16)
        for h in range(LANES // half):
            part = slice(h * half, (h + 1) * half)
            base = pl.multiple_of((first // half) * per + p * (LANES // width) + h * per, per)
            for j in range(per):
                mine = slice((h * per + j) * width, (h * per + j + 1) * width)
                taps = jnp.broadcast_to(lf_ref[pl.ds(base + j, 1), :], (rows, rows))
                taps = pltpu.roll(taps, 0, 1, stride=1, stride_axis=0).astype(BF16)
                toeplitz = jnp.concatenate([taps, taps], 0) * mask_y[...]
                y_turned[mine] = dot(kv_turned[mine], toeplitz)
                g_sel = jnp.where(owner == j, g_rev[:, part], jnp.zeros((rows, half), BF16))
                cross = dot(g_sel, kv_turned[part, :]) * mask_a[...]
                folded = cross[:, 0:rows] + cross[:, rows:]
                folded = pltpu.roll(folded, 0, 1, stride=1, stride_axis=0)
                dh_ref[h * per + j : h * per + j + 1] = jnp.sum(folded, 0, keepdims=True)
        dh = dot(dh_ref[...].astype(BF16), mirror)
        y = y_turned[...].T
        out_ref[:, near] = (q * y).astype(BF16)
        acc, sent, sums = short_stage(
            cot * y, sf_ref[0, :, cols], x_ref[0, :, cols].astype(F32), edge_ref[0, :, cols].astype(F32),
            advance_ref, edge_shift,
        )
        qg_ref[:, near] = acc.astype(BF16)
        tail_ref[:, near] = acc[rows - EDGE :]
        part_ref[:, near] = sent.astype(BF16)
        size = dh.shape[0] * rows // LANES
        for k in range(blocks):
            short_ref[p * blocks + k] = sums[:, k * CHUNK : (k + 1) * CHUNK].astype(BF16)
            lines = range(k * (CHUNK // rows), (k + 1) * (CHUNK // rows))
            long_ref[p * blocks + k] = jnp.concatenate([dh[e * size : (e + 1) * size] for e in lines], 1).astype(BF16)

    return one_step, copies


def pair_part(first, shared, lfr_ref, local_ref, q_head_ref, kv_head_ref, gn_ref, outs, scratch):
    ids_ref, prev_ref, sf_ref, advance_ref, x_ref, cot_ref, edge_ref = shared
    _, qg_hbm, tail_hbm, part_hbm, packed_hbm = outs
    (qg_ref, tail_ref, part_ref, short_ref,
     edge_shift, mask_g, w_g, g_turned, gm_turned, sems) = scratch
    rows = x_ref.shape[1]
    width = x_ref.shape[2] // lfr_ref.shape[0]
    lag = iota2((rows, rows), 0) - iota2((rows, rows), 1)
    id_row = jnp.broadcast_to(ids_ref[...], (rows, rows)).astype(F32)
    next_col = jnp.broadcast_to(gn_ref[rows - 1 : rows, 0:rows].astype(F32), (rows, rows)).T
    mask_g[0:rows] = ones_where((lag >= 0) & (id_row == id_row.T)).astype(BF16)
    mask_g[rows:] = ones_where((lag < 0) & (next_col == id_row)).astype(BF16)
    edge_shifts(ids_ref, prev_ref, edge_shift)
    blocks = LANES // CHUNK

    def copies(p):
        near = lane_range(p * LANES, LANES)
        cols = lane_range(first + p * LANES, LANES)
        pairs = [
            (qg_ref.at[:, :, near], qg_hbm.at[1:3, :, cols]),
            (tail_ref.at[:, :, near], tail_hbm.at[1:3, :, cols]),
            (part_ref.at[:, :, near], part_hbm.at[1:3, :, cols]),
            (
                short_ref.at[pl.ds(p * blocks, blocks)],
                packed_hbm.at[pl.ds(first // CHUNK + p * blocks, blocks), PADDED : 3 * PADDED],
            ),
        ]
        return [pltpu.make_async_copy(src, dst, sems.at[k, p]) for k, (src, dst) in enumerate(pairs)]

    def one_step(p):
        near = lane_range(p * LANES, LANES)
        cols = lane_range(first + p * LANES, LANES)
        q = joined(q_head_ref[0, :, near], local_ref[0, :, near])
        w_g[0:rows] = (cot_ref[:, cols].astype(F32) * q).astype(BF16)
        w_g[rows:] = gn_ref[:, near]
        g_turned[...] = w_g[...].T
        for j in range(LANES // width):
            mine = slice(j * width, (j + 1) * width)
            base = pl.multiple_of(first // width + p * (LANES // width), LANES // width)
            taps = jnp.broadcast_to(lfr_ref[pl.ds(base + j, 1), :], (rows, rows))
            taps = pltpu.roll(taps, 0, 1, stride=1, stride_axis=0).astype(BF16)
            toeplitz = jnp.concatenate([taps, taps], 0) * mask_g[...]
            gm_turned[mine] = dot(g_turned[mine], toeplitz)
        gm = gm_turned[...].T
        heads = []
        for i in (1, 2):
            acc, sent, sums = short_stage(
                gm * joined(kv_head_ref[2 - i, :, near], local_ref[3 - i, :, near]), sf_ref[i, :, cols], x_ref[i, :, cols].astype(F32),
                edge_ref[i, :, cols].astype(F32), advance_ref, edge_shift,
            )
            qg_ref[i - 1, :, near] = acc.astype(BF16)
            tail_ref[i - 1, :, near] = acc[rows - EDGE :]
            part_ref[i - 1, :, near] = sent.astype(BF16)
            heads.append(sums)
        for k in range(blocks):
            picked = [head[:, k * CHUNK : (k + 1) * CHUNK] for head in heads]
            short_ref[p * blocks + k] = jnp.concatenate(picked, 0).astype(BF16)

    return one_step, copies


def mixer_kernel(query_first, pair_first, filled, *refs):
    shared = refs[:7]
    halves = [query_first, pair_first]
    inputs = refs[7:]
    used = 5 * sum(first is not None for first in halves)
    outs = inputs[used + filled : used + filled + 5]
    scratch = inputs[used + filled + 5 :]
    parts = []
    for first, make, size in zip(halves, (query_part, pair_part), (15, 10)):
        if first is not None:
            steps = inputs[4].shape[1] // LANES
            parts.append(make(first, shared, *inputs[:5], outs, scratch[:size]))
            inputs = inputs[5:]
            scratch = scratch[size:]
    run_steps(parts, steps)


def finish_kernel(scale, taps, got_ref, tail_ref, part_ref, qg_in, qg_hbm, long_ref, short_ref, last_ref, sem):
    rows = qg_hbm.shape[1]
    last_ref[...] = (tail_ref[...] + part_ref[...].astype(F32)).astype(BF16)
    copy = pltpu.make_async_copy(last_ref, qg_hbm.at[:, rows - EDGE :, :], sem)
    copy.start()
    total = got_ref[0].astype(F32)
    for k in range(1, got_ref.shape[0]):
        total = total + got_ref[k].astype(F32)
    total = total * scale
    for i in range(3):
        short_ref[i] = total[i * PADDED : i * PADDED + taps]
    size = total.shape[0] - 3 * PADDED
    lags = long_ref.shape[1]
    for p in range(total.shape[1] // lags):
        long_ref[p * size : (p + 1) * size] = total[3 * PADDED :, p * lags : (p + 1) * lags]
    copy.wait()


def shards(qkv, cotangent, doc_ids, short_filter, long_filter):
    _, rows, chans = qkv.shape
    groups, long_taps = long_filter.shape
    taps = short_filter.shape[2]
    devices = lax.axis_size("ctx")
    grad_scale = 1.0 / math.sqrt(rows * devices)
    packed_rows = 3 * PADDED + groups * long_taps // chans
    step_groups = LANES * groups // chans
    params = pltpu.CompilerParams(vmem_limit_bytes=24 << 20)

    ids = doc_ids.reshape(1, rows)
    sf = jnp.transpose(short_filter, (0, 2, 1))

    small = pltpu.CompilerParams(vmem_limit_bytes=8 << 20)
    edge = passed_along(qkv[:, rows - EDGE :, :], 1)
    prev_ids = passed_along(doc_ids, 1).reshape(1, rows)

    shifts = ((taps - 1) * rows, rows)
    delay, advance, lf_rev = pl.pallas_call(
        prepare_kernel,
        in_specs=[VMEM] * 2,
        out_specs=[VMEM] * 3,
        out_shape=[
            jax.ShapeDtypeStruct(shifts, BF16),
            jax.ShapeDtypeStruct(shifts, BF16),
            jax.ShapeDtypeStruct((groups, long_taps), F32),
        ],
        cost_estimate=pl.CostEstimate(flops=6_000_000_000, bytes_accessed=16_000_000, transcendentals=0),
        compiler_params=small,
        name="prepare",
    )(ids, long_filter)

    count = chans // PARTS
    after = ids
    features = []
    for part in range(PARTS):
        local = pl.pallas_call(
            functools.partial(local_kernel, part * count),
            in_specs=[VMEM] * 2 + [HBM] * 2 + [ANY],
            out_specs=VMEM,
            out_shape=jax.ShapeDtypeStruct((3, rows, count), F32),
            scratch_shapes=[
                pltpu.VMEM((3, taps, count), F32),
                pltpu.VMEM((3, rows, count), BF16),
                pltpu.SemaphoreType.DMA((2, count // LANES)),
            ],
            compiler_params=params,
            cost_estimate=pl.CostEstimate(flops=2_000_000_000, bytes_accessed=4_000_000, transcendentals=0),
            name="local",
        )(ids, delay, sf, qkv, after)
        made = [local]
        after = ids
        for streams, distance in (((1, 2), 1), ((0,), -1)):
            head, message = pl.pallas_call(
                functools.partial(message_kernel, part * count, streams),
                in_specs=[VMEM] * 6 + [ANY],
                out_specs=[VMEM] * 2,
                out_shape=[
                    jax.ShapeDtypeStruct((len(streams), EDGE, count), F32),
                    jax.ShapeDtypeStruct((rows, count), BF16),
                ],
                scratch_shapes=[pltpu.VMEM(((taps - 1) * EDGE, rows), F32)],
                compiler_params=params,
                cost_estimate=pl.CostEstimate(flops=500_000_000, bytes_accessed=1_000_000, transcendentals=0),
                name="message",
            )(ids, prev_ids, edge, sf, cotangent, local, after)
            after = message
            made += [head, passed_along(message, distance)]
        features.append(made)

    full = [
        jax.ShapeDtypeStruct((rows, chans), BF16),
        jax.ShapeDtypeStruct((3, rows, chans), BF16),
        jax.ShapeDtypeStruct((3, EDGE, chans), F32),
        jax.ShapeDtypeStruct((3, EDGE, chans), BF16),
        jax.ShapeDtypeStruct((chans // CHUNK, packed_rows, CHUNK), BF16),
    ]
    edge_scratch = pltpu.VMEM(((taps - 1) * EDGE, rows), BF16)
    query_scratch = [
        pltpu.VMEM((rows, count), BF16),
        pltpu.VMEM((rows, count), BF16),
        pltpu.VMEM((EDGE, count), F32),
        pltpu.VMEM((EDGE, count), BF16),
        pltpu.VMEM((count // CHUNK, PADDED, CHUNK), BF16),
        pltpu.VMEM((count // CHUNK, packed_rows - 3 * PADDED, CHUNK), BF16),
        edge_scratch,
        pltpu.VMEM((2 * rows, rows), BF16),
        pltpu.VMEM((rows, 2 * rows), F32),
        pltpu.VMEM((2 * rows, LANES), BF16),
        pltpu.VMEM((rows, LANES), BF16),
        pltpu.VMEM((step_groups, long_taps), F32),
        pltpu.VMEM((LANES, 2 * rows), BF16),
        pltpu.VMEM((LANES, rows), F32),
        pltpu.SemaphoreType.DMA((6, count // LANES)),
    ]
    pair_scratch = [
        pltpu.VMEM((2, rows, count), BF16),
        pltpu.VMEM((2, EDGE, count), F32),
        pltpu.VMEM((2, EDGE, count), BF16),
        pltpu.VMEM((count // CHUNK, 2 * PADDED, CHUNK), BF16),
        edge_scratch,
        pltpu.VMEM((2 * rows, rows), BF16),
        pltpu.VMEM((2 * rows, LANES), BF16),
        pltpu.VMEM((LANES, 2 * rows), BF16),
        pltpu.VMEM((LANES, rows), F32),
        pltpu.SemaphoreType.DMA((4, count // LANES)),
    ]
    results = []
    stages = [pair for stage in range(PARTS) for pair in ((stage, None), (None, stage))]
    for query, pair in stages:
        operands = [ids, prev_ids, sf, advance, qkv, cotangent, edge]
        scratch = []
        query_first = pair_first = None
        if query is not None:
            query_first = query * count
            local, kv_head, kv_prev, q_head, grad_next = features[query]
            operands += [long_filter, local, q_head, kv_head, kv_prev]
            scratch += query_scratch
        if pair is not None:
            pair_first = pair * count
            local, kv_head, kv_prev, q_head, grad_next = features[pair]
            operands += [lf_rev, local, q_head, kv_head, grad_next]
            scratch += pair_scratch
        filled = len(results)
        results = pl.pallas_call(
            functools.partial(mixer_kernel, query_first, pair_first, filled),
            in_specs=[VMEM] * len(operands) + [ANY] * filled,
            out_specs=[ANY] * 5,
            out_shape=full,
            input_output_aliases={len(operands) + k: k for k in range(filled)},
            scratch_shapes=scratch,
            compiler_params=params,
            cost_estimate=pl.CostEstimate(flops=4_000_000_000, bytes_accessed=4_000_000, transcendentals=0),
            name="query" if pair is None else "pair",
        )(*operands, *results)
    out, qg, tail, part, packed = results

    part = passed_along(part, -1)
    per = chans // devices
    if per == CHUNK:
        got = lax.all_to_all(packed, "ctx", 0, 0)
        qg, long_grad, short_grad = pl.pallas_call(
            functools.partial(finish_kernel, grad_scale, taps),
            in_specs=[VMEM, VMEM, VMEM, ANY],
            out_specs=[ANY, VMEM, VMEM],
            out_shape=[
                jax.ShapeDtypeStruct(qg.shape, BF16),
                jax.ShapeDtypeStruct((groups // devices, long_taps), F32),
                jax.ShapeDtypeStruct((3, taps, per), F32),
            ],
            input_output_aliases={3: 0},
            scratch_shapes=[pltpu.VMEM((3, EDGE, chans), BF16), pltpu.SemaphoreType.DMA],
            compiler_params=small,
            cost_estimate=pl.CostEstimate(flops=1_000_000, bytes_accessed=200_000, transcendentals=0),
            name="finish",
        )(got, tail, part, qg)
        return (out, qg, long_grad, short_grad.transpose(0, 2, 1))
    qg = lax.dynamic_update_slice(qg, (tail + part.astype(F32)).astype(BF16), (0, rows - EDGE, 0))
    head = 3 * PADDED
    short_part = packed[:, :head].transpose(1, 0, 2).reshape(head, devices, per)
    long_part = packed[:, head:].reshape(-1, packed_rows - head, CHUNK // long_taps, long_taps)
    long_part = long_part.transpose(0, 2, 1, 3).reshape(devices, -1, per)
    got = jnp.concatenate([short_part.transpose(1, 0, 2), long_part], 1)
    got = lax.all_to_all(got, "ctx", 0, 0)
    total = jnp.sum(got.astype(F32), 0) * grad_scale
    short_grad = total[:head].reshape(3, PADDED, per)[:, :taps].transpose(0, 2, 1)
    long_grad = total[head:].reshape(groups // devices, long_taps)
    return (out, qg, long_grad, short_grad)


def solution(mesh):
    in_specs = (P(None, "ctx", "tp"), P("ctx", "tp"), P("ctx"), P(None, "tp", None), P("tp", None))
    out_specs = (
        P("ctx", "tp"),
        P(None, "ctx", "tp"),
        P(("tp", "ctx"), None),
        P(None, ("tp", "ctx"), None),
    )
    return jax.shard_map(shards, mesh=mesh, in_specs=in_specs, out_specs=out_specs, check_vma=False)
```

```python
import functools
import math

import jax
import jax.numpy as jnp
from jax import lax
from jax.experimental import pallas as pl
from jax.experimental.pallas import tpu as pltpu
from jax.sharding import PartitionSpec as P

F32 = jnp.float32
BF16 = jnp.bfloat16
EDGE = 8
LANES = 512
CHUNK = 256
PADDED = 8
PARTS = 2

VMEM = pl.BlockSpec(memory_space=pltpu.VMEM)
ANY = pl.BlockSpec(memory_space=pl.ANY)
HBM = pl.BlockSpec(memory_space=pltpu.HBM)


def passed_along(block, distance):
    devices = range(lax.axis_size("ctx"))
    route = [(i - distance, i) for i in devices if i - distance in devices]
    return lax.ppermute(block, "ctx", route)


def iota2(shape, dim):
    return lax.broadcasted_iota(jnp.int32, shape, dim)


def dot(a, b):
    return jnp.dot(a, b, preferred_element_type=F32)


def lane_range(start, size):
    return pl.ds(pl.multiple_of(start, size), size)


def ones_where(cond):
    return jnp.where(cond, 1.0, 0.0)


def prepare_kernel(ids_ref, delay_ref, advance_ref):
    rows = delay_ref.shape[1]
    taps = delay_ref.shape[0] // rows + 1
    id_row = jnp.broadcast_to(ids_ref[...], (rows, rows)).astype(F32)
    same = id_row == id_row.T
    lag = iota2((rows, rows), 0) - iota2((rows, rows), 1)
    for t in range(1, taps):
        delay_ref[(t - 1) * rows : t * rows] = ones_where((lag == t) & same).astype(BF16)
        advance_ref[(t - 1) * rows : t * rows] = ones_where((lag == -t) & same).astype(BF16)


def local_kernel(first, ids_ref, delay_ref, sf_hbm, x_hbm, _, feat_ref, sf_ref, x_ref, sems):
    rows = x_ref.shape[1]
    taps = sf_ref.shape[1]
    steps = feat_ref.shape[2] // LANES

    def loads(p):
        near = lane_range(p * LANES, LANES)
        cols = lane_range(first + p * LANES, LANES)
        pairs = [
            (sf_hbm.at[:, :, cols], sf_ref.at[:, :, near]),
            (x_hbm.at[:, :, cols], x_ref.at[:, :, near]),
        ]
        return [pltpu.make_async_copy(src, dst, sems.at[k, p]) for k, (src, dst) in enumerate(pairs)]

    for p in range(steps):
        for copy in loads(p):
            copy.start()

    def one_step(p, carry):
        near = lane_range(p * LANES, LANES)
        for copy in loads(p):
            copy.wait()
        for i in range(3):
            x = x_ref[i, :, near]
            w = sf_ref[i, :, near]
            moved = dot(delay_ref[...], x)
            acc = w[0:1] * x.astype(F32)
            for t in range(1, taps):
                acc = acc + w[t : t + 1] * moved[(t - 1) * rows : t * rows]
            feat_ref[i, :, near] = acc
        return carry

    lax.fori_loop(0, steps, one_step, 0)


def message_kernel(first, streams, ids_ref, edge_ref, sf_ref, cot_ref, local_ref, _,
                   head_ref, sent_ref, edge_shift):
    rows = local_ref.shape[1]
    taps = sf_ref.shape[1]
    head_ids = jnp.broadcast_to(ids_ref[...], (rows, rows)).astype(F32).T[0:EDGE]
    before = pltpu.roll(jnp.broadcast_to(edge_ref[0, 0:1, 0:rows].astype(F32), (EDGE, rows)), EDGE, 1)
    lag = iota2((EDGE, rows), 0) + EDGE - iota2((EDGE, rows), 1)
    for t in range(1, taps):
        edge_shift[(t - 1) * EDGE : t * EDGE] = ones_where((lag == t) & (before == head_ids))
    id_wide = jnp.concatenate([ids_ref[...].astype(F32)] * (LANES // rows), 1)

    def one_step(p, carry):
        near = lane_range(p * LANES, LANES)
        cols = lane_range(first + p * LANES, LANES)
        feats = []
        for i, stream in enumerate(streams):
            w = sf_ref[stream, :, cols]
            edge = edge_ref[stream, :, cols].astype(F32)
            edge = jnp.concatenate([edge, jnp.zeros((rows - EDGE, LANES), F32)], 0)
            moved = dot(edge_shift[...].astype(BF16), edge.astype(BF16))
            head = local_ref[stream, 0:EDGE, near] + w[1:2] * moved[0:EDGE]
            for t in range(2, taps):
                head = head + w[t : t + 1] * moved[(t - 1) * EDGE : t * EDGE]
            head_ref[i, :, near] = head
            feats.append(jnp.concatenate([head, local_ref[stream, EDGE:, near]], 0))
        if len(streams) == 1:
            g = cot_ref[:, cols].astype(F32) * feats[0]
            last = iota2(g.shape, 0) == rows - 1
            sent_ref[:, near] = jnp.where(last, jnp.broadcast_to(id_wide, g.shape), g).astype(BF16)
        else:
            sent_ref[:, near] = (feats[0] * feats[1]).astype(BF16)
        return carry

    lax.fori_loop(0, sent_ref.shape[1] // LANES, one_step, 0)


def run_steps(parts, steps):
    def start(p, carry):
        for one_step, copies in parts:
            one_step(p)
            for copy in copies(p):
                copy.start()
        return carry

    def drain(p, carry):
        for _, copies in parts:
            for copy in copies(p):
                copy.wait()
        return carry

    lax.fori_loop(0, steps, start, 0)
    lax.fori_loop(0, steps, drain, 0)


def joined(head, local):
    return jnp.concatenate([head, local[EDGE:]], 0)


def edge_shifts(ids_ref, edge_ref, edge_shift):
    rows = edge_shift.shape[1]
    taps = edge_shift.shape[0] // EDGE + 1
    id_head = jnp.broadcast_to(ids_ref[...], (EDGE, rows)).astype(F32)
    prev = jnp.broadcast_to(edge_ref[0, 0:1, 0:rows].astype(F32), (rows, rows)).T
    lag = iota2((EDGE, rows), 1) + EDGE - iota2((EDGE, rows), 0)
    same = prev[rows - EDGE :] == id_head
    pieces = [ones_where((lag == t) & same) for t in range(1, taps)]
    edge_shift[...] = jnp.concatenate(pieces, 0).astype(BF16)


def short_stage(gf, w, x, xe, advance_ref, edge_shift):
    rows = gf.shape[0]
    taps = w.shape[0]
    gf_sent = gf.astype(BF16)
    moved = dot(advance_ref[...], gf_sent)
    moved_edge = dot(edge_shift[...], gf_sent)
    acc = w[0:1] * gf
    sums = [jnp.sum(x * gf, 0, keepdims=True)]
    sent = jnp.zeros((EDGE, LANES), F32)
    for t in range(1, taps):
        piece = moved[(t - 1) * rows : t * rows]
        piece_edge = moved_edge[(t - 1) * EDGE : t * EDGE]
        acc = acc + w[t : t + 1] * piece
        sent = sent + w[t : t + 1] * piece_edge
        sums.append(jnp.sum(x * piece, 0, keepdims=True) + jnp.sum(xe * piece_edge, 0, keepdims=True))
    sums.append(jnp.zeros((PADDED - taps, LANES), F32))
    return acc, sent, jnp.concatenate(sums, 0)


def query_part(first, shared, lf_ref, local_ref, q_head_ref, kv_head_ref, kvp_ref, outs, scratch):
    ids_ref, sf_ref, advance_ref, x_ref, cot_ref, edge_ref = shared
    out_hbm, qg_hbm, tail_hbm, part_hbm, packed_hbm = outs
    (out_ref, qg_ref, tail_ref, part_ref, short_ref, long_ref,
     edge_shift, mask_y, mask_a, w_kv, g_rev, dh_ref, kv_turned, y_turned, sems) = scratch
    rows = x_ref.shape[1]
    width = x_ref.shape[2] // lf_ref.shape[0]
    half = rows
    per = half // width
    lag = iota2((rows, rows), 0) - iota2((rows, rows), 1)
    mirror = ones_where(iota2((rows, rows), 0) + iota2((rows, rows), 1) == rows - 1).astype(BF16)
    id_row = jnp.broadcast_to(ids_ref[...], (rows, rows)).astype(F32)
    id_col = id_row.T
    prev_row = jnp.broadcast_to(edge_ref[0, 0:1, 0:rows].astype(F32), (rows, rows))
    same = id_row == id_col
    mask_y[0:rows] = ones_where((lag <= 0) & same).astype(BF16)
    mask_y[rows:] = ones_where((lag > 0) & (prev_row.T == id_row)).astype(BF16)
    mask_a[:, 0:rows] = dot(mirror, ones_where((lag >= 0) & same).astype(BF16))
    mask_a[:, rows:] = dot(mirror, ones_where((lag < 0) & (prev_row == id_col)).astype(BF16))
    edge_shifts(ids_ref, edge_ref, edge_shift)
    owner = iota2((rows, half), 1) // width
    blocks = LANES // CHUNK
    head = 3 * PADDED

    def copies(p):
        near = lane_range(p * LANES, LANES)
        cols = lane_range(first + p * LANES, LANES)
        here = pl.ds(p * blocks, blocks)
        there = pl.ds(first // CHUNK + p * blocks, blocks)
        pairs = [
            (out_ref.at[:, near], out_hbm.at[:, cols]),
            (qg_ref.at[:, near], qg_hbm.at[0, :, cols]),
            (tail_ref.at[:, near], tail_hbm.at[0, :, cols]),
            (part_ref.at[:, near], part_hbm.at[0, :, cols]),
            (short_ref.at[here], packed_hbm.at[there, 0:PADDED]),
            (long_ref.at[here], packed_hbm.at[there, head:]),
        ]
        return [pltpu.make_async_copy(src, dst, sems.at[k, p]) for k, (src, dst) in enumerate(pairs)]

    def one_step(p):
        near = lane_range(p * LANES, LANES)
        cols = lane_range(first + p * LANES, LANES)
        cot = cot_ref[:, cols].astype(F32)
        q = joined(q_head_ref[0, :, near], local_ref[0, :, near])
        k = joined(kv_head_ref[0, :, near], local_ref[1, :, near])
        v = joined(kv_head_ref[1, :, near], local_ref[2, :, near])
        w_kv[0:rows] = (k * v).astype(BF16)
        w_kv[rows:] = kvp_ref[:, near]
        kv_turned[...] = w_kv[...].T
        g_rev[...] = dot(mirror, (cot * q).astype(BF16)).astype(BF16)
        for h in range(LANES // half):
            part = slice(h * half, (h + 1) * half)
            base = pl.multiple_of((first // half) * per + p * (LANES // width) + h * per, per)
            for j in range(per):
                mine = slice((h * per + j) * width, (h * per + j + 1) * width)
                taps = jnp.broadcast_to(lf_ref[pl.ds(base + j, 1), :], (rows, rows))
                taps = pltpu.roll(taps, 0, 1, stride=1, stride_axis=0).astype(BF16)
                toeplitz = jnp.concatenate([taps, taps], 0) * mask_y[...]
                y_turned[mine] = dot(kv_turned[mine], toeplitz)
                g_sel = jnp.where(owner == j, g_rev[:, part], jnp.zeros((rows, half), BF16))
                cross = dot(g_sel, kv_turned[part, :]) * mask_a[...]
                folded = cross[:, 0:rows] + cross[:, rows:]
                folded = pltpu.roll(folded, 0, 1, stride=1, stride_axis=0)
                dh_ref[h * per + j : h * per + j + 1] = jnp.sum(folded, 0, keepdims=True)
        dh = dot(dh_ref[...].astype(BF16), mirror)
        y = y_turned[...].T
        out_ref[:, near] = (q * y).astype(BF16)
        acc, sent, sums = short_stage(
            cot * y, sf_ref[0, :, cols], x_ref[0, :, cols].astype(F32), edge_ref[0, :, cols].astype(F32),
            advance_ref, edge_shift,
        )
        qg_ref[:, near] = acc.astype(BF16)
        tail_ref[:, near] = acc[rows - EDGE :]
        part_ref[:, near] = sent.astype(BF16)
        size = dh.shape[0] * rows // LANES
        for k in range(blocks):
            short_ref[p * blocks + k] = sums[:, k * CHUNK : (k + 1) * CHUNK].astype(BF16)
            lines = range(k * (CHUNK // rows), (k + 1) * (CHUNK // rows))
            long_ref[p * blocks + k] = jnp.concatenate([dh[e * size : (e + 1) * size] for e in lines], 1).astype(BF16)

    return one_step, copies


def pair_part(first, shared, lf_ref, local_ref, q_head_ref, kv_head_ref, gn_ref, outs, scratch):
    ids_ref, sf_ref, advance_ref, x_ref, cot_ref, edge_ref = shared
    _, qg_hbm, tail_hbm, part_hbm, packed_hbm = outs
    (qg_ref, tail_ref, part_ref, short_ref,
     edge_shift, mask_g, w_g, g_turned, gm_turned, lfr_ref, sems) = scratch
    rows = x_ref.shape[1]
    width = x_ref.shape[2] // lfr_ref.shape[0]
    lag = iota2((rows, rows), 0) - iota2((rows, rows), 1)
    id_row = jnp.broadcast_to(ids_ref[...], (rows, rows)).astype(F32)
    next_col = jnp.broadcast_to(gn_ref[rows - 1 : rows, 0:rows].astype(F32), (rows, rows)).T
    backward = ones_where((iota2((rows, rows), 0) + iota2((rows, rows), 1)) % rows == 0)
    lfr_ref[...] = dot(lf_ref[...].astype(BF16), backward.astype(BF16))
    mask_g[0:rows] = ones_where((lag >= 0) & (id_row == id_row.T)).astype(BF16)
    mask_g[rows:] = ones_where((lag < 0) & (next_col == id_row)).astype(BF16)
    edge_shifts(ids_ref, edge_ref, edge_shift)
    blocks = LANES // CHUNK

    def copies(p):
        near = lane_range(p * LANES, LANES)
        cols = lane_range(first + p * LANES, LANES)
        pairs = [
            (qg_ref.at[:, :, near], qg_hbm.at[1:3, :, cols]),
            (tail_ref.at[:, :, near], tail_hbm.at[1:3, :, cols]),
            (part_ref.at[:, :, near], part_hbm.at[1:3, :, cols]),
            (
                short_ref.at[pl.ds(p * blocks, blocks)],
                packed_hbm.at[pl.ds(first // CHUNK + p * blocks, blocks), PADDED : 3 * PADDED],
            ),
        ]
        return [pltpu.make_async_copy(src, dst, sems.at[k, p]) for k, (src, dst) in enumerate(pairs)]

    def one_step(p):
        near = lane_range(p * LANES, LANES)
        cols = lane_range(first + p * LANES, LANES)
        q = joined(q_head_ref[0, :, near], local_ref[0, :, near])
        w_g[0:rows] = (cot_ref[:, cols].astype(F32) * q).astype(BF16)
        w_g[rows:] = gn_ref[:, near]
        g_turned[...] = w_g[...].T
        for j in range(LANES // width):
            mine = slice(j * width, (j + 1) * width)
            base = pl.multiple_of(first // width + p * (LANES // width), LANES // width)
            taps = jnp.broadcast_to(lfr_ref[pl.ds(base + j, 1), :], (rows, rows))
            taps = pltpu.roll(taps, 0, 1, stride=1, stride_axis=0).astype(BF16)
            toeplitz = jnp.concatenate([taps, taps], 0) * mask_g[...]
            gm_turned[mine] = dot(g_turned[mine], toeplitz)
        gm = gm_turned[...].T
        heads = []
        for i in (1, 2):
            acc, sent, sums = short_stage(
                gm * joined(kv_head_ref[2 - i, :, near], local_ref[3 - i, :, near]), sf_ref[i, :, cols], x_ref[i, :, cols].astype(F32),
                edge_ref[i, :, cols].astype(F32), advance_ref, edge_shift,
            )
            qg_ref[i - 1, :, near] = acc.astype(BF16)
            tail_ref[i - 1, :, near] = acc[rows - EDGE :]
            part_ref[i - 1, :, near] = sent.astype(BF16)
            heads.append(sums)
        for k in range(blocks):
            picked = [head[:, k * CHUNK : (k + 1) * CHUNK] for head in heads]
            short_ref[p * blocks + k] = jnp.concatenate(picked, 0).astype(BF16)

    return one_step, copies


def mixer_kernel(query_first, pair_first, filled, *refs):
    shared = refs[:6]
    halves = [query_first, pair_first]
    inputs = refs[6:]
    used = 5 * sum(first is not None for first in halves)
    outs = inputs[used + filled : used + filled + 5]
    scratch = inputs[used + filled + 5 :]
    parts = []
    for first, make, size in zip(halves, (query_part, pair_part), (15, 11)):
        if first is not None:
            steps = inputs[4].shape[1] // LANES
            parts.append(make(first, shared, *inputs[:5], outs, scratch[:size]))
            inputs = inputs[5:]
            scratch = scratch[size:]
    run_steps(parts, steps)


def last_rows_kernel(tail_ref, part_ref, qg_in, _, qg_hbm, last_ref, sem):
    rows = qg_hbm.shape[1]
    last_ref[...] = (tail_ref[...] + part_ref[...].astype(F32)).astype(BF16)
    copy = pltpu.make_async_copy(last_ref, qg_hbm.at[:, rows - EDGE :, :], sem)
    copy.start()
    copy.wait()


def total_kernel(scale, taps, got_ref, long_ref, short_ref):
    total = got_ref[0].astype(F32)
    for k in range(1, got_ref.shape[0]):
        total = total + got_ref[k].astype(F32)
    total = total * scale
    for i in range(3):
        short_ref[i] = total[i * PADDED : i * PADDED + taps]
    size = total.shape[0] - 3 * PADDED
    lags = long_ref.shape[1]
    for p in range(total.shape[1] // lags):
        long_ref[p * size : (p + 1) * size] = total[3 * PADDED :, p * lags : (p + 1) * lags]


def shards(qkv, cotangent, doc_ids, short_filter, long_filter):
    _, rows, chans = qkv.shape
    groups, long_taps = long_filter.shape
    taps = short_filter.shape[2]
    devices = lax.axis_size("ctx")
    grad_scale = 1.0 / math.sqrt(rows * devices)
    packed_rows = 3 * PADDED + groups * long_taps // chans
    step_groups = LANES * groups // chans
    params = pltpu.CompilerParams(vmem_limit_bytes=24 << 20)

    ids = doc_ids.reshape(1, rows)
    sf = jnp.transpose(short_filter, (0, 2, 1))

    small = pltpu.CompilerParams(vmem_limit_bytes=8 << 20)
    edge = qkv[:, rows - EDGE :, :]
    edge = passed_along(edge.at[0, 0, :rows].set(doc_ids.astype(BF16)), 1)

    shifts = ((taps - 1) * rows, rows)
    delay, advance = pl.pallas_call(
        prepare_kernel,
        in_specs=[VMEM],
        out_specs=[VMEM] * 2,
        out_shape=[jax.ShapeDtypeStruct(shifts, BF16), jax.ShapeDtypeStruct(shifts, BF16)],
        cost_estimate=pl.CostEstimate(flops=6_000_000_000, bytes_accessed=16_000_000, transcendentals=0),
        compiler_params=small,
        name="prepare",
    )(ids)

    count = chans // PARTS
    after = ids
    features = []
    for part in range(PARTS):
        local = pl.pallas_call(
            functools.partial(local_kernel, part * count),
            in_specs=[VMEM] * 2 + [HBM] * 2 + [ANY],
            out_specs=VMEM,
            out_shape=jax.ShapeDtypeStruct((3, rows, count), F32),
            scratch_shapes=[
                pltpu.VMEM((3, taps, count), F32),
                pltpu.VMEM((3, rows, count), BF16),
                pltpu.SemaphoreType.DMA((2, count // LANES)),
            ],
            compiler_params=params,
            cost_estimate=pl.CostEstimate(flops=2_000_000_000, bytes_accessed=4_000_000, transcendentals=0),
            name="local",
        )(ids, delay, sf, qkv, after)
        made = [local]
        after = ids
        for streams, distance in (((1, 2), 1), ((0,), -1)):
            head, message = pl.pallas_call(
                functools.partial(message_kernel, part * count, streams),
                in_specs=[VMEM] * 5 + [ANY],
                out_specs=[VMEM] * 2,
                out_shape=[
                    jax.ShapeDtypeStruct((len(streams), EDGE, count), F32),
                    jax.ShapeDtypeStruct((rows, count), BF16),
                ],
                scratch_shapes=[pltpu.VMEM(((taps - 1) * EDGE, rows), F32)],
                compiler_params=params,
                cost_estimate=pl.CostEstimate(flops=500_000_000, bytes_accessed=1_000_000, transcendentals=0),
                name="message",
            )(ids, edge, sf, cotangent, local, after)
            after = message
            made += [head, passed_along(message, distance)]
        features.append(made)

    full = [
        jax.ShapeDtypeStruct((rows, chans), BF16),
        jax.ShapeDtypeStruct((3, rows, chans), BF16),
        jax.ShapeDtypeStruct((3, EDGE, chans), F32),
        jax.ShapeDtypeStruct((3, EDGE, chans), BF16),
        jax.ShapeDtypeStruct((chans // CHUNK, packed_rows, CHUNK), BF16),
    ]
    edge_scratch = pltpu.VMEM(((taps - 1) * EDGE, rows), BF16)
    query_scratch = [
        pltpu.VMEM((rows, count), BF16),
        pltpu.VMEM((rows, count), BF16),
        pltpu.VMEM((EDGE, count), F32),
        pltpu.VMEM((EDGE, count), BF16),
        pltpu.VMEM((count // CHUNK, PADDED, CHUNK), BF16),
        pltpu.VMEM((count // CHUNK, packed_rows - 3 * PADDED, CHUNK), BF16),
        edge_scratch,
        pltpu.VMEM((2 * rows, rows), BF16),
        pltpu.VMEM((rows, 2 * rows), F32),
        pltpu.VMEM((2 * rows, LANES), BF16),
        pltpu.VMEM((rows, LANES), BF16),
        pltpu.VMEM((step_groups, long_taps), F32),
        pltpu.VMEM((LANES, 2 * rows), BF16),
        pltpu.VMEM((LANES, rows), F32),
        pltpu.SemaphoreType.DMA((6, count // LANES)),
    ]
    pair_scratch = [
        pltpu.VMEM((2, rows, count), BF16),
        pltpu.VMEM((2, EDGE, count), F32),
        pltpu.VMEM((2, EDGE, count), BF16),
        pltpu.VMEM((count // CHUNK, 2 * PADDED, CHUNK), BF16),
        edge_scratch,
        pltpu.VMEM((2 * rows, rows), BF16),
        pltpu.VMEM((2 * rows, LANES), BF16),
        pltpu.VMEM((LANES, 2 * rows), BF16),
        pltpu.VMEM((LANES, rows), F32),
        pltpu.VMEM((groups, long_taps), F32),
        pltpu.SemaphoreType.DMA((4, count // LANES)),
    ]
    results = []
    stages = [pair for stage in range(PARTS) for pair in ((stage, None), (None, stage))]
    for query, pair in stages:
        operands = [ids, sf, advance, qkv, cotangent, edge]
        scratch = []
        query_first = pair_first = None
        if query is not None:
            query_first = query * count
            local, kv_head, kv_prev, q_head, grad_next = features[query]
            operands += [long_filter, local, q_head, kv_head, kv_prev]
            scratch += query_scratch
        if pair is not None:
            pair_first = pair * count
            local, kv_head, kv_prev, q_head, grad_next = features[pair]
            operands += [long_filter, local, q_head, kv_head, grad_next]
            scratch += pair_scratch
        filled = len(results)
        results = pl.pallas_call(
            functools.partial(mixer_kernel, query_first, pair_first, filled),
            in_specs=[VMEM] * len(operands) + [ANY] * filled,
            out_specs=[ANY] * 5,
            out_shape=full,
            input_output_aliases={len(operands) + k: k for k in range(filled)},
            scratch_shapes=scratch,
            compiler_params=params,
            cost_estimate=pl.CostEstimate(flops=4_000_000_000, bytes_accessed=4_000_000, transcendentals=0),
            name="query" if pair is None else "pair",
        )(*operands, *results)
    out, qg, tail, part, packed = results

    part = passed_along(part, -1)
    per = chans // devices
    if per == CHUNK:
        got = lax.all_to_all(packed, "ctx", 0, 0)
        long_grad, short_grad = pl.pallas_call(
            functools.partial(total_kernel, grad_scale, taps),
            in_specs=[VMEM],
            out_specs=[VMEM] * 2,
            out_shape=[
                jax.ShapeDtypeStruct((groups // devices, long_taps), F32),
                jax.ShapeDtypeStruct((3, taps, per), F32),
            ],
            compiler_params=small,
            cost_estimate=pl.CostEstimate(flops=1_000_000, bytes_accessed=200_000, transcendentals=0),
            name="total",
        )(got)
        short_grad = short_grad.transpose(0, 2, 1)
    else:
        head = 3 * PADDED
        short_part = packed[:, :head].transpose(1, 0, 2).reshape(head, devices, per)
        long_part = packed[:, head:].reshape(-1, packed_rows - head, CHUNK // long_taps, long_taps)
        long_part = long_part.transpose(0, 2, 1, 3).reshape(devices, -1, per)
        got = jnp.concatenate([short_part.transpose(1, 0, 2), long_part], 1)
        got = lax.all_to_all(got, "ctx", 0, 0)
        total = jnp.sum(got.astype(F32), 0) * grad_scale
        short_grad = total[:head].reshape(3, PADDED, per)[:, :taps].transpose(0, 2, 1)
        long_grad = total[head:].reshape(groups // devices, long_taps)
    qg = pl.pallas_call(
        last_rows_kernel,
        in_specs=[VMEM, VMEM, ANY, ANY],
        out_specs=ANY,
        out_shape=jax.ShapeDtypeStruct(qg.shape, BF16),
        input_output_aliases={2: 0},
        scratch_shapes=[pltpu.VMEM((3, EDGE, chans), BF16), pltpu.SemaphoreType.DMA],
        compiler_params=small,
        cost_estimate=pl.CostEstimate(flops=100_000, bytes_accessed=200_000, transcendentals=0),
        name="last_rows",
    )(tail, part, qg, got)
    return (out, qg, long_grad, short_grad)


def solution(mesh):
    in_specs = (P(None, "ctx", "tp"), P("ctx", "tp"), P("ctx"), P(None, "tp", None), P("tp", None))
    out_specs = (
        P("ctx", "tp"),
        P(None, "ctx", "tp"),
        P(("tp", "ctx"), None),
        P(None, ("tp", "ctx"), None),
    )
    return jax.shard_map(shards, mesh=mesh, in_specs=in_specs, out_specs=out_specs, check_vma=False)
```

```python
import functools
import math

import jax
import jax.numpy as jnp
from jax import lax
from jax.experimental import pallas as pl
from jax.experimental.pallas import tpu as pltpu
from jax.sharding import PartitionSpec as P

F32 = jnp.float32
BF16 = jnp.bfloat16
EDGE = 8
LANES = 512
CHUNK = 256
PADDED = 8
PARTS = 2

VMEM = pl.BlockSpec(memory_space=pltpu.VMEM)
ANY = pl.BlockSpec(memory_space=pl.ANY)
HBM = pl.BlockSpec(memory_space=pltpu.HBM)


def passed_along(block, distance):
    devices = range(lax.axis_size("ctx"))
    route = [(i - distance, i) for i in devices if i - distance in devices]
    return lax.ppermute(block, "ctx", route)


def iota2(shape, dim):
    return lax.broadcasted_iota(jnp.int32, shape, dim)


def dot(a, b):
    return jnp.dot(a, b, preferred_element_type=F32)


def lane_range(start, size):
    return pl.ds(pl.multiple_of(start, size), size)


def ones_where(cond):
    return jnp.where(cond, 1.0, 0.0)


def prepare_kernel(ids_ref, delay_ref, advance_ref):
    rows = delay_ref.shape[1]
    taps = delay_ref.shape[0] // rows + 1
    id_row = jnp.broadcast_to(ids_ref[...], (rows, rows)).astype(F32)
    same = id_row == id_row.T
    lag = iota2((rows, rows), 0) - iota2((rows, rows), 1)
    for t in range(1, taps):
        delay_ref[(t - 1) * rows : t * rows] = ones_where((lag == t) & same).astype(BF16)
        advance_ref[(t - 1) * rows : t * rows] = ones_where((lag == -t) & same).astype(BF16)


def local_kernel(first, ids_ref, delay_ref, sf_hbm, x_hbm, _, feat_ref, sf_ref, x_ref, sems):
    rows = x_ref.shape[1]
    taps = sf_ref.shape[1]
    steps = feat_ref.shape[2] // LANES

    def loads(p):
        near = lane_range(p * LANES, LANES)
        cols = lane_range(first + p * LANES, LANES)
        pairs = [
            (sf_hbm.at[:, :, cols], sf_ref.at[:, :, near]),
            (x_hbm.at[:, :, cols], x_ref.at[:, :, near]),
        ]
        return [pltpu.make_async_copy(src, dst, sems.at[k, p]) for k, (src, dst) in enumerate(pairs)]

    for p in range(steps):
        for copy in loads(p):
            copy.start()

    def one_step(p):
        near = lane_range(p * LANES, LANES)
        for copy in loads(p):
            copy.wait()
        for i in range(3):
            x = x_ref[i, :, near]
            w = sf_ref[i, :, near]
            moved = dot(delay_ref[...], x)
            acc = w[0:1] * x.astype(F32)
            for t in range(1, taps):
                acc = acc + w[t : t + 1] * moved[(t - 1) * rows : t * rows]
            feat_ref[i, :, near] = acc

    for p in range(steps):
        one_step(p)


def message_kernel(first, streams, ids_ref, edge_ref, sf_ref, cot_ref, local_ref, _,
                   head_ref, sent_ref, edge_shift):
    rows = local_ref.shape[1]
    taps = sf_ref.shape[1]
    head_ids = jnp.broadcast_to(ids_ref[...], (rows, rows)).astype(F32).T[0:EDGE]
    before = pltpu.roll(jnp.broadcast_to(edge_ref[0, 0:1, 0:rows].astype(F32), (EDGE, rows)), EDGE, 1)
    lag = iota2((EDGE, rows), 0) + EDGE - iota2((EDGE, rows), 1)
    for t in range(1, taps):
        edge_shift[(t - 1) * EDGE : t * EDGE] = ones_where((lag == t) & (before == head_ids))
    id_wide = jnp.concatenate([ids_ref[...].astype(F32)] * (LANES // rows), 1)

    def one_step(p):
        near = lane_range(p * LANES, LANES)
        cols = lane_range(first + p * LANES, LANES)
        feats = []
        for i, stream in enumerate(streams):
            w = sf_ref[stream, :, cols]
            edge = edge_ref[stream, :, cols].astype(F32)
            edge = jnp.concatenate([edge, jnp.zeros((rows - EDGE, LANES), F32)], 0)
            moved = dot(edge_shift[...].astype(BF16), edge.astype(BF16))
            head = local_ref[stream, 0:EDGE, near] + w[1:2] * moved[0:EDGE]
            for t in range(2, taps):
                head = head + w[t : t + 1] * moved[(t - 1) * EDGE : t * EDGE]
            head_ref[i, :, near] = head
            feats.append(jnp.concatenate([head, local_ref[stream, EDGE:, near]], 0))
        if len(streams) == 1:
            g = cot_ref[:, cols].astype(F32) * feats[0]
            last = iota2(g.shape, 0) == rows - 1
            sent_ref[:, near] = jnp.where(last, jnp.broadcast_to(id_wide, g.shape), g).astype(BF16)
        else:
            sent_ref[:, near] = (feats[0] * feats[1]).astype(BF16)

    for p in range(sent_ref.shape[1] // LANES):
        one_step(p)


def run_steps(parts, steps):
    for p in range(steps):
        for one_step, copies in parts:
            one_step(p)
            for copy in copies(p):
                copy.start()
    for p in range(steps):
        for _, copies in parts:
            for copy in copies(p):
                copy.wait()


def joined(head, local):
    return jnp.concatenate([head, local[EDGE:]], 0)


def edge_shifts(ids_ref, edge_ref, edge_shift):
    rows = edge_shift.shape[1]
    taps = edge_shift.shape[0] // EDGE + 1
    id_head = jnp.broadcast_to(ids_ref[...], (EDGE, rows)).astype(F32)
    prev = jnp.broadcast_to(edge_ref[0, 0:1, 0:rows].astype(F32), (rows, rows)).T
    lag = iota2((EDGE, rows), 1) + EDGE - iota2((EDGE, rows), 0)
    same = prev[rows - EDGE :] == id_head
    pieces = [ones_where((lag == t) & same) for t in range(1, taps)]
    edge_shift[...] = jnp.concatenate(pieces, 0).astype(BF16)


def short_stage(gf, w, x, xe, advance_ref, edge_shift):
    rows = gf.shape[0]
    taps = w.shape[0]
    gf_sent = gf.astype(BF16)
    moved = dot(advance_ref[...], gf_sent)
    moved_edge = dot(edge_shift[...], gf_sent)
    acc = w[0:1] * gf
    sums = [jnp.sum(x * gf, 0, keepdims=True)]
    sent = jnp.zeros((EDGE, LANES), F32)
    for t in range(1, taps):
        piece = moved[(t - 1) * rows : t * rows]
        piece_edge = moved_edge[(t - 1) * EDGE : t * EDGE]
        acc = acc + w[t : t + 1] * piece
        sent = sent + w[t : t + 1] * piece_edge
        sums.append(jnp.sum(x * piece, 0, keepdims=True) + jnp.sum(xe * piece_edge, 0, keepdims=True))
    sums.append(jnp.zeros((PADDED - taps, LANES), F32))
    return acc, sent, jnp.concatenate(sums, 0)


def query_part(first, shared, lf_ref, local_ref, q_head_ref, kv_head_ref, kvp_ref, outs, scratch):
    ids_ref, sf_ref, advance_ref, x_ref, cot_ref, edge_ref = shared
    out_hbm, qg_hbm, tail_hbm, part_hbm, packed_hbm = outs
    (out_ref, qg_ref, tail_ref, part_ref, short_ref, long_ref,
     edge_shift, mask_y, mask_a, w_kv, g_rev, dh_ref, kv_turned, y_turned, sems) = scratch
    rows = x_ref.shape[1]
    width = x_ref.shape[2] // lf_ref.shape[0]
    half = rows
    per = half // width
    lag = iota2((rows, rows), 0) - iota2((rows, rows), 1)
    mirror = ones_where(iota2((rows, rows), 0) + iota2((rows, rows), 1) == rows - 1).astype(BF16)
    id_row = jnp.broadcast_to(ids_ref[...], (rows, rows)).astype(F32)
    id_col = id_row.T
    prev_row = jnp.broadcast_to(edge_ref[0, 0:1, 0:rows].astype(F32), (rows, rows))
    same = id_row == id_col
    mask_y[0:rows] = ones_where((lag <= 0) & same).astype(BF16)
    mask_y[rows:] = ones_where((lag > 0) & (prev_row.T == id_row)).astype(BF16)
    mask_a[:, 0:rows] = dot(mirror, ones_where((lag >= 0) & same).astype(BF16))
    mask_a[:, rows:] = dot(mirror, ones_where((lag < 0) & (prev_row == id_col)).astype(BF16))
    edge_shifts(ids_ref, edge_ref, edge_shift)
    owner = iota2((rows, half), 1) // width
    blocks = LANES // CHUNK
    head = 3 * PADDED

    def copies(p):
        near = lane_range(p * LANES, LANES)
        cols = lane_range(first + p * LANES, LANES)
        here = pl.ds(p * blocks, blocks)
        there = pl.ds(first // CHUNK + p * blocks, blocks)
        pairs = [
            (out_ref.at[:, near], out_hbm.at[:, cols]),
            (qg_ref.at[:, near], qg_hbm.at[0, :, cols]),
            (tail_ref.at[:, near], tail_hbm.at[0, :, cols]),
            (part_ref.at[:, near], part_hbm.at[0, :, cols]),
            (short_ref.at[here], packed_hbm.at[there, 0:PADDED]),
            (long_ref.at[here], packed_hbm.at[there, head:]),
        ]
        return [pltpu.make_async_copy(src, dst, sems.at[k, p]) for k, (src, dst) in enumerate(pairs)]

    def one_step(p):
        near = lane_range(p * LANES, LANES)
        cols = lane_range(first + p * LANES, LANES)
        cot = cot_ref[:, cols].astype(F32)
        q = joined(q_head_ref[0, :, near], local_ref[0, :, near])
        k = joined(kv_head_ref[0, :, near], local_ref[1, :, near])
        v = joined(kv_head_ref[1, :, near], local_ref[2, :, near])
        w_kv[0:rows] = (k * v).astype(BF16)
        w_kv[rows:] = kvp_ref[:, near]
        kv_turned[...] = w_kv[...].T
        g_rev[...] = dot(mirror, (cot * q).astype(BF16)).astype(BF16)
        for h in range(LANES // half):
            part = slice(h * half, (h + 1) * half)
            base = pl.multiple_of((first // half) * per + p * (LANES // width) + h * per, per)
            for j in range(per):
                mine = slice((h * per + j) * width, (h * per + j + 1) * width)
                taps = jnp.broadcast_to(lf_ref[pl.ds(base + j, 1), :], (rows, rows))
                taps = pltpu.roll(taps, 0, 1, stride=1, stride_axis=0).astype(BF16)
                toeplitz = jnp.concatenate([taps, taps], 0) * mask_y[...]
                y_turned[mine] = dot(kv_turned[mine], toeplitz)
                g_sel = jnp.where(owner == j, g_rev[:, part], jnp.zeros((rows, half), BF16))
                cross = dot(g_sel, kv_turned[part, :]) * mask_a[...]
                folded = cross[:, 0:rows] + cross[:, rows:]
                folded = pltpu.roll(folded, 0, 1, stride=1, stride_axis=0)
                dh_ref[h * per + j : h * per + j + 1] = jnp.sum(folded, 0, keepdims=True)
        dh = dot(dh_ref[...].astype(BF16), mirror)
        y = y_turned[...].T
        out_ref[:, near] = (q * y).astype(BF16)
        acc, sent, sums = short_stage(
            cot * y, sf_ref[0, :, cols], x_ref[0, :, cols].astype(F32), edge_ref[0, :, cols].astype(F32),
            advance_ref, edge_shift,
        )
        qg_ref[:, near] = acc.astype(BF16)
        tail_ref[:, near] = acc[rows - EDGE :]
        part_ref[:, near] = sent.astype(BF16)
        size = dh.shape[0] * rows // LANES
        for k in range(blocks):
            short_ref[p * blocks + k] = sums[:, k * CHUNK : (k + 1) * CHUNK].astype(BF16)
            lines = range(k * (CHUNK // rows), (k + 1) * (CHUNK // rows))
            long_ref[p * blocks + k] = jnp.concatenate([dh[e * size : (e + 1) * size] for e in lines], 1).astype(BF16)

    return one_step, copies


def pair_part(first, shared, lf_ref, local_ref, q_head_ref, kv_head_ref, gn_ref, outs, scratch):
    ids_ref, sf_ref, advance_ref, x_ref, cot_ref, edge_ref = shared
    _, qg_hbm, tail_hbm, part_hbm, packed_hbm = outs
    (qg_ref, tail_ref, part_ref, short_ref,
     edge_shift, mask_g, w_g, g_turned, gm_turned, lfr_ref, sems) = scratch
    rows = x_ref.shape[1]
    width = x_ref.shape[2] // lfr_ref.shape[0]
    lag = iota2((rows, rows), 0) - iota2((rows, rows), 1)
    id_row = jnp.broadcast_to(ids_ref[...], (rows, rows)).astype(F32)
    next_col = jnp.broadcast_to(gn_ref[rows - 1 : rows, 0:rows].astype(F32), (rows, rows)).T
    backward = ones_where((iota2((rows, rows), 0) + iota2((rows, rows), 1)) % rows == 0)
    lfr_ref[...] = dot(lf_ref[...].astype(BF16), backward.astype(BF16))
    mask_g[0:rows] = ones_where((lag >= 0) & (id_row == id_row.T)).astype(BF16)
    mask_g[rows:] = ones_where((lag < 0) & (next_col == id_row)).astype(BF16)
    edge_shifts(ids_ref, edge_ref, edge_shift)
    blocks = LANES // CHUNK

    def copies(p):
        near = lane_range(p * LANES, LANES)
        cols = lane_range(first + p * LANES, LANES)
        pairs = [
            (qg_ref.at[:, :, near], qg_hbm.at[1:3, :, cols]),
            (tail_ref.at[:, :, near], tail_hbm.at[1:3, :, cols]),
            (part_ref.at[:, :, near], part_hbm.at[1:3, :, cols]),
            (
                short_ref.at[pl.ds(p * blocks, blocks)],
                packed_hbm.at[pl.ds(first // CHUNK + p * blocks, blocks), PADDED : 3 * PADDED],
            ),
        ]
        return [pltpu.make_async_copy(src, dst, sems.at[k, p]) for k, (src, dst) in enumerate(pairs)]

    def one_step(p):
        near = lane_range(p * LANES, LANES)
        cols = lane_range(first + p * LANES, LANES)
        q = joined(q_head_ref[0, :, near], local_ref[0, :, near])
        w_g[0:rows] = (cot_ref[:, cols].astype(F32) * q).astype(BF16)
        w_g[rows:] = gn_ref[:, near]
        g_turned[...] = w_g[...].T
        for j in range(LANES // width):
            mine = slice(j * width, (j + 1) * width)
            base = pl.multiple_of(first // width + p * (LANES // width), LANES // width)
            taps = jnp.broadcast_to(lfr_ref[pl.ds(base + j, 1), :], (rows, rows))
            taps = pltpu.roll(taps, 0, 1, stride=1, stride_axis=0).astype(BF16)
            toeplitz = jnp.concatenate([taps, taps], 0) * mask_g[...]
            gm_turned[mine] = dot(g_turned[mine], toeplitz)
        gm = gm_turned[...].T
        heads = []
        for i in (1, 2):
            acc, sent, sums = short_stage(
                gm * joined(kv_head_ref[2 - i, :, near], local_ref[3 - i, :, near]), sf_ref[i, :, cols], x_ref[i, :, cols].astype(F32),
                edge_ref[i, :, cols].astype(F32), advance_ref, edge_shift,
            )
            qg_ref[i - 1, :, near] = acc.astype(BF16)
            tail_ref[i - 1, :, near] = acc[rows - EDGE :]
            part_ref[i - 1, :, near] = sent.astype(BF16)
            heads.append(sums)
        for k in range(blocks):
            picked = [head[:, k * CHUNK : (k + 1) * CHUNK] for head in heads]
            short_ref[p * blocks + k] = jnp.concatenate(picked, 0).astype(BF16)

    return one_step, copies


def mixer_kernel(query_first, pair_first, filled, *refs):
    shared = refs[:6]
    halves = [query_first, pair_first]
    inputs = refs[6:]
    used = 5 * sum(first is not None for first in halves)
    outs = inputs[used + filled : used + filled + 5]
    scratch = inputs[used + filled + 5 :]
    parts = []
    for first, make, size in zip(halves, (query_part, pair_part), (15, 11)):
        if first is not None:
            steps = inputs[4].shape[1] // LANES
            parts.append(make(first, shared, *inputs[:5], outs, scratch[:size]))
            inputs = inputs[5:]
            scratch = scratch[size:]
    run_steps(parts, steps)


def last_rows_kernel(tail_ref, part_ref, qg_in, _, qg_hbm, last_ref, sem):
    rows = qg_hbm.shape[1]
    last_ref[...] = (tail_ref[...] + part_ref[...].astype(F32)).astype(BF16)
    copy = pltpu.make_async_copy(last_ref, qg_hbm.at[:, rows - EDGE :, :], sem)
    copy.start()
    copy.wait()


def total_kernel(scale, taps, got_ref, long_ref, short_ref):
    total = got_ref[0].astype(F32)
    for k in range(1, got_ref.shape[0]):
        total = total + got_ref[k].astype(F32)
    total = total * scale
    for i in range(3):
        short_ref[i] = total[i * PADDED : i * PADDED + taps]
    size = total.shape[0] - 3 * PADDED
    lags = long_ref.shape[1]
    for p in range(total.shape[1] // lags):
        long_ref[p * size : (p + 1) * size] = total[3 * PADDED :, p * lags : (p + 1) * lags]


def shards(qkv, cotangent, doc_ids, short_filter, long_filter):
    _, rows, chans = qkv.shape
    groups, long_taps = long_filter.shape
    taps = short_filter.shape[2]
    devices = lax.axis_size("ctx")
    grad_scale = 1.0 / math.sqrt(rows * devices)
    packed_rows = 3 * PADDED + groups * long_taps // chans
    step_groups = LANES * groups // chans
    params = pltpu.CompilerParams(vmem_limit_bytes=24 << 20)

    ids = doc_ids.reshape(1, rows)
    sf = jnp.transpose(short_filter, (0, 2, 1))

    small = pltpu.CompilerParams(vmem_limit_bytes=8 << 20)
    edge = qkv[:, rows - EDGE :, :]
    edge = passed_along(edge.at[0, 0, :rows].set(doc_ids.astype(BF16)), 1)

    shifts = ((taps - 1) * rows, rows)
    delay, advance = pl.pallas_call(
        prepare_kernel,
        in_specs=[VMEM],
        out_specs=[VMEM] * 2,
        out_shape=[jax.ShapeDtypeStruct(shifts, BF16), jax.ShapeDtypeStruct(shifts, BF16)],
        cost_estimate=pl.CostEstimate(flops=6_000_000_000, bytes_accessed=16_000_000, transcendentals=0),
        compiler_params=small,
        name="prepare",
    )(ids)

    count = chans // PARTS
    after = ids
    features = []
    for part in range(PARTS):
        local = pl.pallas_call(
            functools.partial(local_kernel, part * count),
            in_specs=[VMEM] * 2 + [HBM] * 2 + [ANY],
            out_specs=VMEM,
            out_shape=jax.ShapeDtypeStruct((3, rows, count), F32),
            scratch_shapes=[
                pltpu.VMEM((3, taps, count), F32),
                pltpu.VMEM((3, rows, count), BF16),
                pltpu.SemaphoreType.DMA((2, count // LANES)),
            ],
            compiler_params=params,
            cost_estimate=pl.CostEstimate(flops=2_000_000_000, bytes_accessed=4_000_000, transcendentals=0),
            name="local",
        )(ids, delay, sf, qkv, after)
        made = [local]
        after = ids
        for streams, distance in (((1, 2), 1), ((0,), -1)):
            head, message = pl.pallas_call(
                functools.partial(message_kernel, part * count, streams),
                in_specs=[VMEM] * 5 + [ANY],
                out_specs=[VMEM] * 2,
                out_shape=[
                    jax.ShapeDtypeStruct((len(streams), EDGE, count), F32),
                    jax.ShapeDtypeStruct((rows, count), BF16),
                ],
                scratch_shapes=[pltpu.VMEM(((taps - 1) * EDGE, rows), F32)],
                compiler_params=params,
                cost_estimate=pl.CostEstimate(flops=500_000_000, bytes_accessed=1_000_000, transcendentals=0),
                name="message",
            )(ids, edge, sf, cotangent, local, after)
            after = message
            made += [head, passed_along(message, distance)]
        features.append(made)

    full = [
        jax.ShapeDtypeStruct((rows, chans), BF16),
        jax.ShapeDtypeStruct((3, rows, chans), BF16),
        jax.ShapeDtypeStruct((3, EDGE, chans), F32),
        jax.ShapeDtypeStruct((3, EDGE, chans), BF16),
        jax.ShapeDtypeStruct((chans // CHUNK, packed_rows, CHUNK), BF16),
    ]
    edge_scratch = pltpu.VMEM(((taps - 1) * EDGE, rows), BF16)
    query_scratch = [
        pltpu.VMEM((rows, count), BF16),
        pltpu.VMEM((rows, count), BF16),
        pltpu.VMEM((EDGE, count), F32),
        pltpu.VMEM((EDGE, count), BF16),
        pltpu.VMEM((count // CHUNK, PADDED, CHUNK), BF16),
        pltpu.VMEM((count // CHUNK, packed_rows - 3 * PADDED, CHUNK), BF16),
        edge_scratch,
        pltpu.VMEM((2 * rows, rows), BF16),
        pltpu.VMEM((rows, 2 * rows), F32),
        pltpu.VMEM((2 * rows, LANES), BF16),
        pltpu.VMEM((rows, LANES), BF16),
        pltpu.VMEM((step_groups, long_taps), F32),
        pltpu.VMEM((LANES, 2 * rows), BF16),
        pltpu.VMEM((LANES, rows), F32),
        pltpu.SemaphoreType.DMA((6, count // LANES)),
    ]
    pair_scratch = [
        pltpu.VMEM((2, rows, count), BF16),
        pltpu.VMEM((2, EDGE, count), F32),
        pltpu.VMEM((2, EDGE, count), BF16),
        pltpu.VMEM((count // CHUNK, 2 * PADDED, CHUNK), BF16),
        edge_scratch,
        pltpu.VMEM((2 * rows, rows), BF16),
        pltpu.VMEM((2 * rows, LANES), BF16),
        pltpu.VMEM((LANES, 2 * rows), BF16),
        pltpu.VMEM((LANES, rows), F32),
        pltpu.VMEM((groups, long_taps), F32),
        pltpu.SemaphoreType.DMA((4, count // LANES)),
    ]
    results = []
    stages = [pair for stage in range(PARTS) for pair in ((stage, None), (None, stage))]
    for query, pair in stages:
        operands = [ids, sf, advance, qkv, cotangent, edge]
        scratch = []
        query_first = pair_first = None
        if query is not None:
            query_first = query * count
            local, kv_head, kv_prev, q_head, grad_next = features[query]
            operands += [long_filter, local, q_head, kv_head, kv_prev]
            scratch += query_scratch
        if pair is not None:
            pair_first = pair * count
            local, kv_head, kv_prev, q_head, grad_next = features[pair]
            operands += [long_filter, local, q_head, kv_head, grad_next]
            scratch += pair_scratch
        filled = len(results)
        results = pl.pallas_call(
            functools.partial(mixer_kernel, query_first, pair_first, filled),
            in_specs=[VMEM] * len(operands) + [ANY] * filled,
            out_specs=[ANY] * 5,
            out_shape=full,
            input_output_aliases={len(operands) + k: k for k in range(filled)},
            scratch_shapes=scratch,
            compiler_params=params,
            cost_estimate=pl.CostEstimate(flops=4_000_000_000, bytes_accessed=4_000_000, transcendentals=0),
            name="query" if pair is None else "pair",
        )(*operands, *results)
    out, qg, tail, part, packed = results

    part = passed_along(part, -1)
    per = chans // devices
    if per == CHUNK:
        got = lax.all_to_all(packed, "ctx", 0, 0)
        long_grad, short_grad = pl.pallas_call(
            functools.partial(total_kernel, grad_scale, taps),
            in_specs=[VMEM],
            out_specs=[VMEM] * 2,
            out_shape=[
                jax.ShapeDtypeStruct((groups // devices, long_taps), F32),
                jax.ShapeDtypeStruct((3, taps, per), F32),
            ],
            compiler_params=small,
            cost_estimate=pl.CostEstimate(flops=1_000_000, bytes_accessed=200_000, transcendentals=0),
            name="total",
        )(got)
        short_grad = short_grad.transpose(0, 2, 1)
    else:
        head = 3 * PADDED
        short_part = packed[:, :head].transpose(1, 0, 2).reshape(head, devices, per)
        long_part = packed[:, head:].reshape(-1, packed_rows - head, CHUNK // long_taps, long_taps)
        long_part = long_part.transpose(0, 2, 1, 3).reshape(devices, -1, per)
        got = jnp.concatenate([short_part.transpose(1, 0, 2), long_part], 1)
        got = lax.all_to_all(got, "ctx", 0, 0)
        total = jnp.sum(got.astype(F32), 0) * grad_scale
        short_grad = total[:head].reshape(3, PADDED, per)[:, :taps].transpose(0, 2, 1)
        long_grad = total[head:].reshape(groups // devices, long_taps)
    qg = pl.pallas_call(
        last_rows_kernel,
        in_specs=[VMEM, VMEM, ANY, ANY],
        out_specs=ANY,
        out_shape=jax.ShapeDtypeStruct(qg.shape, BF16),
        input_output_aliases={2: 0},
        scratch_shapes=[pltpu.VMEM((3, EDGE, chans), BF16), pltpu.SemaphoreType.DMA],
        compiler_params=small,
        cost_estimate=pl.CostEstimate(flops=100_000, bytes_accessed=200_000, transcendentals=0),
        name="last_rows",
    )(tail, part, qg, got)
    return (out, qg, long_grad, short_grad)


def solution(mesh):
    in_specs = (P(None, "ctx", "tp"), P("ctx", "tp"), P("ctx"), P(None, "tp", None), P("tp", None))
    out_specs = (
        P("ctx", "tp"),
        P(None, "ctx", "tp"),
        P(("tp", "ctx"), None),
        P(None, ("tp", "ctx"), None),
    )
    return jax.shard_map(shards, mesh=mesh, in_specs=in_specs, out_specs=out_specs, check_vma=False)
```

```python
import functools
import math

import jax
import jax.numpy as jnp
from jax import lax
from jax.experimental import pallas as pl
from jax.experimental.pallas import tpu as pltpu
from jax.sharding import PartitionSpec as P

F32 = jnp.float32
BF16 = jnp.bfloat16
EDGE = 8
LANES = 512
CHUNK = 256
PADDED = 8
PARTS = 2

VMEM = pl.BlockSpec(memory_space=pltpu.VMEM)
ANY = pl.BlockSpec(memory_space=pl.ANY)
HBM = pl.BlockSpec(memory_space=pltpu.HBM)


def passed_along(block, distance):
    devices = range(lax.axis_size("ctx"))
    route = [(i - distance, i) for i in devices if i - distance in devices]
    return lax.ppermute(block, "ctx", route)


def iota2(shape, dim):
    return lax.broadcasted_iota(jnp.int32, shape, dim)


def dot(a, b):
    return jnp.dot(a, b, preferred_element_type=F32)


def lane_range(start, size):
    return pl.ds(pl.multiple_of(start, size), size)


def ones_where(cond):
    return jnp.where(cond, 1.0, 0.0)


def prepare_kernel(ids_ref, delay_ref, advance_ref):
    rows = delay_ref.shape[1]
    taps = delay_ref.shape[0] // rows + 1
    id_row = jnp.broadcast_to(ids_ref[...].astype(F32), (rows, rows))
    same = id_row == id_row.T
    lag = iota2((rows, rows), 0) - iota2((rows, rows), 1)
    for t in range(1, taps):
        delay_ref[(t - 1) * rows : t * rows] = ones_where((lag == t) & same).astype(BF16)
        advance_ref[(t - 1) * rows : t * rows] = ones_where((lag == -t) & same).astype(BF16)


def local_kernel(first, delay_ref, sf_hbm, x_hbm, _, feat_ref, sf_ref, x_ref, sems):
    rows = x_ref.shape[1]
    taps = sf_ref.shape[1]
    steps = feat_ref.shape[2] // LANES

    def loads(p):
        near = lane_range(p * LANES, LANES)
        cols = lane_range(first + p * LANES, LANES)
        pairs = [
            (sf_hbm.at[:, :, cols], sf_ref.at[:, :, near]),
            (x_hbm.at[:, :, cols], x_ref.at[:, :, near]),
        ]
        return [pltpu.make_async_copy(src, dst, sems.at[k, p]) for k, (src, dst) in enumerate(pairs)]

    for p in range(steps):
        for copy in loads(p):
            copy.start()

    def one_step(p):
        near = lane_range(p * LANES, LANES)
        for copy in loads(p):
            copy.wait()
        for i in range(3):
            x = x_ref[i, :, near]
            w = sf_ref[i, :, near]
            moved = dot(delay_ref[...], x)
            acc = w[0:1] * x.astype(F32)
            for t in range(1, taps):
                acc = acc + w[t : t + 1] * moved[(t - 1) * rows : t * rows]
            feat_ref[i, :, near] = acc

    for p in range(steps):
        one_step(p)


def message_kernel(first, streams, ids_ref, edge_ref, sf_ref, cot_ref, local_ref, _,
                   head_ref, sent_ref, edge_shift):
    rows = local_ref.shape[1]
    taps = sf_ref.shape[1]
    head_ids = jnp.broadcast_to(ids_ref[...].astype(F32), (rows, rows)).T[0:EDGE]
    before = pltpu.roll(jnp.broadcast_to(edge_ref[0, 0:1, 0:rows].astype(F32), (EDGE, rows)), EDGE, 1)
    lag = iota2((EDGE, rows), 0) + EDGE - iota2((EDGE, rows), 1)
    for t in range(1, taps):
        edge_shift[(t - 1) * EDGE : t * EDGE] = ones_where((lag == t) & (before == head_ids))
    id_wide = jnp.concatenate([ids_ref[...].astype(F32)] * (LANES // rows), 1)

    def one_step(p):
        near = lane_range(p * LANES, LANES)
        cols = lane_range(first + p * LANES, LANES)
        feats = []
        for i, stream in enumerate(streams):
            w = sf_ref[stream, :, cols]
            edge = edge_ref[stream, :, cols].astype(F32)
            edge = jnp.concatenate([edge, jnp.zeros((rows - EDGE, LANES), F32)], 0)
            moved = dot(edge_shift[...].astype(BF16), edge.astype(BF16))
            head = local_ref[stream, 0:EDGE, near] + w[1:2] * moved[0:EDGE]
            for t in range(2, taps):
                head = head + w[t : t + 1] * moved[(t - 1) * EDGE : t * EDGE]
            head_ref[i, :, near] = head
            feats.append(jnp.concatenate([head, local_ref[stream, EDGE:, near]], 0))
        if len(streams) == 1:
            g = cot_ref[:, cols].astype(F32) * feats[0]
            last = iota2(g.shape, 0) == rows - 1
            sent_ref[:, near] = jnp.where(last, jnp.broadcast_to(id_wide, g.shape), g).astype(BF16)
        else:
            sent_ref[:, near] = (feats[0] * feats[1]).astype(BF16)

    for p in range(sent_ref.shape[1] // LANES):
        one_step(p)


def run_steps(parts, steps):
    for p in range(steps):
        for one_step, copies in parts:
            one_step(p)
            for copy in copies(p):
                copy.start()
    for p in range(steps):
        for _, copies in parts:
            for copy in copies(p):
                copy.wait()


def joined(head, local):
    return jnp.concatenate([head, local[EDGE:]], 0)


def edge_shifts(ids_ref, edge_ref, edge_shift):
    rows = edge_shift.shape[1]
    taps = edge_shift.shape[0] // EDGE + 1
    id_head = jnp.broadcast_to(ids_ref[...].astype(F32), (EDGE, rows))
    prev = jnp.broadcast_to(edge_ref[0, 0:1, 0:rows].astype(F32), (rows, rows)).T
    lag = iota2((EDGE, rows), 1) + EDGE - iota2((EDGE, rows), 0)
    same = prev[rows - EDGE :] == id_head
    pieces = [ones_where((lag == t) & same) for t in range(1, taps)]
    edge_shift[...] = jnp.concatenate(pieces, 0).astype(BF16)


def short_stage(gf, w, x, xe, advance_ref, edge_shift):
    rows = gf.shape[0]
    taps = w.shape[0]
    gf_sent = gf.astype(BF16)
    moved = dot(advance_ref[...], gf_sent)
    moved_edge = dot(edge_shift[...], gf_sent)
    acc = w[0:1] * gf
    sums = [jnp.sum(x * gf, 0, keepdims=True)]
    sent = jnp.zeros((EDGE, LANES), F32)
    for t in range(1, taps):
        piece = moved[(t - 1) * rows : t * rows]
        piece_edge = moved_edge[(t - 1) * EDGE : t * EDGE]
        acc = acc + w[t : t + 1] * piece
        sent = sent + w[t : t + 1] * piece_edge
        sums.append(jnp.sum(x * piece, 0, keepdims=True) + jnp.sum(xe * piece_edge, 0, keepdims=True))
    sums.append(jnp.zeros((PADDED - taps, LANES), F32))
    return acc, sent, jnp.concatenate(sums, 0)


def query_part(first, shared, lf_ref, local_ref, q_head_ref, kv_head_ref, kvp_ref, outs, scratch):
    ids_ref, sf_ref, advance_ref, x_ref, cot_ref, edge_ref = shared
    out_hbm, qg_hbm, tail_hbm, part_hbm, packed_hbm = outs
    (out_ref, qg_ref, tail_ref, part_ref, short_ref, long_ref,
     edge_shift, mask_y, mask_a, w_kv, g_rev, dh_ref, kv_turned, y_turned, sems) = scratch
    rows = x_ref.shape[1]
    width = x_ref.shape[2] // lf_ref.shape[0]
    half = rows
    per = half // width
    lag = iota2((rows, rows), 0) - iota2((rows, rows), 1)
    mirror = ones_where(iota2((rows, rows), 0) + iota2((rows, rows), 1) == rows - 1).astype(BF16)
    id_row = jnp.broadcast_to(ids_ref[...].astype(F32), (rows, rows))
    id_col = id_row.T
    prev_row = jnp.broadcast_to(edge_ref[0, 0:1, 0:rows].astype(F32), (rows, rows))
    same = id_row == id_col
    mask_y[0:rows] = ones_where((lag <= 0) & same).astype(BF16)
    mask_y[rows:] = ones_where((lag > 0) & (prev_row.T == id_row)).astype(BF16)
    mask_a[:, 0:rows] = dot(mirror, ones_where((lag >= 0) & same).astype(BF16))
    mask_a[:, rows:] = dot(mirror, ones_where((lag < 0) & (prev_row == id_col)).astype(BF16))
    edge_shifts(ids_ref, edge_ref, edge_shift)
    owner = iota2((rows, half), 1) // width
    blocks = LANES // CHUNK
    head = 3 * PADDED

    def copies(p):
        near = lane_range(p * LANES, LANES)
        cols = lane_range(first + p * LANES, LANES)
        here = pl.ds(p * blocks, blocks)
        there = pl.ds(first // CHUNK + p * blocks, blocks)
        pairs = [
            (out_ref.at[:, near], out_hbm.at[:, cols]),
            (qg_ref.at[:, near], qg_hbm.at[0, :, cols]),
            (tail_ref.at[:, near], tail_hbm.at[0, :, cols]),
            (part_ref.at[:, near], part_hbm.at[0, :, cols]),
            (short_ref.at[here], packed_hbm.at[there, 0:PADDED]),
            (long_ref.at[here], packed_hbm.at[there, head:]),
        ]
        return [pltpu.make_async_copy(src, dst, sems.at[k, p]) for k, (src, dst) in enumerate(pairs)]

    def one_step(p):
        near = lane_range(p * LANES, LANES)
        cols = lane_range(first + p * LANES, LANES)
        cot = cot_ref[:, cols].astype(F32)
        q = joined(q_head_ref[0, :, near], local_ref[0, :, near])
        k = joined(kv_head_ref[0, :, near], local_ref[1, :, near])
        v = joined(kv_head_ref[1, :, near], local_ref[2, :, near])
        w_kv[0:rows] = (k * v).astype(BF16)
        w_kv[rows:] = kvp_ref[:, near]
        kv_turned[...] = w_kv[...].T
        g_rev[...] = dot(mirror, (cot * q).astype(BF16)).astype(BF16)
        for h in range(LANES // half):
            part = slice(h * half, (h + 1) * half)
            base = pl.multiple_of((first // half) * per + p * (LANES // width) + h * per, per)
            for j in range(per):
                mine = slice((h * per + j) * width, (h * per + j + 1) * width)
                taps = jnp.broadcast_to(lf_ref[pl.ds(base + j, 1), :], (rows, rows))
                taps = pltpu.roll(taps, 0, 1, stride=1, stride_axis=0).astype(BF16)
                toeplitz = jnp.concatenate([taps, taps], 0) * mask_y[...]
                y_turned[mine] = dot(kv_turned[mine], toeplitz)
                g_sel = jnp.where(owner == j, g_rev[:, part], jnp.zeros((rows, half), BF16))
                cross = dot(g_sel, kv_turned[part, :]) * mask_a[...]
                folded = cross[:, 0:rows] + cross[:, rows:]
                folded = pltpu.roll(folded, 0, 1, stride=1, stride_axis=0)
                dh_ref[h * per + j : h * per + j + 1] = jnp.sum(folded, 0, keepdims=True)
        dh = dot(dh_ref[...].astype(BF16), mirror)
        y = y_turned[...].T
        out_ref[:, near] = (q * y).astype(BF16)
        acc, sent, sums = short_stage(
            cot * y, sf_ref[0, :, cols], x_ref[0, :, cols].astype(F32), edge_ref[0, :, cols].astype(F32),
            advance_ref, edge_shift,
        )
        qg_ref[:, near] = acc.astype(BF16)
        tail_ref[:, near] = acc[rows - EDGE :]
        part_ref[:, near] = sent.astype(BF16)
        size = dh.shape[0] * rows // LANES
        for k in range(blocks):
            short_ref[p * blocks + k] = sums[:, k * CHUNK : (k + 1) * CHUNK].astype(BF16)
            lines = range(k * (CHUNK // rows), (k + 1) * (CHUNK // rows))
            long_ref[p * blocks + k] = jnp.concatenate([dh[e * size : (e + 1) * size] for e in lines], 1).astype(BF16)

    return one_step, copies


def pair_part(first, shared, lf_ref, local_ref, q_head_ref, kv_head_ref, gn_ref, outs, scratch):
    ids_ref, sf_ref, advance_ref, x_ref, cot_ref, edge_ref = shared
    _, qg_hbm, tail_hbm, part_hbm, packed_hbm = outs
    (qg_ref, tail_ref, part_ref, short_ref,
     edge_shift, mask_g, w_g, g_turned, gm_turned, lfr_ref, sems) = scratch
    rows = x_ref.shape[1]
    width = x_ref.shape[2] // lfr_ref.shape[0]
    lag = iota2((rows, rows), 0) - iota2((rows, rows), 1)
    id_row = jnp.broadcast_to(ids_ref[...].astype(F32), (rows, rows))
    next_col = jnp.broadcast_to(gn_ref[rows - 1 : rows, 0:rows].astype(F32), (rows, rows)).T
    backward = ones_where((iota2((rows, rows), 0) + iota2((rows, rows), 1)) % rows == 0)
    lfr_ref[...] = dot(lf_ref[...].astype(BF16), backward.astype(BF16))
    mask_g[0:rows] = ones_where((lag >= 0) & (id_row == id_row.T)).astype(BF16)
    mask_g[rows:] = ones_where((lag < 0) & (next_col == id_row)).astype(BF16)
    edge_shifts(ids_ref, edge_ref, edge_shift)
    blocks = LANES // CHUNK

    def copies(p):
        near = lane_range(p * LANES, LANES)
        cols = lane_range(first + p * LANES, LANES)
        pairs = [
            (qg_ref.at[:, :, near], qg_hbm.at[1:3, :, cols]),
            (tail_ref.at[:, :, near], tail_hbm.at[1:3, :, cols]),
            (part_ref.at[:, :, near], part_hbm.at[1:3, :, cols]),
            (
                short_ref.at[pl.ds(p * blocks, blocks)],
                packed_hbm.at[pl.ds(first // CHUNK + p * blocks, blocks), PADDED : 3 * PADDED],
            ),
        ]
        return [pltpu.make_async_copy(src, dst, sems.at[k, p]) for k, (src, dst) in enumerate(pairs)]

    def one_step(p):
        near = lane_range(p * LANES, LANES)
        cols = lane_range(first + p * LANES, LANES)
        q = joined(q_head_ref[0, :, near], local_ref[0, :, near])
        w_g[0:rows] = (cot_ref[:, cols].astype(F32) * q).astype(BF16)
        w_g[rows:] = gn_ref[:, near]
        g_turned[...] = w_g[...].T
        for j in range(LANES // width):
            mine = slice(j * width, (j + 1) * width)
            base = pl.multiple_of(first // width + p * (LANES // width), LANES // width)
            taps = jnp.broadcast_to(lfr_ref[pl.ds(base + j, 1), :], (rows, rows))
            taps = pltpu.roll(taps, 0, 1, stride=1, stride_axis=0).astype(BF16)
            toeplitz = jnp.concatenate([taps, taps], 0) * mask_g[...]
            gm_turned[mine] = dot(g_turned[mine], toeplitz)
        gm = gm_turned[...].T
        heads = []
        for i in (1, 2):
            acc, sent, sums = short_stage(
                gm * joined(kv_head_ref[2 - i, :, near], local_ref[3 - i, :, near]), sf_ref[i, :, cols], x_ref[i, :, cols].astype(F32),
                edge_ref[i, :, cols].astype(F32), advance_ref, edge_shift,
            )
            qg_ref[i - 1, :, near] = acc.astype(BF16)
            tail_ref[i - 1, :, near] = acc[rows - EDGE :]
            part_ref[i - 1, :, near] = sent.astype(BF16)
            heads.append(sums)
        for k in range(blocks):
            picked = [head[:, k * CHUNK : (k + 1) * CHUNK] for head in heads]
            short_ref[p * blocks + k] = jnp.concatenate(picked, 0).astype(BF16)

    return one_step, copies


def mixer_kernel(query_first, pair_first, filled, *refs):
    shared = refs[:6]
    halves = [query_first, pair_first]
    inputs = refs[6:]
    used = 5 * sum(first is not None for first in halves)
    outs = inputs[used + filled : used + filled + 5]
    scratch = inputs[used + filled + 5 :]
    parts = []
    for first, make, size in zip(halves, (query_part, pair_part), (15, 11)):
        if first is not None:
            steps = inputs[4].shape[1] // LANES
            parts.append(make(first, shared, *inputs[:5], outs, scratch[:size]))
            inputs = inputs[5:]
            scratch = scratch[size:]
    run_steps(parts, steps)


def last_rows_kernel(tail_ref, part_ref, qg_in, _, qg_hbm, last_ref, sem):
    rows = qg_hbm.shape[1]
    last_ref[...] = (tail_ref[...] + part_ref[...].astype(F32)).astype(BF16)
    copy = pltpu.make_async_copy(last_ref, qg_hbm.at[:, rows - EDGE :, :], sem)
    copy.start()
    copy.wait()


def total_kernel(scale, taps, got_ref, long_ref, short_ref):
    total = got_ref[0].astype(F32)
    for k in range(1, got_ref.shape[0]):
        total = total + got_ref[k].astype(F32)
    total = total * scale
    for i in range(3):
        short_ref[i] = total[i * PADDED : i * PADDED + taps]
    size = total.shape[0] - 3 * PADDED
    lags = long_ref.shape[1]
    for p in range(total.shape[1] // lags):
        long_ref[p * size : (p + 1) * size] = total[3 * PADDED :, p * lags : (p + 1) * lags]


def shards(qkv, cotangent, doc_ids, short_filter, long_filter):
    _, rows, chans = qkv.shape
    groups, long_taps = long_filter.shape
    taps = short_filter.shape[2]
    devices = lax.axis_size("ctx")
    grad_scale = 1.0 / math.sqrt(rows * devices)
    packed_rows = 3 * PADDED + groups * long_taps // chans
    step_groups = LANES * groups // chans
    params = pltpu.CompilerParams(vmem_limit_bytes=24 << 20)

    ids = doc_ids.astype(BF16).reshape(1, rows)
    sf = jnp.transpose(short_filter, (0, 2, 1))

    small = pltpu.CompilerParams(vmem_limit_bytes=8 << 20)
    edge = qkv[:, rows - EDGE :, :]
    edge = passed_along(edge.at[0, 0, :rows].set(ids[0]), 1)

    shifts = ((taps - 1) * rows, rows)
    delay, advance = pl.pallas_call(
        prepare_kernel,
        in_specs=[VMEM],
        out_specs=[VMEM] * 2,
        out_shape=[jax.ShapeDtypeStruct(shifts, BF16), jax.ShapeDtypeStruct(shifts, BF16)],
        cost_estimate=pl.CostEstimate(flops=6_000_000_000, bytes_accessed=16_000_000, transcendentals=0),
        compiler_params=small,
        name="prepare",
    )(ids)

    count = chans // PARTS
    after = ids
    features = []
    for part in range(PARTS):
        local = pl.pallas_call(
            functools.partial(local_kernel, part * count),
            in_specs=[VMEM] + [HBM] * 2 + [ANY],
            out_specs=VMEM,
            out_shape=jax.ShapeDtypeStruct((3, rows, count), F32),
            scratch_shapes=[
                pltpu.VMEM((3, taps, count), F32),
                pltpu.VMEM((3, rows, count), BF16),
                pltpu.SemaphoreType.DMA((2, count // LANES)),
            ],
            compiler_params=params,
            cost_estimate=pl.CostEstimate(flops=2_000_000_000, bytes_accessed=4_000_000, transcendentals=0),
            name="local",
        )(delay, sf, qkv, after)
        made = [local]
        after = ids
        for streams, distance in (((1, 2), 1), ((0,), -1)):
            head, message = pl.pallas_call(
                functools.partial(message_kernel, part * count, streams),
                in_specs=[VMEM] * 5 + [ANY],
                out_specs=[VMEM] * 2,
                out_shape=[
                    jax.ShapeDtypeStruct((len(streams), EDGE, count), F32),
                    jax.ShapeDtypeStruct((rows, count), BF16),
                ],
                scratch_shapes=[pltpu.VMEM(((taps - 1) * EDGE, rows), F32)],
                compiler_params=params,
                cost_estimate=pl.CostEstimate(flops=500_000_000, bytes_accessed=1_000_000, transcendentals=0),
                name="message",
            )(ids, edge, sf, cotangent, local, after)
            after = message
            made += [head, passed_along(message, distance)]
        features.append(made)

    full = [
        jax.ShapeDtypeStruct((rows, chans), BF16),
        jax.ShapeDtypeStruct((3, rows, chans), BF16),
        jax.ShapeDtypeStruct((3, EDGE, chans), F32),
        jax.ShapeDtypeStruct((3, EDGE, chans), BF16),
        jax.ShapeDtypeStruct((chans // CHUNK, packed_rows, CHUNK), BF16),
    ]
    edge_scratch = pltpu.VMEM(((taps - 1) * EDGE, rows), BF16)
    query_scratch = [
        pltpu.VMEM((rows, count), BF16),
        pltpu.VMEM((rows, count), BF16),
        pltpu.VMEM((EDGE, count), F32),
        pltpu.VMEM((EDGE, count), BF16),
        pltpu.VMEM((count // CHUNK, PADDED, CHUNK), BF16),
        pltpu.VMEM((count // CHUNK, packed_rows - 3 * PADDED, CHUNK), BF16),
        edge_scratch,
        pltpu.VMEM((2 * rows, rows), BF16),
        pltpu.VMEM((rows, 2 * rows), F32),
        pltpu.VMEM((2 * rows, LANES), BF16),
        pltpu.VMEM((rows, LANES), BF16),
        pltpu.VMEM((step_groups, long_taps), F32),
        pltpu.VMEM((LANES, 2 * rows), BF16),
        pltpu.VMEM((LANES, rows), F32),
        pltpu.SemaphoreType.DMA((6, count // LANES)),
    ]
    pair_scratch = [
        pltpu.VMEM((2, rows, count), BF16),
        pltpu.VMEM((2, EDGE, count), F32),
        pltpu.VMEM((2, EDGE, count), BF16),
        pltpu.VMEM((count // CHUNK, 2 * PADDED, CHUNK), BF16),
        edge_scratch,
        pltpu.VMEM((2 * rows, rows), BF16),
        pltpu.VMEM((2 * rows, LANES), BF16),
        pltpu.VMEM((LANES, 2 * rows), BF16),
        pltpu.VMEM((LANES, rows), F32),
        pltpu.VMEM((groups, long_taps), F32),
        pltpu.SemaphoreType.DMA((4, count // LANES)),
    ]
    results = []
    stages = [pair for stage in range(PARTS) for pair in ((stage, None), (None, stage))]
    for query, pair in stages:
        operands = [ids, sf, advance, qkv, cotangent, edge]
        scratch = []
        query_first = pair_first = None
        if query is not None:
            query_first = query * count
            local, kv_head, kv_prev, q_head, grad_next = features[query]
            operands += [long_filter, local, q_head, kv_head, kv_prev]
            scratch += query_scratch
        if pair is not None:
            pair_first = pair * count
            local, kv_head, kv_prev, q_head, grad_next = features[pair]
            operands += [long_filter, local, q_head, kv_head, grad_next]
            scratch += pair_scratch
        filled = len(results)
        results = pl.pallas_call(
            functools.partial(mixer_kernel, query_first, pair_first, filled),
            in_specs=[VMEM] * len(operands) + [ANY] * filled,
            out_specs=[ANY] * 5,
            out_shape=full,
            input_output_aliases={len(operands) + k: k for k in range(filled)},
            scratch_shapes=scratch,
            compiler_params=params,
            cost_estimate=pl.CostEstimate(flops=4_000_000_000, bytes_accessed=4_000_000, transcendentals=0),
            name="query" if pair is None else "pair",
        )(*operands, *results)
    out, qg, tail, part, packed = results

    part = passed_along(part, -1)
    per = chans // devices
    if per == CHUNK:
        got = lax.all_to_all(packed, "ctx", 0, 0)
        long_grad, short_grad = pl.pallas_call(
            functools.partial(total_kernel, grad_scale, taps),
            in_specs=[VMEM],
            out_specs=[VMEM] * 2,
            out_shape=[
                jax.ShapeDtypeStruct((groups // devices, long_taps), F32),
                jax.ShapeDtypeStruct((3, taps, per), F32),
            ],
            compiler_params=small,
            cost_estimate=pl.CostEstimate(flops=1_000_000, bytes_accessed=200_000, transcendentals=0),
            name="total",
        )(got)
        short_grad = short_grad.transpose(0, 2, 1)
    else:
        head = 3 * PADDED
        short_part = packed[:, :head].transpose(1, 0, 2).reshape(head, devices, per)
        long_part = packed[:, head:].reshape(-1, packed_rows - head, CHUNK // long_taps, long_taps)
        long_part = long_part.transpose(0, 2, 1, 3).reshape(devices, -1, per)
        got = jnp.concatenate([short_part.transpose(1, 0, 2), long_part], 1)
        got = lax.all_to_all(got, "ctx", 0, 0)
        total = jnp.sum(got.astype(F32), 0) * grad_scale
        short_grad = total[:head].reshape(3, PADDED, per)[:, :taps].transpose(0, 2, 1)
        long_grad = total[head:].reshape(groups // devices, long_taps)
    qg = pl.pallas_call(
        last_rows_kernel,
        in_specs=[VMEM, VMEM, ANY, ANY],
        out_specs=ANY,
        out_shape=jax.ShapeDtypeStruct(qg.shape, BF16),
        input_output_aliases={2: 0},
        scratch_shapes=[pltpu.VMEM((3, EDGE, chans), BF16), pltpu.SemaphoreType.DMA],
        compiler_params=small,
        cost_estimate=pl.CostEstimate(flops=100_000, bytes_accessed=200_000, transcendentals=0),
        name="last_rows",
    )(tail, part, qg, got)
    return (out, qg, long_grad, short_grad)


def solution(mesh):
    in_specs = (P(None, "ctx", "tp"), P("ctx", "tp"), P("ctx"), P(None, "tp", None), P("tp", None))
    out_specs = (
        P("ctx", "tp"),
        P(None, "ctx", "tp"),
        P(("tp", "ctx"), None),
        P(None, ("tp", "ctx"), None),
    )
    return jax.shard_map(shards, mesh=mesh, in_specs=in_specs, out_specs=out_specs, check_vma=False)
```
